32 devices in a mesh: fsdp: 32 (over z, y, x, core).
Axes of the slice: x: 2, y: 2, z: 4, core: 2. Of those that a mesh axis runs over, the one named last changes fastest.
Arguments:
- images: bfloat16 [32, 196, 512], P('fsdp'), may hold values from -90 to 90
- cotangent: bfloat16 [32, 196, 512], P('fsdp'), may hold values from -6 to 6
- counts: int32 [32], P('fsdp'), may hold values from 0 to 1, as said below
- attn_gain: bfloat16 [2, 512], P(None, 'fsdp'), may hold values from 0.099609375 to 1.8984375
- attn_bias: bfloat16 [2, 512], P(None, 'fsdp'), may hold values from -3 to 3
- qkv_weight: bfloat16 [2, 512, 1536], P(None, 'fsdp'), may hold values from -0.25 to 0.25
- qv_bias: bfloat16 [2, 2, 512], P(None, None, 'fsdp'), may hold values from -3 to 3
- rel_table: bfloat16 [2, 192, 16], P(None, 'fsdp'), may hold values from -320 to 320
- proj_weight: bfloat16 [2, 512, 512], P(None, 'fsdp'), may hold values from -2 to 2
- proj_bias: bfloat16 [2, 512], P(None, 'fsdp'), may hold values from -3 to 3
- mlp_gain: bfloat16 [2, 512], P(None, 'fsdp'), may hold values from 0.099609375 to 1.8984375
- mlp_bias: bfloat16 [2, 512], P(None, 'fsdp'), may hold values from -3 to 3
- fc1_weight: bfloat16 [2, 512, 2048], P(None, 'fsdp'), may hold values from -0.25 to 0.25
- fc1_bias: bfloat16 [2, 2048], P(None, 'fsdp'), may hold values from -3 to 3
- fc2_weight: bfloat16 [2, 2048, 512], P(None, 'fsdp'), may hold values from -0.125 to 0.125
- fc2_bias: bfloat16 [2, 512], P(None, 'fsdp'), may hold values from -3 to 3
Outputs:
- out_tokens: float32 [32, 196, 512], P('fsdp')
- in_grad: float32 [32, 196, 512], P('fsdp')
- grad_attn_gain: float32 [2, 512], P(None, 'fsdp')
- grad_attn_bias: float32 [2, 512], P(None, 'fsdp')
- grad_qkv_weight: float32 [2, 512, 1536], P(None, 'fsdp')
- grad_qv_bias: float32 [2, 2, 512], P(None, None, 'fsdp')
- grad_rel_table: float32 [2, 192, 16], P(None, 'fsdp')
- grad_proj_weight: float32 [2, 512, 512], P(None, 'fsdp')
- grad_proj_bias: float32 [2, 512], P(None, 'fsdp')
- grad_mlp_gain: float32 [2, 512], P(None, 'fsdp')
- grad_mlp_bias: float32 [2, 512], P(None, 'fsdp')
- grad_fc1_weight: float32 [2, 512, 2048], P(None, 'fsdp')
- grad_fc1_bias: float32 [2, 2048], P(None, 'fsdp')
- grad_fc2_weight: float32 [2, 2048, 512], P(None, 'fsdp')
- grad_fc2_bias: float32 [2, 512], P(None, 'fsdp')
The draws below stay inside these ranges and needn't reach their ends.
Inputs may be any that keep to these rules, and one draw needn't show every extreme that they name: `counts`: every draw has a device with 1 images and a device with 0.
All inputs are finite; a program needn't handle non-finite values.
Results may differ from the reference program's by a relative error of at most 0.014.
The reference program's roundings to bfloat16 on the way count: a program that leaves them out, or rounds other values in their place, can miss the bound.
Values may be sent and summed in bfloat16 or wider, within the bound.
A program may use at most 128 MiB of HBM per device.

```python
import jax
import jax.numpy as jnp
from jax import lax

D = 512
HEADS = 16
MLP_UNITS = 2048
WIN = 7
SIDE = 14
LAYERS = 2
IMG_DEV = 1
SHIFT = 3
TOK_IMG = 196
SLOTS = 32
HOLDERS = 32
TABLE_ROWS = 192


def draw_images(key, part):
    key_base = jax.random.fold_in(key, 21)
    key_rows = jax.random.fold_in(key, 22)
    key_cols = jax.random.fold_in(key, 23)
    shape_all = (SLOTS, SIDE * SIDE, D)
    row_scale = jnp.exp(jax.random.uniform(key_rows, (SLOTS, SIDE * SIDE, 1), jnp.float32, -1.2, 1.2))
    col_scale = jnp.exp(jax.random.uniform(key_cols, (1, 1, D), jnp.float32, -1.2, 1.2))
    base = jnp.clip(jax.random.normal(key_base, shape_all, jnp.float32), -6.5, 6.5)
    return (base * row_scale * col_scale).astype(jnp.bfloat16)


def draw_counts(key, part):
    key_base = jax.random.fold_in(key, 31)
    key_full = jax.random.fold_in(key, 32)
    key_short = jax.random.fold_in(key, 33)
    drawn = jax.random.randint(key_base, (HOLDERS,), IMG_DEV - 1, IMG_DEV + 1)
    full_at = jax.random.randint(key_full, (), 0, HOLDERS)
    short_at = (full_at + 1 + jax.random.randint(key_short, (), 0, HOLDERS - 1)) % HOLDERS
    places = jnp.arange(HOLDERS, dtype=jnp.int32)
    drawn = jnp.where(places == full_at, IMG_DEV, drawn)
    drawn = jnp.where(places == short_at, IMG_DEV - 1, drawn)
    return drawn.astype(jnp.int32)


def draw_rel_table(key, part):
    key_base = jax.random.fold_in(key, 41)
    shape_all = (LAYERS, TABLE_ROWS, HEADS)
    values = jnp.clip(jax.random.normal(key_base, shape_all, jnp.float32), -6.0, 6.0)
    return values.astype(jnp.bfloat16)


def block_scale(key, extent, split, low, top_value):
    loudness = 1.0
    for axis_at, blocks in split:
        steps = jax.random.uniform(jax.random.fold_in(jax.random.fold_in(key, 6), axis_at), (blocks,), jnp.float32, low / len(split), top_value / len(split))
        loudness = loudness * jnp.repeat(jnp.exp(steps), extent[axis_at] // blocks).reshape((-1,) + (1,) * (len(extent) - 1 - axis_at))
    return loudness


def bell_draw(key, dims, deviation, most, split=(), kind=jnp.bfloat16):
    array = jax.random.normal(key, dims, jnp.float32) * deviation
    if len(split) > 0:
        array = block_scale(key, dims, split, -0.22, 0.18) * array
    return jnp.clip(array, min=-most, max=most).astype(kind)


def setup_inputs(seed: int = 0) -> dict:
    streams_of = jax.random.split(jax.random.key(seed), 17)
    return {
        "images": draw_images(jax.random.fold_in(streams_of[16], 71), 0),
        "cotangent": bell_draw(streams_of[1], (SLOTS, TOK_IMG, D), 1.0, 6.0, ((0, 32),)),
        "counts": draw_counts(jax.random.fold_in(streams_of[16], 71), 0),
        "attn_gain": jnp.clip(1.0 + 0.18 * jax.random.normal(streams_of[3], (LAYERS, D), jnp.float32), 0.099609375, 1.8984375).astype(jnp.bfloat16),
        "attn_bias": bell_draw(streams_of[4], (LAYERS, D), 0.5, 3.0, ((1, 32),)),
        "qkv_weight": bell_draw(streams_of[5], (LAYERS, D, 3 * D), D ** -0.5, 0.25, ((1, 32),)),
        "qv_bias": bell_draw(streams_of[6], (LAYERS, 2, D), 0.5, 3.0, ((2, 32),)),
        "rel_table": draw_rel_table(jax.random.fold_in(streams_of[16], 71), 0),
        "proj_weight": bell_draw(streams_of[8], (LAYERS, D, D), (D // (WIN * WIN)) ** -0.5, 2.0, ((1, 32),)),
        "proj_bias": bell_draw(streams_of[9], (LAYERS, D), 0.5, 3.0, ((1, 32),)),
        "mlp_gain": jnp.clip(1.0 + 0.18 * jax.random.normal(streams_of[10], (LAYERS, D), jnp.float32), 0.099609375, 1.8984375).astype(jnp.bfloat16),
        "mlp_bias": bell_draw(streams_of[11], (LAYERS, D), 0.5, 3.0, ((1, 32),)),
        "fc1_weight": bell_draw(streams_of[12], (LAYERS, D, MLP_UNITS), D ** -0.5, 0.25, ((1, 32),)),
        "fc1_bias": bell_draw(streams_of[13], (LAYERS, MLP_UNITS), 0.5, 3.0, ((1, 32),)),
        "fc2_weight": bell_draw(streams_of[14], (LAYERS, MLP_UNITS, D), MLP_UNITS ** -0.5, 0.125, ((1, 32),)),
        "fc2_bias": bell_draw(streams_of[15], (LAYERS, D), 0.5, 3.0, ((1, 32),)),
    }


norm_eps = 1e-05
mask_fill = -10000.0
highest = lax.Precision.HIGHEST
half_root = 0.7071067811865476
inv_root_tau = 0.3989422804014327

def layer_norm(rows, gain, offset):
    centre = lax.optimization_barrier(jnp.mean(rows, axis=-1, keepdims=True))
    centred = rows - centre
    spread = lax.optimization_barrier(jnp.mean(centred * centred, axis=-1, keepdims=True))
    return centred * lax.rsqrt(spread + norm_eps) * gain + offset

def gelu_slope(values):
    cumul = 0.5 * (1.0 + lax.erf(values * half_root))
    density = jnp.exp(-0.5 * values * values) * inv_root_tau
    return cumul + values * density

def batched(form, left, right):
    return jnp.einsum(form, left.astype(jnp.float32), right.astype(jnp.float32))

def to_windows(rows, shift_by):
    channels = rows.shape[-1]
    grid = rows.reshape(SIDE, SIDE, channels)
    if shift_by:
        grid = jnp.roll(grid, (-shift_by, -shift_by), axis=(0, 1))
    across = SIDE // WIN
    grid = grid.reshape(across, WIN, across, WIN, channels).transpose(0, 2, 1, 3, 4)
    return grid.reshape(across * across, WIN * WIN, channels)

def from_windows(blocks, shift_by):
    channels = blocks.shape[-1]
    across = SIDE // WIN
    grid = blocks.reshape(across, across, WIN, WIN, channels).transpose(0, 2, 1, 3, 4)
    grid = grid.reshape(SIDE, SIDE, channels)
    if shift_by:
        grid = jnp.roll(grid, (shift_by, shift_by), axis=(0, 1))
    return grid.reshape(SIDE * SIDE, channels)

def offset_onehot(table_rows):
    places = jnp.arange(WIN * WIN, dtype=jnp.int32)
    row_at = places // WIN
    col_at = places % WIN
    index = (row_at[:, None] - row_at[None, :] + WIN - 1) * (2 * WIN - 1) + (col_at[:, None] - col_at[None, :] + WIN - 1)
    targets = jnp.arange(table_rows, dtype=jnp.int32)
    return (index.reshape(-1)[:, None] == targets[None, :]).astype(jnp.float32)

def block_mask(shift_by):
    across = SIDE // WIN
    if not shift_by:
        return jnp.zeros((across * across, WIN * WIN, WIN * WIN), jnp.float32)
    coord = jnp.arange(SIDE, dtype=jnp.int32)
    region = jnp.where(coord < SIDE - WIN, 0, jnp.where(coord < SIDE - shift_by, 1, 2)).astype(jnp.int32)
    labels = (region[:, None] * 3 + region[None, :]).reshape(SIDE * SIDE, 1)
    labels = to_windows(labels, 0)[:, :, 0]
    return jnp.where(labels[:, :, None] == labels[:, None, :], 0.0, mask_fill).astype(jnp.float32)

def attend_scores(query, keys, pos_bias, mask_add, scaling):
    scores = batched('nqhd,nkhd->nhqk', query, keys) * scaling
    return scores + pos_bias[None] + mask_add[:, None]

def block_forward(current, layer_weights, onehot, mask_add, shift_by):
    gain_one, bias_one, w_qkv, b_qv, table, w_proj, b_proj, gain_two, bias_two, w_first, b_first, w_second, b_second = layer_weights
    features = current.shape[-1]
    head_count = table.shape[-1]
    head_size = features // head_count
    scaling = head_size ** (-0.5)
    normed = layer_norm(current, gain_one.astype(jnp.float32), bias_one.astype(jnp.float32)).astype(jnp.bfloat16)
    windowed = to_windows(normed, shift_by)
    win_count, win_len = (windowed.shape[0], windowed.shape[1])
    flat_in = windowed.reshape(win_count * win_len, features)
    full_bias = jnp.concatenate([b_qv[0].astype(jnp.float32), jnp.zeros((features,), jnp.float32), b_qv[1].astype(jnp.float32)])
    packed = (jnp.dot(flat_in, w_qkv, preferred_element_type=jnp.float32) + full_bias).astype(jnp.bfloat16)
    packed = packed.reshape(win_count, win_len, 3, head_count, head_size)
    query, keys, values = (packed[:, :, 0], packed[:, :, 1], packed[:, :, 2])
    pos_bias = jnp.dot(onehot, table.astype(jnp.float32), precision=highest)
    pos_bias = pos_bias.reshape(win_len, win_len, head_count).transpose(2, 0, 1)
    scores = attend_scores(query, keys, pos_bias, mask_add, scaling)
    peak = lax.optimization_barrier(jnp.max(scores, axis=-1, keepdims=True))
    log_total = peak + jnp.log(lax.optimization_barrier(jnp.sum(jnp.exp(scores - peak), axis=-1, keepdims=True)))
    probs = jnp.exp(scores - log_total).astype(jnp.bfloat16)
    mixed = batched('nhqk,nkhd->nqhd', probs, values).astype(jnp.bfloat16).reshape(win_count * win_len, features)
    attended = jnp.dot(mixed, w_proj, preferred_element_type=jnp.float32) + b_proj.astype(jnp.float32)
    middle = current + from_windows(attended.reshape(win_count, win_len, features), shift_by)
    second_in = layer_norm(middle, gain_two.astype(jnp.float32), bias_two.astype(jnp.float32)).astype(jnp.bfloat16)
    pre_act = jnp.dot(second_in, w_first, preferred_element_type=jnp.float32) + b_first.astype(jnp.float32)
    activ = jax.nn.gelu(pre_act, approximate=False).astype(jnp.bfloat16)
    after = middle + jnp.dot(activ, w_second, preferred_element_type=jnp.float32) + b_second.astype(jnp.float32)
    memo = (current, flat_in, query, keys, values, pos_bias, log_total, mixed, middle, second_in, pre_act, activ)
    return (after, memo)

def block_backward(grad_rows, layer_weights, memo, onehot, mask_add, shift_by):
    gain_one, bias_one, w_qkv, b_qv, table, w_proj, b_proj, gain_two, bias_two, w_first, b_first, w_second, b_second = layer_weights
    current, flat_in, query, keys, values, pos_bias, log_total, mixed, middle, second_in, pre_act, activ = memo
    features = current.shape[-1]
    head_count = table.shape[-1]
    head_size = features // head_count
    scaling = head_size ** (-0.5)
    win_count, win_len = (query.shape[0], query.shape[1])
    grad_low = grad_rows.astype(jnp.bfloat16)
    g_second = jnp.dot(activ.T, grad_low, preferred_element_type=jnp.float32)
    g_b_second = lax.optimization_barrier(jnp.sum(grad_rows, axis=0))
    grad_pre = jnp.dot(grad_low, w_second.T, preferred_element_type=jnp.float32) * gelu_slope(pre_act)
    g_b_first = lax.optimization_barrier(jnp.sum(grad_pre, axis=0))
    pre_low = grad_pre.astype(jnp.bfloat16)
    g_first = jnp.dot(second_in.T, pre_low, preferred_element_type=jnp.float32)
    grad_norm_two = jnp.dot(pre_low, w_first.T, preferred_element_type=jnp.float32)
    unused, pull_two = jax.vjp(layer_norm, middle, gain_two.astype(jnp.float32), bias_two.astype(jnp.float32))
    back_mid, g_gain_two, g_bias_two = pull_two(grad_norm_two)
    grad_middle = grad_rows + back_mid
    attn_low = to_windows(grad_middle, shift_by).reshape(win_count * win_len, features).astype(jnp.bfloat16)
    g_proj = jnp.dot(mixed.T, attn_low, preferred_element_type=jnp.float32)
    g_b_proj = lax.optimization_barrier(jnp.sum(grad_middle, axis=0))
    grad_mixed = jnp.dot(attn_low, w_proj.T, preferred_element_type=jnp.float32).astype(jnp.bfloat16)
    grad_mixed = grad_mixed.reshape(win_count, win_len, head_count, head_size)
    scores = attend_scores(query, keys, pos_bias, mask_add, scaling)
    probs_full = jnp.exp(scores - log_total)
    grad_probs = batched('nqhd,nkhd->nhqk', grad_mixed, values)
    grad_values = batched('nhqk,nqhd->nkhd', probs_full.astype(jnp.bfloat16), grad_mixed)
    grad_scores = probs_full * (grad_probs - lax.optimization_barrier(jnp.sum(probs_full * grad_probs, axis=-1, keepdims=True)))
    per_pair = lax.optimization_barrier(jnp.sum(grad_scores, axis=0)).reshape(head_count, win_len * win_len)
    g_table = jnp.dot(per_pair, onehot, precision=highest).T
    scores_low = grad_scores.astype(jnp.bfloat16)
    grad_query = batched('nhqk,nkhd->nqhd', scores_low, keys) * scaling
    grad_keys = batched('nhqk,nqhd->nkhd', scores_low, query) * scaling
    g_qv = jnp.stack([lax.optimization_barrier(jnp.sum(grad_query, axis=(0, 1))).reshape(features), lax.optimization_barrier(jnp.sum(grad_values, axis=(0, 1))).reshape(features)])
    grad_packed = jnp.stack([grad_query, grad_keys, grad_values], axis=2).reshape(win_count * win_len, 3 * features).astype(jnp.bfloat16)
    g_qkv = jnp.dot(flat_in.T, grad_packed, preferred_element_type=jnp.float32)
    grad_norm_one = jnp.dot(grad_packed, w_qkv.T, preferred_element_type=jnp.float32)
    grad_norm_one = from_windows(grad_norm_one.reshape(win_count, win_len, features), shift_by)
    unused_too, pull_one = jax.vjp(layer_norm, current, gain_one.astype(jnp.float32), bias_one.astype(jnp.float32))
    back_in, g_gain_one, g_bias_one = pull_one(grad_norm_one)
    grad_terms = (g_gain_one, g_bias_one, g_qkv, g_qv, g_table, g_proj, g_b_proj, g_gain_two, g_bias_two, g_first, g_b_first, g_second, g_b_second)
    return (grad_middle + back_in, grad_terms)

def image_forward(picture, weights, onehot):
    current = picture.astype(jnp.float32)
    history = []
    for layer_idx in range(LAYERS):
        shift_by = SHIFT if layer_idx % 2 else 0
        layer_weights = tuple((tensor[layer_idx] for tensor in weights))
        current, memo = block_forward(current, layer_weights, onehot, block_mask(shift_by), shift_by)
        history.append(memo)
    return (current, history)

def image_backward(grad_rows, weights, history, onehot):
    layer_grads = [None] * LAYERS
    for layer_idx in reversed(range(LAYERS)):
        shift_by = SHIFT if layer_idx % 2 else 0
        layer_weights = tuple((tensor[layer_idx] for tensor in weights))
        grad_rows, layer_grads[layer_idx] = block_backward(grad_rows, layer_weights, history[layer_idx], onehot, block_mask(shift_by), shift_by)
    stacked = jax.tree.map(lambda *pieces: jnp.stack(pieces), *layer_grads)
    return (grad_rows, stacked)

def reference(images, cotangent, counts, attn_gain, attn_bias, qkv_weight, qv_bias, rel_table, proj_weight, proj_bias, mlp_gain, mlp_bias, fc1_weight, fc1_bias, fc2_weight, fc2_bias):
    weights = (attn_gain, attn_bias, qkv_weight, qv_bias, rel_table, proj_weight, proj_bias, mlp_gain, mlp_bias, fc1_weight, fc1_bias, fc2_weight, fc2_bias)
    onehot = offset_onehot(TABLE_ROWS)
    slot_ids = jnp.arange(SLOTS, dtype=jnp.int32)
    active_all = slot_ids % IMG_DEV < counts[slot_ids // IMG_DEV]
    totals = tuple((jnp.zeros(tensor.shape, jnp.float32) for tensor in weights))

    def advance(running, record):
        picture, upstream, active = record
        output_rows, history = image_forward(picture, weights, onehot)
        shown = jnp.where(active, output_rows, 0.0)
        seed_grad = jnp.where(active, upstream.astype(jnp.float32), 0.0)
        grad_in, grad_terms = image_backward(seed_grad, weights, history, onehot)
        running = tuple((left + right for left, right in zip(running, grad_terms)))
        return (running, (shown, grad_in))
    running, (outs, grads_in) = lax.scan(advance, totals, (images, cotangent, active_all))
    return (outs, grads_in, running[0], running[1], running[2], running[3], running[4], running[5], running[6], running[7], running[8], running[9], running[10], running[11], running[12])
```

```python
import functools

import jax
import jax.numpy as jnp
import numpy as np
from jax import lax
from jax.experimental import pallas as pl
from jax.experimental.pallas import tpu as pltpu
from jax.sharding import PartitionSpec as P

WIN = 7
SIDE = 14
LAYERS = 2
SHIFT = 3

norm_eps = 1e-05
mask_fill = -10000.0
outside_fill = -1e30
half_root = 0.7071067811865476
inv_root_tau = 0.3989422804014327
lanes = 128
bf16 = jnp.bfloat16
f32 = jnp.float32


def dot_nn(left, right):
    return lax.dot_general(left, right, (((1,), (0,)), ((), ())), preferred_element_type=f32)


def dot_nt(left, right):
    return lax.dot_general(left, right, (((1,), (1,)), ((), ())), preferred_element_type=f32)


def dot_tn(left, right):
    return lax.dot_general(left, right, (((0,), (0,)), ((), ())), preferred_element_type=f32)


def normalize(rows):
    centred = rows - jnp.mean(rows, axis=-1, keepdims=True)
    spread = jnp.mean(centred * centred, axis=-1, keepdims=True)
    inverse = lax.rsqrt(spread + norm_eps)
    return centred * inverse, inverse


def norm_pull(rows, gain, grad):
    unit, inverse = normalize(rows)
    g_gain = jnp.sum(grad * unit, axis=0, keepdims=True)
    g_bias = jnp.sum(grad, axis=0, keepdims=True)
    scaled = grad * gain
    back = inverse * (
        scaled
        - jnp.mean(scaled, axis=-1, keepdims=True)
        - unit * jnp.mean(scaled * unit, axis=-1, keepdims=True)
    )
    return back, g_gain, g_bias


def head_mask(local_head, head_size):
    lane = lax.broadcasted_iota(jnp.int32, (1, lanes), 1)
    return jnp.where(lane // head_size == local_head, 1.0, 0.0).astype(bf16)


def bias_kernel(pairs_ref, spread_ref, spread_t_ref, mask_ref, out_ref):
    def step(head, carry):
        rows = dot_nn(spread_ref[...], pairs_ref[head]).astype(bf16)
        out_ref[head] = dot_nn(rows, spread_t_ref[...]) + mask_ref[...]
        return carry

    lax.fori_loop(0, pairs_ref.shape[0], step, 0)


def attn_fwd_kernel(
    x_ref, gain_ref, off_ref, wqkv_ref, bqkv_ref, bias_ref, wproj_ref, bproj_ref,
    mid_ref, xn_ref, qkv_ref, key_t_ref, probs_ref, mixed_t_ref,
    val_t,
):
    rows = x_ref[...]
    features = rows.shape[1]
    heads = bias_ref.shape[0]
    size = features // heads
    scaling = size ** (-0.5)
    unit, _ = normalize(rows)
    xn = (unit * gain_ref[...] + off_ref[...]).astype(bf16)
    xn_ref[...] = xn
    for part in range(3):
        cols = pl.ds(part * features, features)
        block = dot_nn(xn, wqkv_ref[part]) + bqkv_ref[:, cols]
        qkv_ref[:, cols] = block.astype(bf16)
        if part == 1:
            key_t_ref[...] = block.T.astype(bf16)
        if part == 2:
            val_t[...] = block.T.astype(bf16)
    per = lanes // size

    def group(g, carry):
        start = pl.multiple_of(g * lanes, lanes)
        query = qkv_ref[:, pl.ds(start, lanes)]
        keys = qkv_ref[:, pl.ds(pl.multiple_of(features + start, lanes), lanes)]
        for one in range(per):
            head = g * per + one
            at = pl.ds(pl.multiple_of(head * size, size), size)
            scores = dot_nt(keys * head_mask(one, size), query) * scaling + bias_ref[head]
            peak = jnp.max(scores, axis=0, keepdims=True)
            raised = jnp.exp(scores - peak)
            total = jnp.sum(raised, axis=0, keepdims=True)
            probs = raised * (1.0 / total)
            probs_ref[head] = probs
            mixed_t_ref[at, :] = dot_nn(val_t[at, :], probs.astype(bf16)).astype(bf16)
        return carry

    lax.fori_loop(0, heads // per, group, 0)
    mixed = mixed_t_ref[...].astype(f32).T.astype(bf16)
    mid_ref[...] = rows + dot_nn(mixed, wproj_ref[...]) + bproj_ref[...]


def mlp_fwd_kernel(
    mid_ref, gain_ref, off_ref, w1_ref, b1_ref, w2_ref, b2_ref,
    out_ref, yn_ref, slope_ref, act_ref,
):
    middle = mid_ref[...]
    features = middle.shape[1]
    unit, _ = normalize(middle)
    yn = (unit * gain_ref[...] + off_ref[...]).astype(bf16)
    yn_ref[...] = yn
    total = middle + b2_ref[...]
    for chunk in range(w1_ref.shape[0]):
        cols = pl.ds(chunk * features, features)
        pre = dot_nn(yn, w1_ref[chunk]) + b1_ref[:, cols]
        cumul = 0.5 * (1.0 + lax.erf(pre * half_root))
        slope_ref[:, cols] = cumul + pre * (jnp.exp(-0.5 * pre * pre) * inv_root_tau)
        act = (pre * cumul).astype(bf16)
        act_ref[:, cols] = act
        total = total + dot_nn(act, w2_ref[cols, :])
    out_ref[...] = total


def mlp_bwd_kernel(
    g_ref, mid_ref, gain_ref, w1_ref, w2_ref, yn_ref, slope_ref, act_ref,
    gm_ref, gw1_ref, gw2_ref, gb1_ref, gb2_ref, ggain_ref, goff_ref, gbproj_ref,
):
    grad = g_ref[...]
    features = grad.shape[1]
    low = grad.astype(bf16)
    gb2_ref[...] = jnp.sum(grad, axis=0, keepdims=True)
    yn = yn_ref[...]
    g_yn = jnp.zeros_like(grad)
    for chunk in range(w1_ref.shape[0]):
        cols = pl.ds(chunk * features, features)
        gw2_ref[cols, :] = dot_tn(act_ref[:, cols], low).astype(bf16)
        g_pre = dot_nt(low, w2_ref[cols, :]) * slope_ref[:, cols]
        gb1_ref[:, cols] = jnp.sum(g_pre, axis=0, keepdims=True)
        pre_low = g_pre.astype(bf16)
        gw1_ref[chunk] = dot_tn(yn, pre_low).astype(bf16)
        g_yn = g_yn + dot_nt(pre_low, w1_ref[chunk])
    back, g_gain, g_off = norm_pull(mid_ref[...], gain_ref[...], g_yn)
    ggain_ref[...] = g_gain
    goff_ref[...] = g_off
    g_mid = grad + back
    gm_ref[...] = g_mid
    gbproj_ref[...] = jnp.sum(g_mid, axis=0, keepdims=True)


def attn_bwd_kernel(
    gm_ref, x_ref, gain_ref, wqkv_ref, wproj_ref, xn_ref, qkv_ref, key_t_ref, probs_ref,
    mixed_t_ref, spread_ref, spread_t_ref,
    gx_ref, gwqkv_ref, gwproj_ref, gqv_ref, gpairs_ref, ggain_ref, goff_ref,
    dmix, dq_t, dqkv,
):
    g_mid = gm_ref[...]
    features = g_mid.shape[1]
    heads = probs_ref.shape[0]
    size = features // heads
    scaling = size ** (-0.5)
    low = g_mid.astype(bf16)
    gwproj_ref[...] = dot_nn(mixed_t_ref[...], low).astype(bf16)
    dmix[...] = dot_nt(low, wproj_ref[...]).astype(bf16)
    per = lanes // size

    def group(g, carry):
        start = pl.multiple_of(g * lanes, lanes)
        k_at = pl.multiple_of(features + start, lanes)
        v_at = pl.multiple_of(2 * features + start, lanes)
        query = qkv_ref[:, pl.ds(start, lanes)]
        values = qkv_ref[:, pl.ds(v_at, lanes)]
        d_mix = dmix[:, pl.ds(start, lanes)]
        d_keys = jnp.zeros(query.shape, f32)
        d_values = jnp.zeros(query.shape, f32)
        for one in range(per):
            head = g * per + one
            at = pl.ds(pl.multiple_of(head * size, size), size)
            keep = head_mask(one, size)
            probs = probs_ref[head]
            d_probs = dot_nt(values * keep, d_mix)
            d_values = d_values + dot_nn(probs.astype(bf16), d_mix * keep)
            weighed = probs * d_probs
            d_scores = weighed - probs * jnp.sum(weighed, axis=0, keepdims=True)
            scores_low = d_scores.astype(bf16)
            d_keys = d_keys + dot_nn(scores_low, query * keep)
            dq_t[at, :] = dot_nn(key_t_ref[at, :], scores_low)
            folded = dot_nn(spread_t_ref[...], scores_low).astype(bf16)
            gpairs_ref[head] = dot_nn(folded, spread_ref[...])
        dqkv[:, pl.ds(k_at, lanes)] = (d_keys * scaling).astype(bf16)
        dqkv[:, pl.ds(v_at, lanes)] = d_values.astype(bf16)
        gqv_ref[1:2, pl.ds(start, lanes)] = jnp.sum(d_values, axis=0, keepdims=True)
        return carry

    lax.fori_loop(0, heads // per, group, 0)
    d_query = dq_t[...].T * scaling
    gqv_ref[0:1, :] = jnp.sum(d_query, axis=0, keepdims=True)
    dqkv[:, :features] = d_query.astype(bf16)
    xn = xn_ref[...]
    g_xn = jnp.zeros_like(g_mid)
    for part in range(3):
        cols = pl.ds(part * features, features)
        block = dqkv[:, cols]
        gwqkv_ref[part] = dot_tn(xn, block).astype(bf16)
        g_xn = g_xn + dot_nt(block, wqkv_ref[part])
    back, g_gain, g_off = norm_pull(x_ref[...], gain_ref[...], g_xn)
    ggain_ref[...] = g_gain
    goff_ref[...] = g_off
    gx_ref[...] = g_mid + back


def bit_of(index, place):
    return lax.rem(index // (1 << place), 2)


def peers_of(me, places):
    return [me + (1 - 2 * bit_of(me, place)) * (1 << place) for place in range(places)]


def greet(me, places):
    barrier = pltpu.get_barrier_semaphore()
    for peer in peers_of(me, places):
        pl.semaphore_signal(
            barrier, inc=1, device_id=(peer,), device_id_type=pl.DeviceIdType.MESH
        )
    pl.semaphore_wait(barrier, places)


def routes(places):
    high = list(range(places - 1, 2, -1))
    if places < 3:
        return [list(range(places - 1, -1, -1))]
    return [
        high + [2, 1, 0],
        high + [1, 2, 0],
        [2] + high + [1, 0],
        [1] + high + [2, 0],
    ]


def row_parts(total, count):
    units = total // 16
    sizes = [16 * (units // count + (1 if n < units % count else 0)) for n in range(count)]
    return [(sum(sizes[:n]), sizes[n]) for n in range(count)]


def region(places, free, me, lowest=0, forced=None):
    picks = []
    for place in range(places - 1, lowest - 1, -1):
        if forced is not None and place == forced[0]:
            picks.append(forced[1])
        elif place in free:
            picks.append(slice(None))
        else:
            picks.append(bit_of(me, place))
    return tuple(picks)


def gather_kernel(places, x_ref, out_ref, send_sem, recv_sem, own_sem):
    me = lax.axis_index("fsdp")
    peers = peers_of(me, places)
    greet(me, places)
    own = pltpu.make_async_copy(x_ref, out_ref.at[region(places, (), me)], own_sem)
    own.start()
    orders = routes(places)
    parts = row_parts(x_ref.shape[0], len(orders))
    copies = [[] for _ in orders]
    for stage in range(places):
        for n, (order, (low, size)) in enumerate(zip(orders, parts)):
            rows = pl.ds(low, size)
            place = order[stage]
            if stage == 1 and n == 0:
                own.wait()
            if stage:
                copies[n][-1].wait_recv()
            here = region(places, order[:stage], me)
            target = out_ref.at[here + (rows,)]
            copy = pltpu.make_async_remote_copy(
                src_ref=x_ref.at[rows] if stage == 0 else target,
                dst_ref=target,
                send_sem=send_sem.at[n, stage],
                recv_sem=recv_sem.at[n, stage],
                device_id=(peers[place],),
                device_id_type=pl.DeviceIdType.MESH,
            )
            copy.start()
            copies[n].append(copy)
    for group in copies:
        group[-1].wait_recv()
    for group in copies:
        for copy in group:
            copy.wait_send()


def scatter_kernel(places, g_ref, out_ref, acc, *rest):
    landings, (send_sem, recv_sem) = rest[:places], rest[places:]
    me = lax.axis_index("fsdp")
    peers = peers_of(me, places)
    greet(me, places)
    orders = [order[::-1] for order in routes(places)]
    parts = row_parts(g_ref.shape[-2], len(orders))
    everything = set(range(places))
    copies = [[None] * places for _ in orders]

    def send(n, stage):
        order, (low, size) = orders[n], parts[n]
        rows = pl.ds(low, size)
        place = order[stage]
        free = everything - set(order[: stage + 1])
        away = (place, 1 - bit_of(me, place))
        if stage == 0:
            source = g_ref.at[region(places, free, me, 0, away) + (rows,)]
        else:
            source = acc.at[region(places, free, me, 1, away) + (rows,)]
        copy = pltpu.make_async_remote_copy(
            src_ref=source,
            dst_ref=landings[stage].at[(slice(None),) * len(free) + (rows,)],
            send_sem=send_sem.at[n, stage],
            recv_sem=recv_sem.at[n, stage],
            device_id=(peers[place],),
            device_id_type=pl.DeviceIdType.MESH,
        )
        copy.start()
        copies[n][stage] = copy

    def add(n, stage):
        order, (low, size) = orders[n], parts[n]
        rows = pl.ds(low, size)
        free = sorted(everything - set(order[: stage + 1]), reverse=True)
        copies[n][stage].wait_recv()

        def one(at, carry):
            values = {}
            for spot, place in enumerate(free):
                values[place] = lax.rem(at // (1 << (len(free) - 1 - spot)), 2)
            full = tuple(
                values[place] if place in values else bit_of(me, place)
                for place in range(places - 1, -1, -1)
            )
            kept = full[:-1] + (rows,)
            landed = landings[stage][tuple(values[place] for place in free) + (rows,)]
            if stage == 0:
                acc[kept] = g_ref[full + (rows,)] + landed
            elif stage < places - 1:
                acc[kept] = acc[kept] + landed
            else:
                out_ref[rows] = acc[kept].astype(f32) + landed.astype(f32)
            return carry

        lax.fori_loop(0, 1 << len(free), one, 0)

    for n in range(len(orders)):
        send(n, 0)
    for stage in range(places):
        for n in range(len(orders)):
            add(n, stage)
            if stage < places - 1:
                send(n, stage + 1)
    for group in copies:
        for copy in group:
            copy.wait_send()


def gather_all(shard, devices):
    places = devices.bit_length() - 1
    count = len(routes(places))
    out = pl.pallas_call(
        functools.partial(gather_kernel, places),
        out_shape=shaped((2,) * places + shard.shape, shard.dtype),
        in_specs=[pl.BlockSpec(memory_space=pltpu.VMEM)],
        out_specs=pl.BlockSpec(memory_space=pltpu.VMEM),
        scratch_shapes=[
            pltpu.SemaphoreType.DMA((count, places)),
            pltpu.SemaphoreType.DMA((count, places)),
            pltpu.SemaphoreType.DMA,
        ],
        compiler_params=pltpu.CompilerParams(
            collective_id=0, has_side_effects=True, vmem_limit_bytes=60 * 1024 * 1024
        ),
    )(shard)
    return out.reshape((devices,) + shard.shape)


def scatter_all(grads, devices):
    places = devices.bit_length() - 1
    count = len(routes(places))
    tail = grads.shape[1:]
    return pl.pallas_call(
        functools.partial(scatter_kernel, places),
        out_shape=shaped(tail, f32),
        in_specs=[pl.BlockSpec(memory_space=pltpu.VMEM)],
        out_specs=pl.BlockSpec(memory_space=pltpu.VMEM),
        scratch_shapes=[pltpu.VMEM((2,) * (places - 1) + tail, bf16)]
        + [pltpu.VMEM((2,) * (places - 1 - stage) + tail, bf16) for stage in range(places)]
        + [
            pltpu.SemaphoreType.DMA((count, places)),
            pltpu.SemaphoreType.DMA((count, places)),
        ],
        compiler_params=pltpu.CompilerParams(
            collective_id=1, has_side_effects=True, vmem_limit_bytes=60 * 1024 * 1024
        ),
    )(grads.reshape((2,) * places + tail))


def run(kernel, outs, args, scratch=(), flops=0):
    size = sum(a.size * a.dtype.itemsize for a in args)
    size += sum(a.size * a.dtype.itemsize for a in outs)
    return pl.pallas_call(
        kernel,
        out_shape=tuple(outs),
        in_specs=[pl.BlockSpec(memory_space=pltpu.VMEM)] * len(args),
        out_specs=tuple([pl.BlockSpec(memory_space=pltpu.VMEM)] * len(outs)),
        scratch_shapes=list(scratch),
        compiler_params=pltpu.CompilerParams(vmem_limit_bytes=60 * 1024 * 1024),
        cost_estimate=pl.CostEstimate(flops=flops, bytes_accessed=size, transcendentals=0),
    )(*args)


def shaped(shape, dtype):
    return jax.ShapeDtypeStruct(tuple(shape), dtype)


def offset_onehot(table_rows):
    places = jnp.arange(WIN * WIN, dtype=jnp.int32)
    row_at = places // WIN
    col_at = places % WIN
    index = (row_at[:, None] - row_at[None, :] + WIN - 1) * (2 * WIN - 1) + (
        col_at[:, None] - col_at[None, :] + WIN - 1
    )
    targets = jnp.arange(table_rows, dtype=jnp.int32)
    return (index.reshape(-1)[:, None] == targets[None, :]).astype(f32)


def token_places(shift_by):
    token = jnp.arange(SIDE * SIDE, dtype=jnp.int32)
    row = (token // SIDE - shift_by) % SIDE
    col = (token % SIDE - shift_by) % SIDE
    window = (row // WIN) * (SIDE // WIN) + col // WIN
    inside = (row % WIN) * WIN + col % WIN
    if shift_by:
        edges = SIDE - WIN, SIDE - shift_by
        a_row = (row >= edges[0]).astype(jnp.int32) + (row >= edges[1]).astype(jnp.int32)
        a_col = (col >= edges[0]).astype(jnp.int32) + (col >= edges[1]).astype(jnp.int32)
        label = 3 * a_row + a_col
    else:
        label = jnp.zeros_like(token)
    mask = jnp.where(label[:, None] == label[None, :], 0.0, mask_fill)
    mask = jnp.where(window[:, None] == window[None, :], mask, outside_fill).astype(f32)
    spread = (inside[:, None] == jnp.arange(WIN * WIN)[None, :]).astype(bf16)
    return mask, spread, spread.T


def local(
    images,
    cotangent,
    counts,
    *shards,
):
    devices = lax.axis_size("fsdp")
    gather_dims = (1, 1, 1, 2, 1, 1, 1, 1, 1, 1, 1, 1, 1)
    large_at = (2, 5, 9, 11)
    small_at = (0, 1, 3, 4, 6, 7, 8, 10, 12)
    flats = [tensor.reshape(-1) for tensor in shards]
    tokens, features = images.shape[1:]
    packed = jnp.concatenate([flats[n] for n in small_at])
    small_rows = 16 * -(-packed.shape[0] // (16 * features))
    packed = jnp.pad(packed, (0, small_rows * features - packed.shape[0]))
    blocks, spans = [packed.reshape(small_rows, features)], {}
    filled = small_rows
    for layer in range(LAYERS):
        for n in large_at:
            piece = shards[n][layer]
            rows, wide = piece.shape[0], piece.shape[1] // features
            piece = piece.reshape(rows, wide, features).transpose(1, 0, 2)
            blocks.append(piece.reshape(rows * wide, features))
            spans[n, layer] = (filled, rows, wide)
            filled += rows * wide
    spare = -filled % 16
    if spare:
        blocks.append(jnp.zeros((spare, features), bf16))
    gathered = gather_all(jnp.concatenate(blocks), devices)
    packed = gathered[:, :small_rows].reshape(devices, -1)
    weights = [None] * len(shards)
    at = 0
    for n in small_at:
        shape, axis_dim = shards[n].shape, gather_dims[n]
        size = flats[n].shape[0]
        piece = packed[:, at : at + size].reshape((devices,) + shape)
        piece = jnp.moveaxis(piece, 0, axis_dim)
        full = shape[:axis_dim] + (devices * shape[axis_dim],) + shape[axis_dim + 1 :]
        weights[n] = piece.reshape(full)
        at += size
    for n in large_at:
        weights[n] = [None] * LAYERS
        for layer in range(LAYERS):
            low, rows, wide = spans[n, layer]
            piece = gathered[:, low : low + rows * wide]
            piece = piece.reshape(devices, wide, rows, features).transpose(1, 0, 2, 3)
            piece = piece.reshape(wide, devices * rows, features)
            weights[n][layer] = piece if wide > 1 else piece[0]
    table = weights[4]
    heads = table.shape[-1]
    hidden = weights[10].shape[-1]
    cells = WIN * WIN
    onehot = offset_onehot(table.shape[1])
    pairs = jnp.einsum("pt,lth->lhp", onehot.astype(bf16), table, preferred_element_type=f32)
    pairs = pairs.reshape(LAYERS, heads, cells, cells).transpose(0, 1, 3, 2).astype(bf16)
    zero = jnp.zeros((features,), f32)

    def row(n, layer):
        return weights[n][layer].astype(f32).reshape(1, -1)

    active = counts[0] > 0
    current = images[0].astype(f32)
    saved = []
    for layer in range(LAYERS):
        mask, spread, spread_t = token_places(SHIFT if layer % 2 else 0)
        bias = run(
            bias_kernel,
            [shaped((heads, tokens, tokens), f32)],
            (pairs[layer], spread, spread_t, mask),
        )[0]
        b_qv = weights[3][layer].astype(f32)
        b_qkv = jnp.concatenate([b_qv[0], zero, b_qv[1]]).reshape(1, -1)
        attn = run(
            attn_fwd_kernel,
            [
                shaped((tokens, features), f32),
                shaped((tokens, features), bf16),
                shaped((tokens, 3 * features), bf16),
                shaped((features, tokens), bf16),
                shaped((heads, tokens, tokens), f32),
                shaped((features, tokens), bf16),
            ],
            (current, row(0, layer), row(1, layer), weights[2][layer], b_qkv, bias,
             weights[5][layer], row(6, layer)),
            [pltpu.VMEM((features, tokens), bf16)],
        )
        mlp = run(
            mlp_fwd_kernel,
            [
                shaped((tokens, features), f32),
                shaped((tokens, features), bf16),
                shaped((tokens, hidden), f32),
                shaped((tokens, hidden), bf16),
            ],
            (attn[0], row(7, layer), row(8, layer), weights[9][layer], row(10, layer),
             weights[11][layer], row(12, layer)),
        )
        saved.append((current, attn, mlp, spread, spread_t))
        current = mlp[0]
    outs = jnp.where(active, current, 0.0)[None]
    grad = jnp.where(active, cotangent[0].astype(f32), 0.0)
    sums = [[None] * LAYERS for _ in shards]
    owned = [[None] * LAYERS for _ in shards]

    def scatter(value):
        return value

    for layer in reversed(range(LAYERS)):
        entry, attn, mlp, spread, spread_t = saved[layer]
        g_mid, g_w1, g_w2, *rest = run(
            mlp_bwd_kernel,
            [
                shaped((tokens, features), f32),
                shaped((hidden // features, features, features), bf16),
                shaped((hidden, features), bf16),
                shaped((1, hidden), f32),
                shaped((1, features), f32),
                shaped((1, features), f32),
                shaped((1, features), f32),
                shaped((1, features), f32),
            ],
            (grad, attn[0], row(7, layer), weights[9][layer], weights[11][layer], *mlp[1:]),
        )
        sums[10][layer], sums[12][layer], sums[7][layer], sums[8][layer], sums[6][layer] = rest
        owned[11][layer] = scatter(g_w2)
        owned[9][layer] = scatter(g_w1)
        grad, g_qkv, g_proj, g_qv, g_pairs, g_gain, g_off = run(
            attn_bwd_kernel,
            [
                shaped((tokens, features), f32),
                shaped((3, features, features), bf16),
                shaped((features, features), bf16),
                shaped((2, features), f32),
                shaped((heads, cells, cells), f32),
                shaped((1, features), f32),
                shaped((1, features), f32),
            ],
            (g_mid, entry, row(0, layer), weights[2][layer], weights[5][layer], *attn[1:],
             spread, spread_t),
            [
                pltpu.VMEM((tokens, features), bf16),
                pltpu.VMEM((features, tokens), f32),
                pltpu.VMEM((tokens, 3 * features), bf16),
            ],
        )
        owned[5][layer] = scatter(g_proj)
        owned[2][layer] = scatter(g_qkv)
        sums[0][layer], sums[1][layer], sums[3][layer] = g_gain, g_off, g_qv
        per_pair = g_pairs.transpose(0, 2, 1).reshape(heads, cells * cells)
        sums[4][layer] = jnp.dot(per_pair, onehot, precision=lax.Precision.HIGHEST).T
    parts = []
    for n in small_at:
        shape, axis_dim = shards[n].shape, gather_dims[n]
        both = jnp.stack(sums[n])
        both = both.reshape(shape[:axis_dim] + (devices,) + shape[axis_dim:])
        parts.append(jnp.moveaxis(both, axis_dim, 0).reshape(devices, -1))
    packed = jnp.concatenate(parts, axis=1).astype(bf16)
    packed = jnp.pad(packed, ((0, 0), (0, small_rows * features - packed.shape[1])))
    blocks = [packed.reshape(devices, small_rows, features)]
    for layer in range(LAYERS):
        for n in large_at:
            low, rows, wide = spans[n, layer]
            piece = owned[n][layer].reshape(wide, devices, rows, features)
            blocks.append(piece.transpose(1, 0, 2, 3).reshape(devices, rows * wide, features))
    if spare:
        blocks.append(jnp.zeros((devices, spare, features), bf16))
    reduced = scatter_all(jnp.concatenate(blocks, axis=1), devices)
    summed = reduced[:small_rows].reshape(-1)
    at = 0
    for n in small_at:
        size = flats[n].shape[0]
        owned[n] = summed[at : at + size].reshape(shards[n].shape)
        at += size
    for n in large_at:
        for layer in range(LAYERS):
            low, rows, wide = spans[n, layer]
            piece = reduced[low : low + rows * wide].reshape(wide, rows, features)
            owned[n][layer] = piece.transpose(1, 0, 2).reshape(rows, wide * features)
        owned[n] = jnp.stack(owned[n])
    return (outs, grad[None], *owned)


def stack_rows(parts):
    return jnp.concatenate(parts, axis=0)


def permute_f32(matrix, rows):
    high = rows.astype(bf16)
    rest = rows - high.astype(f32)
    middle = rest.astype(bf16)
    low = (rest - middle.astype(f32)).astype(bf16)
    return dot_nn(matrix, high) + (dot_nn(matrix, middle) + dot_nn(matrix, low))


def slots_of(window):
    padded = -(-window // 8) * 8
    lanes_each = 64
    return padded, lanes_each


def places_in_windows(shift_by):
    token = np.arange(SIDE * SIDE)
    row = (token // SIDE - shift_by) % SIDE
    col = (token % SIDE - shift_by) % SIDE
    window = (row // WIN) * (SIDE // WIN) + col // WIN
    inside = (row % WIN) * WIN + col % WIN
    edges = SIDE - WIN, SIDE - shift_by
    a_row = (row >= edges[0]).astype(int) + (row >= edges[1]).astype(int)
    a_col = (col >= edges[0]).astype(int) + (col >= edges[1]).astype(int)
    return window, inside, 3 * a_row + a_col


def constants(heads, per_device_rows, devices):
    cells = WIN * WIN
    padded, wide = slots_of(cells)
    windows = (SIDE // WIN) ** 2
    tokens = SIDE * SIDE
    total = windows * padded
    perms = []
    for shift_by in (0, SHIFT):
        window, inside, label = places_in_windows(shift_by)
        perm = np.zeros((total, tokens), np.float32)
        perm[window * padded + inside, np.arange(tokens)] = 1.0
        perms.append(perm)
    mask = np.zeros((windows, padded, wide), np.float32)
    labels = np.zeros((windows, cells), int)
    labels[window, inside] = label
    mask[:, :cells, :cells] = np.where(labels[:, :, None] == labels[:, None, :], 0.0, mask_fill)
    group = 2 * lanes // wide
    mask = np.tile(mask, (1, 1, group))
    span = 2 * WIN - 1
    strips = -(-span * WIN // 16) * 16
    onehot = np.zeros((WIN, strips, devices * 8), np.float32)
    for c_q in range(WIN):
        for d_r in range(span):
            for c_k in range(WIN):
                t = d_r * span + c_q - c_k + WIN - 1
                spot = (t // per_device_rows) * 8 + t % per_device_rows
                onehot[c_q, (span - 1 - d_r) * WIN + c_k, spot] = 1.0
    onehot = onehot.reshape(WIN * strips, devices * 8)
    query = np.arange(heads * wide) % wide
    head = np.arange(heads * wide) // wide
    lane_row = np.where(query < cells, query // WIN, -1)
    lane_col = np.where(query < cells, query % WIN, -1)
    lane_of = np.zeros((8, heads * wide), np.int32)
    lane_of[0], lane_of[1] = lane_row, lane_col
    expand = np.zeros((lanes, heads * wide), np.float32)
    expand[head, np.arange(heads * wide)] = 1.0
    collect = np.zeros((heads * wide, lanes), np.float32)
    real = query < cells
    collect[np.arange(heads * wide)[real], (lane_col * heads + head)[real]] = 1.0
    fold = np.zeros((lanes, lanes), np.float32)
    for lane in range(WIN * heads):
        fold[lane, lane % heads] = 1.0
    plain, shifted = perms
    low = [plain, shifted, shifted @ plain.T, plain @ shifted.T, plain.T, shifted.T,
           onehot, onehot.T, expand, collect, fold]
    return [jnp.asarray(a, bf16) for a in low] + [jnp.asarray(lane_of), jnp.asarray(mask)]


class Links:
    def __init__(self, line, sems):
        me = lax.axis_index("fsdp")
        self.line = line
        self.core, self.x = lax.rem(me, 2), lax.rem(me // 2, 2)
        self.y, self.z = lax.rem(me // 4, 2), me // 8
        self.me = me
        self.sibling = me + 1 - 2 * self.core
        self.across = {"x": me + 2 - 4 * self.x, "y": me + 4 - 8 * self.y}
        low = lax.rem(me, 8)
        self.along = [lax.rem(self.z + k, line) * 8 + low for k in range(1, line)]
        self.sems = sems
        self.copies = {}

    def greet(self):
        barrier = pltpu.get_barrier_semaphore()
        peers = [self.sibling, self.across["x"], self.across["y"]] + self.along
        for peer in peers:
            pl.semaphore_signal(
                barrier, inc=1, device_id=(peer,), device_id_type=pl.DeviceIdType.MESH
            )
        pl.semaphore_wait(barrier, len(peers))

    def send(self, key, way, slot, source, target, peer):
        send_sem, recv_sem = self.sems[way]
        copy = pltpu.make_async_remote_copy(
            src_ref=source,
            dst_ref=target,
            send_sem=send_sem.at[key[1], slot],
            recv_sem=recv_sem.at[key[1], slot],
            device_id=(peer,),
            device_id_type=pl.DeviceIdType.MESH,
        )
        copy.start()
        self.copies.setdefault((way,) + key, []).append(copy)

    def arrive(self, way, key):
        for copy in self.copies[(way,) + key]:
            copy.wait_recv()

    def finish(self):
        for group in self.copies.values():
            for copy in group:
                copy.wait_send()


def all_kernel(
    line, spans,
    count_ref, x_ref, cot_ref, again_ref, aoff_ref, wqkv_ref, bqv_ref, rel_ref, wproj_ref, bproj_ref,
    mgain_ref, moff_ref, w1_ref, b1_ref, w2_ref, b2_ref,
    plain_ref, shifted_ref, forth_ref, back_ref, plain_t_ref, shifted_t_ref,
    onehot_ref, onehot_t_ref, expand_ref, collect_ref, fold_ref, lane_ref, mask_ref,
    out_ref, gin_ref, gagain_ref, gaoff_ref, gwqkv_ref, gbqv_ref, grel_ref, gwproj_ref, gbproj_ref,
    gmgain_ref, gmoff_ref, gw1_ref, gb1_ref, gw2_ref, gb2_ref,
    w, g, land_c, land_x, land_y, land_z, sm, sg, sland_c, sland_x, sland_y, sland_z,
    xs, xn_s, qkv_s, probs_s, mixed_s, mid_s, yn_s, slope_s, act_s,
    bias_s, strip_s, kinds_s, b1_s, own_s, mixf_s, dmix_s, dqkv_s, dsum_s, kg_s, b1g_s, rg_s,
    gs_send, gs_recv, rs_send, rs_recv,
):
    links = Links(line, {"g": (gs_send, gs_recv), "r": (rs_send, rs_recv)})
    c, x, y, z = links.core, links.x, links.y, links.z
    me = links.me
    devices = line * 8
    every = slice(None)
    rows_each = wqkv_ref.shape[1]
    features = wproj_ref.shape[2]
    hidden = w1_ref.shape[2]
    parts = wqkv_ref.shape[2] // features
    wide_parts = hidden // features
    deep = w2_ref.shape[1]
    table_each = rel_ref.shape[1]
    heads = rel_ref.shape[2]
    size = features // heads
    scaling = size ** (-0.5)
    at_proj = parts * rows_each
    at_one = at_proj + rows_each
    at_two = at_one + wide_parts * rows_each
    cells = WIN * WIN
    padded, wide = slots_of(cells)
    windows = (SIDE // WIN) ** 2
    per = lanes // size
    group_lanes = per * wide
    share = features // devices
    pack = lanes // share
    share_one = hidden // devices
    pack_one = lanes // share_one
    span = 2 * WIN - 1
    strips = -(-span * WIN // 16) * 16

    own_s[...] = jnp.zeros_like(own_s)
    at = 0
    for ref in (again_ref, aoff_ref, bqv_ref, bproj_ref, mgain_ref, moff_ref, b2_ref):
        piece = ref[...].astype(f32)
        if ref.shape[0] == LAYERS and len(ref.shape) == 3:
            for layer in range(LAYERS):
                own_s[at : at + ref.shape[1], 0:share] = piece[layer]
                at += ref.shape[1]
        else:
            own_s[at : at + LAYERS, 0:share] = piece
            at += LAYERS
    row_at = lax.broadcasted_iota(jnp.int32, (lanes, lanes), 0)
    lane_at = lax.broadcasted_iota(jnp.int32, (lanes, lanes), 1)
    spot = share * lax.rem(me, pack)
    place = jnp.where((lane_at == row_at + spot) & (row_at < share), 1.0, 0.0).astype(bf16)
    kinds = dot_nn(own_s[...].astype(bf16), place)
    spot = share_one * lax.rem(me, pack_one)
    place = jnp.where((lane_at == row_at + spot) & (row_at < share_one), 1.0, 0.0).astype(bf16)
    own_s[...] = jnp.zeros_like(own_s)
    own_s[0:LAYERS, 0:share_one] = b1_ref[...].astype(f32)
    firsts = dot_nn(own_s[...].astype(bf16), place)
    own_s[...] = jnp.zeros_like(own_s)
    for layer in range(LAYERS):
        own_s[layer * 8 : layer * 8 + table_each, 0:heads] = rel_ref[layer].astype(f32)
        own_s[layer * 8 + table_each : layer * 8 + table_each + 1, :] = firsts[layer : layer + 1]
    sm[z, y, x, c, :, 0:lanes] = kinds.astype(bf16)
    sm[z, y, x, c, :, lanes : 2 * lanes] = own_s[...].astype(bf16)
    for layer in range(LAYERS):
        for part in range(parts):
            w[layer, z, y, x, c, pl.ds(part * rows_each, rows_each), :] = (
                wqkv_ref[layer, :, part * features : (part + 1) * features]
            )
        w[layer, z, y, x, c, pl.ds(at_proj, rows_each), :] = wproj_ref[layer]
        for part in range(wide_parts):
            w[layer, z, y, x, c, pl.ds(at_one + part * rows_each, rows_each), :] = (
                w1_ref[layer, :, part * features : (part + 1) * features]
            )
        w[layer, z, y, x, c, pl.ds(at_two, deep), :] = w2_ref[layer]

    def view(where, n, picks):
        big, small = where
        span_n = spans[n]
        if span_n is None:
            return small.at[picks]
        layer, low, count, _ = span_n
        return big.at[(layer,) + picks + (pl.ds(low, count),)]

    def first_axis(n):
        return "y" if spans[n] is None else spans[n][3]

    def gather(n, stage):
        if stage:
            links.arrive("g", (stage - 1, n))
        if stage == 4:
            return
        axis = first_axis(n)
        if stage == 0:
            ref = view((w, sm), n, (z, y, x, c))
            for k, peer in enumerate(links.along):
                links.send((0, n), "g", k, ref, ref, peer)
            return
        if stage == 1:
            picks, peer = (every, y, x, c), links.across[axis]
        elif stage == 2:
            picks = (every, every, x, c) if axis == "y" else (every, y, every, c)
            peer = links.across["x" if axis == "y" else "y"]
        else:
            picks, peer = (every, every, every, c), links.sibling
        ref = view((w, sm), n, picks)
        links.send((stage, n), "g", line - 2 + stage, ref, ref, peer)

    def add_into(n, pick_of, landed, loops):
        def one(zi, carry):
            for a in range(loops[0]):
                for b in range(loops[1]):
                    here = view((g, sg), n, pick_of(zi, a, b))
                    here[...] = here[...] + landed(zi, a, b)[...]
            return carry

        lax.fori_loop(0, line, one, 0)

    def landing(refs, n, picks):
        return view(refs, n, picks)

    def scatter(n, stage):
        axis = first_axis(n)
        if stage:
            links.arrive("r", (stage - 1, n))
        if stage == 0:
            source = view((g, sg), n, (every, every, every, 1 - c))
            target = landing((land_c, sland_c), n, (every, every, every))
            links.send((0, n), "r", 0, source, target, links.sibling)
        elif stage == 1:
            add_into(
                n,
                lambda zi, a, b: (zi, a, b, c),
                lambda zi, a, b: landing((land_c, sland_c), n, (zi, a, b)),
                (2, 2),
            )
            if axis == "y":
                picks = (every, every, 1 - x, c)
            else:
                picks = (every, 1 - y, every, c)
            target = landing((land_x, sland_x), n, (every, every))
            peer = links.across["x" if axis == "y" else "y"]
            links.send((1, n), "r", 1, view((g, sg), n, picks), target, peer)
        elif stage == 2:
            add_into(
                n,
                lambda zi, a, b: (zi, b, x, c) if axis == "y" else (zi, y, b, c),
                lambda zi, a, b: landing((land_x, sland_x), n, (zi, b)),
                (1, 2),
            )
            picks = (every, 1 - y, x, c) if axis == "y" else (every, y, 1 - x, c)
            target = landing((land_y, sland_y), n, (every,))
            links.send((2, n), "r", 2, view((g, sg), n, picks), target, links.across[axis])
        elif stage == 3:
            add_into(
                n,
                lambda zi, a, b: (zi, y, x, c),
                lambda zi, a, b: landing((land_y, sland_y), n, (zi,)),
                (1, 1),
            )
            for k, peer in enumerate(links.along):
                source = view((g, sg), n, (lax.rem(z + k + 1, line), y, x, c))
                links.send((3, n), "r", 3 + k, source, landing((land_z, sland_z), n, (k,)), peer)
        else:
            if spans[n] is None:
                total = sg[z, y, x, c].astype(f32)
                for k in range(line - 1):
                    total = total + sland_z[k].astype(f32)
                small_out(total)
                return
            layer, low, count, _ = spans[n]
            for unit in range(low, low + count, rows_each):
                rows = pl.ds(unit, rows_each)
                total = g[layer, z, y, x, c, rows, :].astype(f32)
                for k in range(line - 1):
                    total = total + land_z[layer, k, rows, :].astype(f32)
                if unit < at_proj:
                    part = unit // rows_each
                    gwqkv_ref[layer, :, part * features : (part + 1) * features] = total
                elif unit < at_one:
                    gwproj_ref[layer] = total
                elif unit < at_two:
                    part = (unit - at_one) // rows_each
                    gw1_ref[layer, :, part * features : (part + 1) * features] = total
                else:
                    gw2_ref[layer, unit - at_two : unit - at_two + rows_each, :] = total

    def small_out(total):
        spot = share * lax.rem(me, pack)
        mine = jnp.where((lane_at == row_at + spot) & (row_at < share), 1.0, 0.0)
        picked = jnp.where(lax.broadcasted_iota(jnp.int32, (16, lanes), 1) // share == lax.rem(me, pack),
                           total[:, 0:lanes], 0.0)
        folded = picked[:, 0:share]
        for n in range(1, pack):
            folded = folded + picked[:, n * share : (n + 1) * share]
        at = 0
        for ref in (gagain_ref, gaoff_ref, gbqv_ref, gbproj_ref, gmgain_ref, gmoff_ref, gb2_ref):
            if len(ref.shape) == 3:
                for layer in range(LAYERS):
                    ref[layer] = folded[at : at + ref.shape[1]]
                    at += ref.shape[1]
            else:
                ref[...] = folded[at : at + LAYERS]
                at += LAYERS
        tail = total[:, lanes : 2 * lanes]
        for layer in range(LAYERS):
            grel_ref[layer] = tail[layer * 8 : layer * 8 + table_each, 0:heads]
            row = tail[layer * 8 + table_each : layer * 8 + table_each + 1]
            keep = lax.broadcasted_iota(jnp.int32, (1, lanes), 1) // share_one
            row = jnp.where(keep == lax.rem(me, pack_one), row, 0.0)
            folded_row = row[:, 0:share_one]
            for n in range(1, pack_one):
                folded_row = folded_row + row[:, n * share_one : (n + 1) * share_one]
            gb1_ref[layer : layer + 1, :] = folded_row

    def chunk_of(names):
        return [n for n, entry in enumerate(spans) if (entry is None) in names[:1] and False] or names

    def qkv_part(layer, part):
        block = w[layer, :, :, :, :, part * rows_each : (part + 1) * rows_each, :]
        return block.reshape(features, features)

    def proj():
        return None

    def proj_of(layer):
        return w[layer, :, :, :, :, at_proj : at_proj + rows_each, :].reshape(features, features)

    def one_of(layer, part):
        low = at_one + part * rows_each
        return w[layer, :, :, :, :, low : low + rows_each, :].reshape(features, features)

    def two_of(layer, part):
        return w[layer, part, :, :, :, at_two : at_two + deep, :].reshape(features, features)

    def put(layer, low, value):
        g[layer, :, :, :, :, low : low + rows_each, :] = value.astype(bf16).reshape(
            line, 2, 2, 2, rows_each, features
        )

    small_n = len(spans) - 1
    pairs = [[2 * p, 2 * p + 1] for p in range(small_n // 2)]
    gather_pairs = [[small_n] + pairs[0]] + pairs[1:]

    def gather_pair(p, stage):
        for n in gather_pairs[p]:
            gather(n, stage)

    def gather_tick(tick):
        for stage in (4, 3, 2, 1, 0):
            p = tick - stage
            if 0 <= p < len(gather_pairs):
                gather_pair(p, stage)

    links.greet()
    gather_tick(0)

    stream = dot_nn(plain_ref[...], x_ref[0])
    xs[0] = stream
    qkv_s[:, :, 48:64, :] = jnp.zeros((LAYERS, windows, 16, parts * features), bf16)
    dmix_s[:, 48:64, :] = jnp.zeros((windows, 16, features), bf16)
    strip_s[...] = jnp.zeros_like(strip_s)

    gather_tick(1)
    gather_tick(2)
    gather_tick(3)
    for n in gather_pairs[0]:
        links.arrive("g", (3, n))
    def later_tick(tick):
        for stage in (4, 3, 2, 1, 0):
            p = tick - stage
            if 0 < p < len(gather_pairs):
                gather_pair(p, stage)

    small = sm[...].reshape(devices, 16, 2 * lanes).astype(f32)
    for tile in range(features // lanes):
        block = small[tile * pack : (tile + 1) * pack, :, 0:lanes]
        kinds_s[:, tile * lanes : (tile + 1) * lanes] = jnp.sum(block, axis=0)
    for tile in range(hidden // lanes):
        total = small[tile * pack_one, :, lanes : 2 * lanes]
        for n in range(1, pack_one):
            total = total + small[tile * pack_one + n, :, lanes : 2 * lanes]
        for layer in range(LAYERS):
            at = layer * 8 + table_each
            b1_s[layer : layer + 1, tile * lanes : (tile + 1) * lanes] = total[at : at + 1]

    def kind(n):
        return kinds_s[n : n + 1, :]

    lane_row = lane_ref[0:1, :]
    lane_col = lane_ref[1:2, :]
    for layer in range(LAYERS):
        table = small[:, layer * 8 : (layer + 1) * 8, lanes : 2 * lanes]
        table = table.reshape(devices * 8, lanes).astype(bf16)
        spread = dot_nn(table, expand_ref[...]).astype(bf16)
        strip = jnp.zeros((strips, heads * wide), f32)
        for col in range(WIN):
            found = dot_nn(onehot_ref[col * strips : (col + 1) * strips, :], spread)
            strip = jnp.where(lane_col == col, found, strip)
        strip_s[0:strips, :] = strip
        bias = jnp.zeros((padded, heads * wide), f32)
        for row in range(WIN):
            low = (WIN - 1 - row) * WIN
            bias = jnp.where(lane_row == row, strip_s[low : low + padded, :], bias)
        key_at = lax.broadcasted_iota(jnp.int32, (padded, heads * wide), 0)
        bias_s[layer] = jnp.where(key_at < cells, bias, outside_fill)

    keeps = [head_mask(one, size) for one in range(per)]

    def diagonal(block):
        return stack_rows([block * keep for keep in keeps])

    def undiagonal(block):
        total = block[0:padded] * keeps[0].astype(f32)
        for n in range(1, per):
            total = total + block[n * wide : n * wide + padded] * keeps[n].astype(f32)
        return total

    def attention_forward(layer, ticks):
        rows = xs[layer]
        unit, _ = normalize(rows)
        xn = (unit * kind(layer) + kind(LAYERS + layer)).astype(bf16)
        xn_s[layer] = xn
        for part in range(parts):
            block = dot_nn(xn, qkv_part(layer, part))
            if part != 1:
                block = block + kind(2 * LAYERS + 2 * layer + part // 2)
            for window in range(windows):
                qkv_s[layer, window, 0:padded, part * features : (part + 1) * features] = (
                    block[window * padded : (window + 1) * padded].astype(bf16)
                )
        ticks.pop(0)()

        def group(n, carry):
            start = pl.multiple_of(n * lanes, lanes)
            bias = bias_s[layer, :, pl.ds(pl.multiple_of(n * group_lanes, lanes), group_lanes)]
            for window in range(windows):
                query = qkv_s[layer, window, :, pl.ds(start, lanes)]
                key = qkv_s[layer, window, 0:padded, pl.ds(pl.multiple_of(features + start, lanes), lanes)]
                value = qkv_s[layer, window, 0:padded, pl.ds(pl.multiple_of(2 * features + start, lanes), lanes)]
                scores = dot_nt(key, diagonal(query)) * scaling + bias
                if layer % 2:
                    scores = scores + mask_ref[window]
                raised = jnp.exp(scores - jnp.max(scores, axis=0, keepdims=True))
                probs = raised * (1.0 / jnp.sum(raised, axis=0, keepdims=True))
                probs_s[layer, n, window] = probs
                mixed = undiagonal(dot_tn(probs.astype(bf16), value))
                mixf_s[window * padded : (window + 1) * padded, pl.ds(start, lanes)] = mixed
            return carry

        lax.fori_loop(0, heads // per, group, 0)
        ticks.pop(0)()
        mixed = mixf_s[...].astype(bf16)
        mixed_s[layer] = mixed
        mid_s[layer] = rows + dot_nn(mixed, proj_of(layer)) + kind(4 * LAYERS + layer)

    def mlp_forward(layer, ticks):
        middle = mid_s[layer]
        unit, _ = normalize(middle)
        yn = (unit * kind(5 * LAYERS + layer) + kind(6 * LAYERS + layer)).astype(bf16)
        yn_s[layer] = yn
        for part in range(wide_parts):
            cols = slice(part * features, (part + 1) * features)
            pre = dot_nn(yn, one_of(layer, part)) + b1_s[layer : layer + 1, cols]
            cumul = 0.5 * (1.0 + lax.erf(pre * half_root))
            slope_s[layer, :, cols] = cumul + pre * (jnp.exp(-0.5 * pre * pre) * inv_root_tau)
            act_s[layer, :, cols] = (pre * cumul).astype(bf16)
        ticks.pop(0)()
        total = middle + kind(7 * LAYERS + layer)
        for part in range(wide_parts):
            cols = slice(part * features, (part + 1) * features)
            total = total + dot_nn(act_s[layer, :, cols], two_of(layer, part))
        return total

    nothing = lambda: None
    attention_forward(0, [lambda: later_tick(4), lambda: later_tick(5)])
    total = mlp_forward(0, [lambda: later_tick(6)])
    xs[1] = permute_f32(forth_ref[...], total)
    later_tick(7)
    attention_forward(1, [lambda: later_tick(8), nothing])
    later_tick(9)
    total = mlp_forward(1, [nothing])
    active = count_ref[0] > 0
    out_ref[0] = jnp.where(active, permute_f32(shifted_t_ref[...], total), 0.0)

    def mlp_backward(layer, grad, ticks):
        low = grad.astype(bf16)
        kg_s[7 * LAYERS + layer : 7 * LAYERS + layer + 1, :] = jnp.sum(grad, axis=0, keepdims=True)
        yn = yn_s[layer]
        g_yn = jnp.zeros_like(grad)
        for part in range(wide_parts):
            cols = slice(part * features, (part + 1) * features)
            g[layer, part, :, :, :, at_two : at_two + deep, :] = (
                dot_tn(act_s[layer, :, cols], low).astype(bf16).reshape(2, 2, 2, deep, features)
            )
            g_pre = dot_nt(low, two_of(layer, part)) * slope_s[layer, :, cols]
            b1g_s[layer : layer + 1, cols] = jnp.sum(g_pre, axis=0, keepdims=True)
            pre_low = g_pre.astype(bf16)
            put(layer, at_one + part * rows_each, dot_tn(yn, pre_low))
            g_yn = g_yn + dot_nt(pre_low, one_of(layer, part))
            ticks.pop(0)()
        back, g_gain, g_off = norm_pull(mid_s[layer], kind(5 * LAYERS + layer), g_yn)
        kg_s[5 * LAYERS + layer : 5 * LAYERS + layer + 1, :] = g_gain
        kg_s[6 * LAYERS + layer : 6 * LAYERS + layer + 1, :] = g_off
        g_mid = grad + back
        kg_s[4 * LAYERS + layer : 4 * LAYERS + layer + 1, :] = jnp.sum(g_mid, axis=0, keepdims=True)
        return g_mid

    def attention_backward(layer, g_mid, ticks):
        low = g_mid.astype(bf16)
        put(layer, at_proj, dot_tn(mixed_s[layer], low))
        d_mix = dot_nt(low, proj_of(layer))
        for window in range(windows):
            dmix_s[window, 0:padded, :] = d_mix[window * padded : (window + 1) * padded].astype(bf16)
        ticks.pop(0)()

        def group(n, carry):
            start = pl.multiple_of(n * lanes, lanes)
            k_at = pl.multiple_of(features + start, lanes)
            v_at = pl.multiple_of(2 * features + start, lanes)
            total = jnp.zeros((padded, group_lanes), f32)
            for window in range(windows):
                here = slice(window * padded, (window + 1) * padded)
                query = diagonal(qkv_s[layer, window, :, pl.ds(start, lanes)])
                key = qkv_s[layer, window, 0:padded, pl.ds(k_at, lanes)]
                value = qkv_s[layer, window, 0:padded, pl.ds(v_at, lanes)]
                d_out = diagonal(dmix_s[window, :, pl.ds(start, lanes)])
                probs = probs_s[layer, n, window]
                d_probs = dot_nt(value, d_out)
                dqkv_s[here, pl.ds(v_at, lanes)] = dot_nn(probs.astype(bf16), d_out)
                weighed = probs * d_probs
                d_scores = weighed - probs * jnp.sum(weighed, axis=0, keepdims=True)
                total = total + d_scores
                scores_low = d_scores.astype(bf16)
                dqkv_s[here, pl.ds(k_at, lanes)] = dot_nn(scores_low, query) * scaling
                dqkv_s[here, pl.ds(start, lanes)] = undiagonal(dot_tn(scores_low, key)) * scaling
            dsum_s[:, pl.ds(pl.multiple_of(n * group_lanes, lanes), group_lanes)] = total
            return carry

        lax.fori_loop(0, heads // per, group, 0)
        ticks.pop(0)()
        for n, part in ((0, 0), (1, 2)):
            column = jnp.sum(dqkv_s[:, part * features : (part + 1) * features], axis=0, keepdims=True)
            at = 2 * LAYERS + 2 * layer + n
            kg_s[at : at + 1, :] = column
        xn = xn_s[layer]
        g_xn = jnp.zeros_like(g_mid)
        for part in range(parts):
            block = dqkv_s[:, part * features : (part + 1) * features].astype(bf16)
            put(layer, part * rows_each, dot_tn(xn, block))
            g_xn = g_xn + dot_nt(block, qkv_part(layer, part))
        ticks.pop(0)()
        back, g_gain, g_off = norm_pull(xs[layer], kind(layer), g_xn)
        kg_s[layer : layer + 1, :] = g_gain
        kg_s[LAYERS + layer : LAYERS + layer + 1, :] = g_off
        strip_s[...] = jnp.zeros_like(strip_s)
        for row in range(WIN):
            at = (WIN - 1 - row) * WIN
            strip_s[at : at + padded, :] = strip_s[at : at + padded, :] + jnp.where(
                lane_row == row, dsum_s[...], 0.0
            )
        by_col = dot_nn(strip_s[0:strips, :].astype(bf16), collect_ref[...])
        col_at = lax.broadcasted_iota(jnp.int32, (1, lanes), 1) // heads
        stacked = stack_rows([jnp.where(col_at == col, by_col, 0.0).astype(bf16) for col in range(WIN)])
        table = dot_nn(onehot_t_ref[...], stacked)
        high = table.astype(bf16)
        rest = (table - high.astype(f32)).astype(bf16)
        table = dot_nn(high, fold_ref[...]) + dot_nn(rest, fold_ref[...])
        rg_s[:, layer * 8 : (layer + 1) * 8, :] = table.reshape(devices, 8, lanes)
        return g_mid + back

    def scatter_pairs(*steps):
        def act():
            for p, stage in steps:
                for n in pairs[p]:
                    scatter(n, stage)

        return act

    ab0, c0, d0, ab1, c1, d1 = range(6)
    grad = jnp.where(active, dot_nn(shifted_ref[...], cot_ref[0]), 0.0)
    g_mid = mlp_backward(1, grad, [nothing] * wide_parts)
    scatter_pairs((d1, 0), (c1, 0))()
    g_x = attention_backward(
        1,
        g_mid,
        [
            scatter_pairs((d1, 1)),
            scatter_pairs((d1, 2), (c1, 1)),
            scatter_pairs((ab1, 0), (d1, 3), (c1, 2)),
        ],
    )
    grad = permute_f32(back_ref[...], g_x)
    ticks = [
        scatter_pairs((ab1, 1)),
        scatter_pairs((c1, 3)),
        scatter_pairs((ab1, 2), (d1, 4)),
    ] + [nothing] * (wide_parts - 3)
    g_mid = mlp_backward(0, grad, ticks)
    scatter_pairs((d0, 0), (c0, 0), (ab1, 3))()
    g_x = attention_backward(
        0,
        g_mid,
        [
            scatter_pairs((d0, 1), (c1, 4)),
            scatter_pairs((d0, 2), (c0, 1), (ab1, 4)),
            scatter_pairs((ab0, 0), (d0, 3), (c0, 2), (ab0, 1)),
        ],
    )
    for tile in range(hidden // lanes):
        for n in range(pack_one):
            for layer in range(LAYERS):
                at = layer * 8 + table_each
                rg_s[tile * pack_one + n, at : at + 1, :] = (
                    b1g_s[layer : layer + 1, tile * lanes : (tile + 1) * lanes]
                )
    for tile in range(features // lanes):
        block = kg_s[:, tile * lanes : (tile + 1) * lanes].astype(bf16)
        for n in range(pack):
            device = tile * pack + n
            sg[device // 8, (device // 4) % 2, (device // 2) % 2, device % 2, :, 0:lanes] = block
    sg[:, :, :, :, :, lanes : 2 * lanes] = rg_s[...].astype(bf16).reshape(line, 2, 2, 2, 16, lanes)
    scatter(small_n, 0)
    gin_ref[0] = permute_f32(plain_t_ref[...], g_x)
    scatter(small_n, 1)
    scatter_pairs((c0, 3), (ab0, 2))()
    scatter(small_n, 2)
    scatter_pairs((d0, 4), (ab0, 3))()
    scatter(small_n, 3)
    scatter_pairs((c0, 4), (ab0, 4))()
    scatter(small_n, 4)
    links.finish()


def whole(devices):
    def local(images, cotangent, counts, *shards):
        line = devices // 8
        rows_each, features = shards[5].shape[1:]
        hidden = shards[9].shape[2]
        deep = shards[11].shape[1]
        parts, wide_parts = shards[2].shape[2] // features, hidden // features
        heads = shards[4].shape[2]
        cells = WIN * WIN
        padded, wide = slots_of(cells)
        windows = (SIDE // WIN) ** 2
        total = windows * padded
        tokens = images.shape[1]
        at_one = (parts + 1) * rows_each
        at_two = at_one + wide_parts * rows_each
        depth = at_two + deep
        spans = []
        for layer in range(LAYERS):
            for low, high in ((0, at_one), (at_one, at_two), (at_two, depth)):
                half = low + (high - low) // (2 * rows_each) * rows_each
                spans.append((layer, low, half - low, "y"))
                spans.append((layer, half, high - half, "x"))
        spans.append(None)
        consts = constants(heads, shards[4].shape[1], devices)
        args = [counts, images, cotangent, *shards, *consts]
        outs = [shaped(images.shape, f32), shaped(images.shape, f32)]
        outs += [shaped(s.shape, f32) for s in shards]
        vmem = pltpu.VMEM
        strips = -(-(2 * WIN - 1) * WIN // 16) * 16
        tall = (WIN - 1) * WIN + padded
        tall = max(-(-tall // 8) * 8, strips)
        scratch = [
            vmem((LAYERS, line, 2, 2, 2, depth, features), bf16),
            vmem((LAYERS, line, 2, 2, 2, depth, features), bf16),
            vmem((LAYERS, line, 2, 2, depth, features), bf16),
            vmem((LAYERS, line, 2, depth, features), bf16),
            vmem((LAYERS, line, depth, features), bf16),
            vmem((LAYERS, line - 1, depth, features), bf16),
            vmem((line, 2, 2, 2, 16, 2 * lanes), bf16),
            vmem((line, 2, 2, 2, 16, 2 * lanes), bf16),
            vmem((line, 2, 2, 16, 2 * lanes), bf16),
            vmem((line, 2, 16, 2 * lanes), bf16),
            vmem((line, 16, 2 * lanes), bf16),
            vmem((line - 1, 16, 2 * lanes), bf16),
            vmem((LAYERS, total, features), f32),
            vmem((LAYERS, total, features), bf16),
            vmem((LAYERS, windows, wide, parts * features), bf16),
            vmem((LAYERS, heads * wide // (2 * lanes), windows, padded, 2 * lanes), f32),
            vmem((LAYERS, total, features), bf16),
            vmem((LAYERS, total, features), f32),
            vmem((LAYERS, total, features), bf16),
            vmem((LAYERS, total, hidden), f32),
            vmem((LAYERS, total, hidden), bf16),
            vmem((LAYERS, padded, heads * wide), f32),
            vmem((tall, heads * wide), f32),
            vmem((16, features), f32),
            vmem((8, hidden), f32),
            vmem((16, lanes), f32),
            vmem((total, features), f32),
            vmem((windows, wide, features), bf16),
            vmem((total, parts * features), f32),
            vmem((padded, heads * wide), f32),
            vmem((16, features), f32),
            vmem((8, hidden), f32),
            vmem((devices, 16, lanes), f32),
        ] + [pltpu.SemaphoreType.DMA((len(spans), line + 2))] * 4
        space = pl.BlockSpec(memory_space=pltpu.VMEM)
        return pl.pallas_call(
            functools.partial(all_kernel, line, tuple(spans)),
            out_shape=tuple(outs),
            in_specs=[pl.BlockSpec(memory_space=pltpu.SMEM)] + [space] * (len(args) - 1),
            out_specs=tuple([space] * len(outs)),
            scratch_shapes=scratch,
            compiler_params=pltpu.CompilerParams(
                collective_id=2, has_side_effects=True, vmem_limit_bytes=63 * 1024 * 1024
            ),
        )(*args)

    return local


def fits_whole(devices, sizes):
    features, hidden, heads, table_rows = sizes
    if devices % 8 or devices < 16 or features % devices or hidden % devices or table_rows % devices:
        return False
    rows_each, share_one, table_each = features // devices, hidden // devices, table_rows // devices
    return (
        rows_each % 16 == 0
        and lanes % rows_each == 0
        and lanes % share_one == 0
        and table_each <= 7
        and hidden * 8 == features * devices
        and lanes * heads == 4 * features
        and WIN * heads <= lanes
        and LAYERS == 2
    )


def solution(mesh):
    in_specs = (
        P("fsdp", None, None),
        P("fsdp", None, None),
        P("fsdp"),
        P(None, "fsdp"),
        P(None, "fsdp"),
        P(None, "fsdp", None),
        P(None, None, "fsdp"),
        P(None, "fsdp", None),
        P(None, "fsdp", None),
        P(None, "fsdp"),
        P(None, "fsdp"),
        P(None, "fsdp"),
        P(None, "fsdp", None),
        P(None, "fsdp"),
        P(None, "fsdp", None),
        P(None, "fsdp"),
    )
    out_specs = (
        P("fsdp", None, None),
        P("fsdp", None, None),
        P(None, "fsdp"),
        P(None, "fsdp"),
        P(None, "fsdp", None),
        P(None, None, "fsdp"),
        P(None, "fsdp", None),
        P(None, "fsdp", None),
        P(None, "fsdp"),
        P(None, "fsdp"),
        P(None, "fsdp"),
        P(None, "fsdp", None),
        P(None, "fsdp"),
        P(None, "fsdp", None),
        P(None, "fsdp"),
    )
    devices = mesh.shape["fsdp"]

    def step(images, cotangent, counts, *params):
        sizes = (images.shape[2], params[9].shape[2], params[4].shape[2], params[4].shape[1])
        body = whole(devices) if fits_whole(devices, sizes) else local
        return jax.shard_map(
            body, mesh=mesh, in_specs=in_specs, out_specs=out_specs, check_vma=False
        )(images, cotangent, counts, *params)

    return step
```

```python
import functools

import jax
import jax.numpy as jnp
import numpy as np
from jax import lax
from jax.experimental import pallas as pl
from jax.experimental.pallas import tpu as pltpu
from jax.sharding import PartitionSpec as P

WIN = 7
SIDE = 14
LAYERS = 2
SHIFT = 3

norm_eps = 1e-05
mask_fill = -10000.0
outside_fill = -1e30
half_root = 0.7071067811865476
inv_root_tau = 0.3989422804014327
lanes = 128
bf16 = jnp.bfloat16
f32 = jnp.float32


def dot_nn(left, right):
    return lax.dot_general(left, right, (((1,), (0,)), ((), ())), preferred_element_type=f32)


def dot_nt(left, right):
    return lax.dot_general(left, right, (((1,), (1,)), ((), ())), preferred_element_type=f32)


def dot_tn(left, right):
    return lax.dot_general(left, right, (((0,), (0,)), ((), ())), preferred_element_type=f32)


def normalize(rows):
    centred = rows - jnp.mean(rows, axis=-1, keepdims=True)
    spread = jnp.mean(centred * centred, axis=-1, keepdims=True)
    inverse = lax.rsqrt(spread + norm_eps)
    return centred * inverse, inverse


def norm_pull(rows, gain, grad):
    unit, inverse = normalize(rows)
    g_gain = jnp.sum(grad * unit, axis=0, keepdims=True)
    g_bias = jnp.sum(grad, axis=0, keepdims=True)
    scaled = grad * gain
    back = inverse * (
        scaled
        - jnp.mean(scaled, axis=-1, keepdims=True)
        - unit * jnp.mean(scaled * unit, axis=-1, keepdims=True)
    )
    return back, g_gain, g_bias


def head_mask(local_head, head_size):
    lane = lax.broadcasted_iota(jnp.int32, (1, lanes), 1)
    return jnp.where(lane // head_size == local_head, 1.0, 0.0).astype(bf16)


def bias_kernel(pairs_ref, spread_ref, spread_t_ref, mask_ref, out_ref):
    def step(head, carry):
        rows = dot_nn(spread_ref[...], pairs_ref[head]).astype(bf16)
        out_ref[head] = dot_nn(rows, spread_t_ref[...]) + mask_ref[...]
        return carry

    lax.fori_loop(0, pairs_ref.shape[0], step, 0)


def attn_fwd_kernel(
    x_ref, gain_ref, off_ref, wqkv_ref, bqkv_ref, bias_ref, wproj_ref, bproj_ref,
    mid_ref, xn_ref, qkv_ref, key_t_ref, probs_ref, mixed_t_ref,
    val_t,
):
    rows = x_ref[...]
    features = rows.shape[1]
    heads = bias_ref.shape[0]
    size = features // heads
    scaling = size ** (-0.5)
    unit, _ = normalize(rows)
    xn = (unit * gain_ref[...] + off_ref[...]).astype(bf16)
    xn_ref[...] = xn
    for part in range(3):
        cols = pl.ds(part * features, features)
        block = dot_nn(xn, wqkv_ref[part]) + bqkv_ref[:, cols]
        qkv_ref[:, cols] = block.astype(bf16)
        if part == 1:
            key_t_ref[...] = block.T.astype(bf16)
        if part == 2:
            val_t[...] = block.T.astype(bf16)
    per = lanes // size

    def group(g, carry):
        start = pl.multiple_of(g * lanes, lanes)
        query = qkv_ref[:, pl.ds(start, lanes)]
        keys = qkv_ref[:, pl.ds(pl.multiple_of(features + start, lanes), lanes)]
        for one in range(per):
            head = g * per + one
            at = pl.ds(pl.multiple_of(head * size, size), size)
            scores = dot_nt(keys * head_mask(one, size), query) * scaling + bias_ref[head]
            peak = jnp.max(scores, axis=0, keepdims=True)
            raised = jnp.exp(scores - peak)
            total = jnp.sum(raised, axis=0, keepdims=True)
            probs = raised * (1.0 / total)
            probs_ref[head] = probs
            mixed_t_ref[at, :] = dot_nn(val_t[at, :], probs.astype(bf16)).astype(bf16)
        return carry

    lax.fori_loop(0, heads // per, group, 0)
    mixed = mixed_t_ref[...].astype(f32).T.astype(bf16)
    mid_ref[...] = rows + dot_nn(mixed, wproj_ref[...]) + bproj_ref[...]


def mlp_fwd_kernel(
    mid_ref, gain_ref, off_ref, w1_ref, b1_ref, w2_ref, b2_ref,
    out_ref, yn_ref, slope_ref, act_ref,
):
    middle = mid_ref[...]
    features = middle.shape[1]
    unit, _ = normalize(middle)
    yn = (unit * gain_ref[...] + off_ref[...]).astype(bf16)
    yn_ref[...] = yn
    total = middle + b2_ref[...]
    for chunk in range(w1_ref.shape[0]):
        cols = pl.ds(chunk * features, features)
        pre = dot_nn(yn, w1_ref[chunk]) + b1_ref[:, cols]
        cumul = 0.5 * (1.0 + lax.erf(pre * half_root))
        slope_ref[:, cols] = cumul + pre * (jnp.exp(-0.5 * pre * pre) * inv_root_tau)
        act = (pre * cumul).astype(bf16)
        act_ref[:, cols] = act
        total = total + dot_nn(act, w2_ref[cols, :])
    out_ref[...] = total


def mlp_bwd_kernel(
    g_ref, mid_ref, gain_ref, w1_ref, w2_ref, yn_ref, slope_ref, act_ref,
    gm_ref, gw1_ref, gw2_ref, gb1_ref, gb2_ref, ggain_ref, goff_ref, gbproj_ref,
):
    grad = g_ref[...]
    features = grad.shape[1]
    low = grad.astype(bf16)
    gb2_ref[...] = jnp.sum(grad, axis=0, keepdims=True)
    yn = yn_ref[...]
    g_yn = jnp.zeros_like(grad)
    for chunk in range(w1_ref.shape[0]):
        cols = pl.ds(chunk * features, features)
        gw2_ref[cols, :] = dot_tn(act_ref[:, cols], low).astype(bf16)
        g_pre = dot_nt(low, w2_ref[cols, :]) * slope_ref[:, cols]
        gb1_ref[:, cols] = jnp.sum(g_pre, axis=0, keepdims=True)
        pre_low = g_pre.astype(bf16)
        gw1_ref[chunk] = dot_tn(yn, pre_low).astype(bf16)
        g_yn = g_yn + dot_nt(pre_low, w1_ref[chunk])
    back, g_gain, g_off = norm_pull(mid_ref[...], gain_ref[...], g_yn)
    ggain_ref[...] = g_gain
    goff_ref[...] = g_off
    g_mid = grad + back
    gm_ref[...] = g_mid
    gbproj_ref[...] = jnp.sum(g_mid, axis=0, keepdims=True)


def attn_bwd_kernel(
    gm_ref, x_ref, gain_ref, wqkv_ref, wproj_ref, xn_ref, qkv_ref, key_t_ref, probs_ref,
    mixed_t_ref, spread_ref, spread_t_ref,
    gx_ref, gwqkv_ref, gwproj_ref, gqv_ref, gpairs_ref, ggain_ref, goff_ref,
    dmix, dq_t, dqkv,
):
    g_mid = gm_ref[...]
    features = g_mid.shape[1]
    heads = probs_ref.shape[0]
    size = features // heads
    scaling = size ** (-0.5)
    low = g_mid.astype(bf16)
    gwproj_ref[...] = dot_nn(mixed_t_ref[...], low).astype(bf16)
    dmix[...] = dot_nt(low, wproj_ref[...]).astype(bf16)
    per = lanes // size

    def group(g, carry):
        start = pl.multiple_of(g * lanes, lanes)
        k_at = pl.multiple_of(features + start, lanes)
        v_at = pl.multiple_of(2 * features + start, lanes)
        query = qkv_ref[:, pl.ds(start, lanes)]
        values = qkv_ref[:, pl.ds(v_at, lanes)]
        d_mix = dmix[:, pl.ds(start, lanes)]
        d_keys = jnp.zeros(query.shape, f32)
        d_values = jnp.zeros(query.shape, f32)
        for one in range(per):
            head = g * per + one
            at = pl.ds(pl.multiple_of(head * size, size), size)
            keep = head_mask(one, size)
            probs = probs_ref[head]
            d_probs = dot_nt(values * keep, d_mix)
            d_values = d_values + dot_nn(probs.astype(bf16), d_mix * keep)
            weighed = probs * d_probs
            d_scores = weighed - probs * jnp.sum(weighed, axis=0, keepdims=True)
            scores_low = d_scores.astype(bf16)
            d_keys = d_keys + dot_nn(scores_low, query * keep)
            dq_t[at, :] = dot_nn(key_t_ref[at, :], scores_low)
            folded = dot_nn(spread_t_ref[...], scores_low).astype(bf16)
            gpairs_ref[head] = dot_nn(folded, spread_ref[...])
        dqkv[:, pl.ds(k_at, lanes)] = (d_keys * scaling).astype(bf16)
        dqkv[:, pl.ds(v_at, lanes)] = d_values.astype(bf16)
        gqv_ref[1:2, pl.ds(start, lanes)] = jnp.sum(d_values, axis=0, keepdims=True)
        return carry

    lax.fori_loop(0, heads // per, group, 0)
    d_query = dq_t[...].T * scaling
    gqv_ref[0:1, :] = jnp.sum(d_query, axis=0, keepdims=True)
    dqkv[:, :features] = d_query.astype(bf16)
    xn = xn_ref[...]
    g_xn = jnp.zeros_like(g_mid)
    for part in range(3):
        cols = pl.ds(part * features, features)
        block = dqkv[:, cols]
        gwqkv_ref[part] = dot_tn(xn, block).astype(bf16)
        g_xn = g_xn + dot_nt(block, wqkv_ref[part])
    back, g_gain, g_off = norm_pull(x_ref[...], gain_ref[...], g_xn)
    ggain_ref[...] = g_gain
    goff_ref[...] = g_off
    gx_ref[...] = g_mid + back


def bit_of(index, place):
    return lax.rem(index // (1 << place), 2)


def peers_of(me, places):
    return [me + (1 - 2 * bit_of(me, place)) * (1 << place) for place in range(places)]


def greet(me, places):
    barrier = pltpu.get_barrier_semaphore()
    for peer in peers_of(me, places):
        pl.semaphore_signal(
            barrier, inc=1, device_id=(peer,), device_id_type=pl.DeviceIdType.MESH
        )
    pl.semaphore_wait(barrier, places)


def routes(places):
    high = list(range(places - 1, 2, -1))
    if places < 3:
        return [list(range(places - 1, -1, -1))]
    return [
        high + [2, 1, 0],
        high + [1, 2, 0],
        [2] + high + [1, 0],
        [1] + high + [2, 0],
    ]


def row_parts(total, count):
    units = total // 16
    sizes = [16 * (units // count + (1 if n < units % count else 0)) for n in range(count)]
    return [(sum(sizes[:n]), sizes[n]) for n in range(count)]


def region(places, free, me, lowest=0, forced=None):
    picks = []
    for place in range(places - 1, lowest - 1, -1):
        if forced is not None and place == forced[0]:
            picks.append(forced[1])
        elif place in free:
            picks.append(slice(None))
        else:
            picks.append(bit_of(me, place))
    return tuple(picks)


def gather_kernel(places, x_ref, out_ref, send_sem, recv_sem, own_sem):
    me = lax.axis_index("fsdp")
    peers = peers_of(me, places)
    greet(me, places)
    own = pltpu.make_async_copy(x_ref, out_ref.at[region(places, (), me)], own_sem)
    own.start()
    orders = routes(places)
    parts = row_parts(x_ref.shape[0], len(orders))
    copies = [[] for _ in orders]
    for stage in range(places):
        for n, (order, (low, size)) in enumerate(zip(orders, parts)):
            rows = pl.ds(low, size)
            place = order[stage]
            if stage == 1 and n == 0:
                own.wait()
            if stage:
                copies[n][-1].wait_recv()
            here = region(places, order[:stage], me)
            target = out_ref.at[here + (rows,)]
            copy = pltpu.make_async_remote_copy(
                src_ref=x_ref.at[rows] if stage == 0 else target,
                dst_ref=target,
                send_sem=send_sem.at[n, stage],
                recv_sem=recv_sem.at[n, stage],
                device_id=(peers[place],),
                device_id_type=pl.DeviceIdType.MESH,
            )
            copy.start()
            copies[n].append(copy)
    for group in copies:
        group[-1].wait_recv()
    for group in copies:
        for copy in group:
            copy.wait_send()


def scatter_kernel(places, g_ref, out_ref, acc, *rest):
    landings, (send_sem, recv_sem) = rest[:places], rest[places:]
    me = lax.axis_index("fsdp")
    peers = peers_of(me, places)
    greet(me, places)
    orders = [order[::-1] for order in routes(places)]
    parts = row_parts(g_ref.shape[-2], len(orders))
    everything = set(range(places))
    copies = [[None] * places for _ in orders]

    def send(n, stage):
        order, (low, size) = orders[n], parts[n]
        rows = pl.ds(low, size)
        place = order[stage]
        free = everything - set(order[: stage + 1])
        away = (place, 1 - bit_of(me, place))
        if stage == 0:
            source = g_ref.at[region(places, free, me, 0, away) + (rows,)]
        else:
            source = acc.at[region(places, free, me, 1, away) + (rows,)]
        copy = pltpu.make_async_remote_copy(
            src_ref=source,
            dst_ref=landings[stage].at[(slice(None),) * len(free) + (rows,)],
            send_sem=send_sem.at[n, stage],
            recv_sem=recv_sem.at[n, stage],
            device_id=(peers[place],),
            device_id_type=pl.DeviceIdType.MESH,
        )
        copy.start()
        copies[n][stage] = copy

    def add(n, stage):
        order, (low, size) = orders[n], parts[n]
        rows = pl.ds(low, size)
        free = sorted(everything - set(order[: stage + 1]), reverse=True)
        copies[n][stage].wait_recv()

        def one(at, carry):
            values = {}
            for spot, place in enumerate(free):
                values[place] = lax.rem(at // (1 << (len(free) - 1 - spot)), 2)
            full = tuple(
                values[place] if place in values else bit_of(me, place)
                for place in range(places - 1, -1, -1)
            )
            kept = full[:-1] + (rows,)
            landed = landings[stage][tuple(values[place] for place in free) + (rows,)]
            if stage == 0:
                acc[kept] = g_ref[full + (rows,)] + landed
            elif stage < places - 1:
                acc[kept] = acc[kept] + landed
            else:
                out_ref[rows] = acc[kept].astype(f32) + landed.astype(f32)
            return carry

        lax.fori_loop(0, 1 << len(free), one, 0)

    for n in range(len(orders)):
        send(n, 0)
    for stage in range(places):
        for n in range(len(orders)):
            add(n, stage)
            if stage < places - 1:
                send(n, stage + 1)
    for group in copies:
        for copy in group:
            copy.wait_send()


def gather_all(shard, devices):
    places = devices.bit_length() - 1
    count = len(routes(places))
    out = pl.pallas_call(
        functools.partial(gather_kernel, places),
        out_shape=shaped((2,) * places + shard.shape, shard.dtype),
        in_specs=[pl.BlockSpec(memory_space=pltpu.VMEM)],
        out_specs=pl.BlockSpec(memory_space=pltpu.VMEM),
        scratch_shapes=[
            pltpu.SemaphoreType.DMA((count, places)),
            pltpu.SemaphoreType.DMA((count, places)),
            pltpu.SemaphoreType.DMA,
        ],
        compiler_params=pltpu.CompilerParams(
            collective_id=0, has_side_effects=True, vmem_limit_bytes=60 * 1024 * 1024
        ),
    )(shard)
    return out.reshape((devices,) + shard.shape)


def scatter_all(grads, devices):
    places = devices.bit_length() - 1
    count = len(routes(places))
    tail = grads.shape[1:]
    return pl.pallas_call(
        functools.partial(scatter_kernel, places),
        out_shape=shaped(tail, f32),
        in_specs=[pl.BlockSpec(memory_space=pltpu.VMEM)],
        out_specs=pl.BlockSpec(memory_space=pltpu.VMEM),
        scratch_shapes=[pltpu.VMEM((2,) * (places - 1) + tail, bf16)]
        + [pltpu.VMEM((2,) * (places - 1 - stage) + tail, bf16) for stage in range(places)]
        + [
            pltpu.SemaphoreType.DMA((count, places)),
            pltpu.SemaphoreType.DMA((count, places)),
        ],
        compiler_params=pltpu.CompilerParams(
            collective_id=1, has_side_effects=True, vmem_limit_bytes=60 * 1024 * 1024
        ),
    )(grads.reshape((2,) * places + tail))


def run(kernel, outs, args, scratch=(), flops=0):
    size = sum(a.size * a.dtype.itemsize for a in args)
    size += sum(a.size * a.dtype.itemsize for a in outs)
    return pl.pallas_call(
        kernel,
        out_shape=tuple(outs),
        in_specs=[pl.BlockSpec(memory_space=pltpu.VMEM)] * len(args),
        out_specs=tuple([pl.BlockSpec(memory_space=pltpu.VMEM)] * len(outs)),
        scratch_shapes=list(scratch),
        compiler_params=pltpu.CompilerParams(vmem_limit_bytes=60 * 1024 * 1024),
        cost_estimate=pl.CostEstimate(flops=flops, bytes_accessed=size, transcendentals=0),
    )(*args)


def shaped(shape, dtype):
    return jax.ShapeDtypeStruct(tuple(shape), dtype)


def offset_onehot(table_rows):
    places = jnp.arange(WIN * WIN, dtype=jnp.int32)
    row_at = places // WIN
    col_at = places % WIN
    index = (row_at[:, None] - row_at[None, :] + WIN - 1) * (2 * WIN - 1) + (
        col_at[:, None] - col_at[None, :] + WIN - 1
    )
    targets = jnp.arange(table_rows, dtype=jnp.int32)
    return (index.reshape(-1)[:, None] == targets[None, :]).astype(f32)


def token_places(shift_by):
    token = jnp.arange(SIDE * SIDE, dtype=jnp.int32)
    row = (token // SIDE - shift_by) % SIDE
    col = (token % SIDE - shift_by) % SIDE
    window = (row // WIN) * (SIDE // WIN) + col // WIN
    inside = (row % WIN) * WIN + col % WIN
    if shift_by:
        edges = SIDE - WIN, SIDE - shift_by
        a_row = (row >= edges[0]).astype(jnp.int32) + (row >= edges[1]).astype(jnp.int32)
        a_col = (col >= edges[0]).astype(jnp.int32) + (col >= edges[1]).astype(jnp.int32)
        label = 3 * a_row + a_col
    else:
        label = jnp.zeros_like(token)
    mask = jnp.where(label[:, None] == label[None, :], 0.0, mask_fill)
    mask = jnp.where(window[:, None] == window[None, :], mask, outside_fill).astype(f32)
    spread = (inside[:, None] == jnp.arange(WIN * WIN)[None, :]).astype(bf16)
    return mask, spread, spread.T


def local(
    images,
    cotangent,
    counts,
    *shards,
):
    devices = lax.axis_size("fsdp")
    gather_dims = (1, 1, 1, 2, 1, 1, 1, 1, 1, 1, 1, 1, 1)
    large_at = (2, 5, 9, 11)
    small_at = (0, 1, 3, 4, 6, 7, 8, 10, 12)
    flats = [tensor.reshape(-1) for tensor in shards]
    tokens, features = images.shape[1:]
    packed = jnp.concatenate([flats[n] for n in small_at])
    small_rows = 16 * -(-packed.shape[0] // (16 * features))
    packed = jnp.pad(packed, (0, small_rows * features - packed.shape[0]))
    blocks, spans = [packed.reshape(small_rows, features)], {}
    filled = small_rows
    for layer in range(LAYERS):
        for n in large_at:
            piece = shards[n][layer]
            rows, wide = piece.shape[0], piece.shape[1] // features
            piece = piece.reshape(rows, wide, features).transpose(1, 0, 2)
            blocks.append(piece.reshape(rows * wide, features))
            spans[n, layer] = (filled, rows, wide)
            filled += rows * wide
    spare = -filled % 16
    if spare:
        blocks.append(jnp.zeros((spare, features), bf16))
    gathered = gather_all(jnp.concatenate(blocks), devices)
    packed = gathered[:, :small_rows].reshape(devices, -1)
    weights = [None] * len(shards)
    at = 0
    for n in small_at:
        shape, axis_dim = shards[n].shape, gather_dims[n]
        size = flats[n].shape[0]
        piece = packed[:, at : at + size].reshape((devices,) + shape)
        piece = jnp.moveaxis(piece, 0, axis_dim)
        full = shape[:axis_dim] + (devices * shape[axis_dim],) + shape[axis_dim + 1 :]
        weights[n] = piece.reshape(full)
        at += size
    for n in large_at:
        weights[n] = [None] * LAYERS
        for layer in range(LAYERS):
            low, rows, wide = spans[n, layer]
            piece = gathered[:, low : low + rows * wide]
            piece = piece.reshape(devices, wide, rows, features).transpose(1, 0, 2, 3)
            piece = piece.reshape(wide, devices * rows, features)
            weights[n][layer] = piece if wide > 1 else piece[0]
    table = weights[4]
    heads = table.shape[-1]
    hidden = weights[10].shape[-1]
    cells = WIN * WIN
    onehot = offset_onehot(table.shape[1])
    pairs = jnp.einsum("pt,lth->lhp", onehot.astype(bf16), table, preferred_element_type=f32)
    pairs = pairs.reshape(LAYERS, heads, cells, cells).transpose(0, 1, 3, 2).astype(bf16)
    zero = jnp.zeros((features,), f32)

    def row(n, layer):
        return weights[n][layer].astype(f32).reshape(1, -1)

    active = counts[0] > 0
    current = images[0].astype(f32)
    saved = []
    for layer in range(LAYERS):
        mask, spread, spread_t = token_places(SHIFT if layer % 2 else 0)
        bias = run(
            bias_kernel,
            [shaped((heads, tokens, tokens), f32)],
            (pairs[layer], spread, spread_t, mask),
        )[0]
        b_qv = weights[3][layer].astype(f32)
        b_qkv = jnp.concatenate([b_qv[0], zero, b_qv[1]]).reshape(1, -1)
        attn = run(
            attn_fwd_kernel,
            [
                shaped((tokens, features), f32),
                shaped((tokens, features), bf16),
                shaped((tokens, 3 * features), bf16),
                shaped((features, tokens), bf16),
                shaped((heads, tokens, tokens), f32),
                shaped((features, tokens), bf16),
            ],
            (current, row(0, layer), row(1, layer), weights[2][layer], b_qkv, bias,
             weights[5][layer], row(6, layer)),
            [pltpu.VMEM((features, tokens), bf16)],
        )
        mlp = run(
            mlp_fwd_kernel,
            [
                shaped((tokens, features), f32),
                shaped((tokens, features), bf16),
                shaped((tokens, hidden), f32),
                shaped((tokens, hidden), bf16),
            ],
            (attn[0], row(7, layer), row(8, layer), weights[9][layer], row(10, layer),
             weights[11][layer], row(12, layer)),
        )
        saved.append((current, attn, mlp, spread, spread_t))
        current = mlp[0]
    outs = jnp.where(active, current, 0.0)[None]
    grad = jnp.where(active, cotangent[0].astype(f32), 0.0)
    sums = [[None] * LAYERS for _ in shards]
    owned = [[None] * LAYERS for _ in shards]

    def scatter(value):
        return value

    for layer in reversed(range(LAYERS)):
        entry, attn, mlp, spread, spread_t = saved[layer]
        g_mid, g_w1, g_w2, *rest = run(
            mlp_bwd_kernel,
            [
                shaped((tokens, features), f32),
                shaped((hidden // features, features, features), bf16),
                shaped((hidden, features), bf16),
                shaped((1, hidden), f32),
                shaped((1, features), f32),
                shaped((1, features), f32),
                shaped((1, features), f32),
                shaped((1, features), f32),
            ],
            (grad, attn[0], row(7, layer), weights[9][layer], weights[11][layer], *mlp[1:]),
        )
        sums[10][layer], sums[12][layer], sums[7][layer], sums[8][layer], sums[6][layer] = rest
        owned[11][layer] = scatter(g_w2)
        owned[9][layer] = scatter(g_w1)
        grad, g_qkv, g_proj, g_qv, g_pairs, g_gain, g_off = run(
            attn_bwd_kernel,
            [
                shaped((tokens, features), f32),
                shaped((3, features, features), bf16),
                shaped((features, features), bf16),
                shaped((2, features), f32),
                shaped((heads, cells, cells), f32),
                shaped((1, features), f32),
                shaped((1, features), f32),
            ],
            (g_mid, entry, row(0, layer), weights[2][layer], weights[5][layer], *attn[1:],
             spread, spread_t),
            [
                pltpu.VMEM((tokens, features), bf16),
                pltpu.VMEM((features, tokens), f32),
                pltpu.VMEM((tokens, 3 * features), bf16),
            ],
        )
        owned[5][layer] = scatter(g_proj)
        owned[2][layer] = scatter(g_qkv)
        sums[0][layer], sums[1][layer], sums[3][layer] = g_gain, g_off, g_qv
        per_pair = g_pairs.transpose(0, 2, 1).reshape(heads, cells * cells)
        sums[4][layer] = jnp.dot(per_pair, onehot, precision=lax.Precision.HIGHEST).T
    parts = []
    for n in small_at:
        shape, axis_dim = shards[n].shape, gather_dims[n]
        both = jnp.stack(sums[n])
        both = both.reshape(shape[:axis_dim] + (devices,) + shape[axis_dim:])
        parts.append(jnp.moveaxis(both, axis_dim, 0).reshape(devices, -1))
    packed = jnp.concatenate(parts, axis=1).astype(bf16)
    packed = jnp.pad(packed, ((0, 0), (0, small_rows * features - packed.shape[1])))
    blocks = [packed.reshape(devices, small_rows, features)]
    for layer in range(LAYERS):
        for n in large_at:
            low, rows, wide = spans[n, layer]
            piece = owned[n][layer].reshape(wide, devices, rows, features)
            blocks.append(piece.transpose(1, 0, 2, 3).reshape(devices, rows * wide, features))
    if spare:
        blocks.append(jnp.zeros((devices, spare, features), bf16))
    reduced = scatter_all(jnp.concatenate(blocks, axis=1), devices)
    summed = reduced[:small_rows].reshape(-1)
    at = 0
    for n in small_at:
        size = flats[n].shape[0]
        owned[n] = summed[at : at + size].reshape(shards[n].shape)
        at += size
    for n in large_at:
        for layer in range(LAYERS):
            low, rows, wide = spans[n, layer]
            piece = reduced[low : low + rows * wide].reshape(wide, rows, features)
            owned[n][layer] = piece.transpose(1, 0, 2).reshape(rows, wide * features)
        owned[n] = jnp.stack(owned[n])
    return (outs, grad[None], *owned)


GATHERED = (
    (None, 0, 0, 0, 1, 'zyx'),
    (0, 0, 0, 1, 3, 'zxy'),
    (0, 0, 1, 2, 3, 'zyx'),
    (0, 0, 2, 3, 3, 'zxy'),
    (0, 1, 0, 1, 1, 'zyx'),
    (0, 2, 0, 1, 4, 'zxy'),
    (0, 2, 1, 2, 4, 'zyx'),
    (0, 2, 2, 3, 4, 'zxy'),
    (0, 2, 3, 4, 4, 'zyx'),
    (0, 3, 0, 2, 4, 'zxy'),
    (0, 3, 2, 4, 4, 'zyx'),
    (1, 0, 0, 2, 3, 'zxy'),
    (1, 0, 2, 3, 3, 'yzx'),
    (1, 1, 0, 1, 1, 'yzx'),
    (1, 2, 0, 2, 4, 'zyx'),
    (1, 2, 2, 4, 4, 'xzy'),
    (1, 3, 0, 1, 4, 'xzy'),
    (1, 3, 1, 2, 4, 'xzy'),
    (1, 3, 2, 3, 4, 'yzx'),
    (1, 3, 3, 4, 4, 'yxz'),
)
SCATTERED = (
    (1, 3, 0, 2, 4, 'xzy'),
    (1, 3, 2, 4, 4, 'yxz'),
    (1, 2, 0, 2, 4, 'xyz'),
    (1, 2, 2, 4, 4, 'yzx'),
    (1, 1, 0, 1, 1, 'xzy'),
    (1, 0, 0, 1, 3, 'yxz'),
    (1, 0, 1, 2, 3, 'yxz'),
    (1, 0, 2, 3, 3, 'yxz'),
    (0, 3, 0, 2, 4, 'xzy'),
    (0, 3, 2, 4, 4, 'xyz'),
    (0, 2, 0, 2, 4, 'yxz'),
    (0, 2, 2, 4, 4, 'yxz'),
    (0, 1, 0, 1, 1, 'yxz'),
    (0, 0, 0, 1, 3, 'xyz'),
    (0, 0, 1, 2, 3, 'xyz'),
    (0, 0, 2, 3, 3, 'yxz'),
    (None, 0, 0, 0, 1, 'xyz'),
)
AGENDA = (
    (
        (0, 0, 0), (0, 12, 0), (0, 15, 0),
    ),
    (
        (0, 13, 0), (0, 1, 0), (0, 16, 0), (0, 18, 0), (0, 17, 0), (0, 19, 0),
        (0, 0, 1), (0, 2, 0), (0, 19, 1), (0, 1, 1), (0, 3, 0), (0, 0, 2),
        (0, 2, 1), (0, 4, 0), (0, 1, 2), (0, 3, 1), (0, 5, 0), (0, 0, 3),
        (0, 2, 2), (0, 6, 0), (0, 3, 2), (0, 7, 0),
    ),
    (
        (0, 1, 3), (0, 5, 1), (0, 8, 0), (0, 2, 3), (0, 4, 1), (0, 7, 1),
        (0, 9, 0), (0, 3, 3), (0, 5, 2), (0, 4, 2), (0, 10, 0),
    ),
    (
        (0, 6, 1),
    ),
    (
        (0, 5, 3), (0, 9, 1), (0, 7, 2), (0, 11, 0),
    ),
    (
        (0, 4, 3), (0, 6, 2), (0, 8, 1), (0, 12, 1),
    ),
    (
        (0, 7, 3), (0, 9, 2), (0, 11, 1), (0, 13, 1), (0, 6, 3), (0, 8, 2),
        (0, 14, 0), (0, 10, 1), (0, 12, 2), (0, 9, 3), (0, 15, 1), (0, 8, 3),
        (0, 11, 2), (0, 10, 2),
    ),
    (
        (0, 12, 3), (0, 16, 1), (0, 14, 1), (0, 11, 3), (0, 13, 2), (0, 17, 1),
        (0, 10, 3), (0, 15, 2), (0, 14, 2), (0, 18, 1),
    ),
    (
        (0, 13, 3),
    ),
    (
        (0, 19, 2),
    ),
    (
        (0, 16, 2),
    ),
    (
        (0, 15, 3), (0, 18, 2),
    ),
    (
        (0, 14, 3), (0, 17, 2), (0, 16, 3),
    ),
    (
        (0, 18, 3), (0, 19, 3), (0, 17, 3),
    ),
    (
        (1, 0, 0), (1, 1, 0),
    ),
    (
        (1, 0, 1), (1, 1, 1), (1, 2, 0),
    ),
    (
        (1, 3, 0), (1, 4, 0),
    ),
    (
        (1, 2, 1),
    ),
    (
        (1, 3, 1), (1, 0, 2),
    ),
    (
        (1, 5, 0), (1, 6, 0),
    ),
    (
        (1, 7, 0), (1, 1, 2), (1, 5, 1),
    ),
    (
        (1, 8, 0), (1, 3, 2),
    ),
    (
        (1, 9, 0), (1, 4, 1), (1, 0, 3), (1, 2, 2), (1, 10, 0),
    ),
    (
        (1, 11, 0), (1, 5, 2), (1, 12, 0), (1, 0, 4),
    ),
    (
        (1, 8, 1), (1, 6, 1), (1, 1, 3),
    ),
    (
        (1, 7, 1), (1, 2, 3),
    ),
    (
        (1, 3, 3), (1, 10, 1), (1, 4, 2), (1, 13, 0), (1, 6, 2), (1, 14, 0),
        (1, 1, 4),
    ),
    (
        (1, 15, 0), (1, 7, 2), (1, 16, 0), (1, 2, 4), (1, 3, 4),
    ),
    (
        (1, 5, 3), (1, 9, 1),
    ),
    (
        (1, 6, 3), (1, 4, 3), (1, 11, 1), (1, 7, 3), (1, 8, 2), (1, 10, 2),
        (1, 9, 2), (1, 13, 1), (1, 10, 3), (1, 12, 1), (1, 11, 2), (1, 9, 3),
        (1, 8, 3), (1, 14, 1), (1, 13, 2), (1, 11, 3), (1, 15, 1), (1, 12, 2),
        (1, 13, 3), (1, 16, 1), (1, 14, 2), (1, 12, 3), (1, 15, 2), (1, 16, 2),
        (1, 14, 3), (1, 15, 3), (1, 16, 3), (1, 5, 4), (1, 4, 4), (1, 6, 4),
        (1, 7, 4), (1, 10, 4), (1, 8, 4), (1, 9, 4), (1, 11, 4), (1, 13, 4),
        (1, 12, 4), (1, 14, 4), (1, 15, 4), (1, 16, 4),
    ),
)


def stack_rows(parts):
    return jnp.concatenate(parts, axis=0)


def permute_f32(matrix, rows):
    high = rows.astype(bf16)
    rest = rows - high.astype(f32)
    middle = rest.astype(bf16)
    low = (rest - middle.astype(f32)).astype(bf16)
    return dot_nn(matrix, high) + (dot_nn(matrix, middle) + dot_nn(matrix, low))


def slots_of(window):
    padded = -(-window // 8) * 8
    lanes_each = 64
    return padded, lanes_each


def places_in_windows(shift_by):
    token = np.arange(SIDE * SIDE)
    row = (token // SIDE - shift_by) % SIDE
    col = (token % SIDE - shift_by) % SIDE
    window = (row // WIN) * (SIDE // WIN) + col // WIN
    inside = (row % WIN) * WIN + col % WIN
    edges = SIDE - WIN, SIDE - shift_by
    a_row = (row >= edges[0]).astype(int) + (row >= edges[1]).astype(int)
    a_col = (col >= edges[0]).astype(int) + (col >= edges[1]).astype(int)
    return window, inside, 3 * a_row + a_col


def constants(heads, per_device_rows, devices):
    cells = WIN * WIN
    padded, wide = slots_of(cells)
    windows = (SIDE // WIN) ** 2
    tokens = SIDE * SIDE
    total = windows * padded
    perms = []
    for shift_by in (0, SHIFT):
        window, inside, label = places_in_windows(shift_by)
        perm = np.zeros((total, tokens), np.float32)
        perm[window * padded + inside, np.arange(tokens)] = 1.0
        perms.append(perm)
    mask = np.zeros((windows, padded, wide), np.float32)
    labels = np.zeros((windows, cells), int)
    labels[window, inside] = label
    mask[:, :cells, :cells] = np.where(labels[:, :, None] == labels[:, None, :], 0.0, mask_fill)
    group = 2 * lanes // wide
    mask = np.tile(mask, (1, 1, group))
    span = 2 * WIN - 1
    strips = -(-span * WIN // 16) * 16
    onehot = np.zeros((WIN, strips, devices * 8), np.float32)
    for c_q in range(WIN):
        for d_r in range(span):
            for c_k in range(WIN):
                t = d_r * span + c_q - c_k + WIN - 1
                spot = (t // per_device_rows) * 8 + t % per_device_rows
                onehot[c_q, (span - 1 - d_r) * WIN + c_k, spot] = 1.0
    onehot = onehot.reshape(WIN * strips, devices * 8)
    query = np.arange(heads * wide) % wide
    head = np.arange(heads * wide) // wide
    lane_row = np.where(query < cells, query // WIN, -1)
    lane_col = np.where(query < cells, query % WIN, -1)
    lane_of = np.zeros((8, heads * wide), np.int32)
    lane_of[0], lane_of[1] = lane_row, lane_col
    expand = np.zeros((lanes, heads * wide), np.float32)
    expand[head, np.arange(heads * wide)] = 1.0
    collect = np.zeros((heads * wide, lanes), np.float32)
    real = query < cells
    collect[np.arange(heads * wide)[real], (lane_col * heads + head)[real]] = 1.0
    fold = np.zeros((lanes, lanes), np.float32)
    for lane in range(WIN * heads):
        fold[lane, lane % heads] = 1.0
    plain, shifted = perms
    low = [plain, shifted, shifted @ plain.T, plain @ shifted.T, plain.T, shifted.T,
           onehot, onehot.T, expand, collect, fold]
    return [jnp.asarray(a, bf16) for a in low] + [jnp.asarray(lane_of), jnp.asarray(mask)]


class Links:
    def __init__(self, line, sems):
        me = lax.axis_index("fsdp")
        self.line = line
        self.core, self.x = lax.rem(me, 2), lax.rem(me // 2, 2)
        self.y, self.z = lax.rem(me // 4, 2), me // 8
        self.me = me
        self.sibling = me + 1 - 2 * self.core
        self.across = {"x": me + 2 - 4 * self.x, "y": me + 4 - 8 * self.y}
        low = lax.rem(me, 8)
        self.along = [lax.rem(self.z + k, line) * 8 + low for k in range(1, line)]
        self.sems = sems
        self.copies = {}

    def greet(self):
        barrier = pltpu.get_barrier_semaphore()
        peers = [self.sibling, self.across["x"], self.across["y"]] + self.along
        for peer in peers:
            pl.semaphore_signal(
                barrier, inc=1, device_id=(peer,), device_id_type=pl.DeviceIdType.MESH
            )
        pl.semaphore_wait(barrier, len(peers))

    def send(self, key, way, slot, source, target, peer):
        send_sem, recv_sem = self.sems[way]
        copy = pltpu.make_async_remote_copy(
            src_ref=source,
            dst_ref=target,
            send_sem=send_sem.at[key[1], slot],
            recv_sem=recv_sem.at[key[1], slot],
            device_id=(peer,),
            device_id_type=pl.DeviceIdType.MESH,
        )
        copy.start()
        self.copies.setdefault((way,) + key, []).append(copy)

    def arrive(self, way, key):
        for copy in self.copies[(way,) + key]:
            copy.wait_recv()

    def finish(self):
        for group in self.copies.values():
            for copy in group:
                copy.wait_send()


def all_kernel(
    line, gspans, rspans, agenda,
    count_ref, x_ref, cot_ref, again_ref, aoff_ref, wqkv_ref, bqv_ref, rel_ref, wproj_ref, bproj_ref,
    mgain_ref, moff_ref, w1_ref, b1_ref, w2_ref, b2_ref,
    plain_ref, shifted_ref, forth_ref, back_ref, plain_t_ref, shifted_t_ref,
    onehot_ref, onehot_t_ref, expand_ref, collect_ref, fold_ref, lane_ref, mask_ref,
    out_ref, gin_ref, gagain_ref, gaoff_ref, gwqkv_ref, gbqv_ref, grel_ref, gwproj_ref, gbproj_ref,
    gmgain_ref, gmoff_ref, gw1_ref, gb1_ref, gw2_ref, gb2_ref,
    w, g, land_c, land_1, land_2, land_3, sm, sg, sland_c, sland_1, sland_2, sland_3,
    xs, xn_s, qkv_s, probs_s, mixed_s, mid_s, yn_s, slope_s, act_s,
    bias_s, strip_s, kinds_s, b1_s, own_s, mixf_s, dmix_s, dqkv_s, dsum_s, kg_s, b1g_s, rg_s,
    gs_send, gs_recv, rs_send, rs_recv,
):
    links = Links(line, {"g": (gs_send, gs_recv), "r": (rs_send, rs_recv)})
    c, x, y, z = links.core, links.x, links.y, links.z
    me = links.me
    devices = line * 8
    every = slice(None)
    rows_each = wqkv_ref.shape[1]
    features = wproj_ref.shape[2]
    hidden = w1_ref.shape[2]
    parts = wqkv_ref.shape[2] // features
    wide_parts = hidden // features
    deep = w2_ref.shape[1]
    table_each = rel_ref.shape[1]
    heads = rel_ref.shape[2]
    size = features // heads
    scaling = size ** (-0.5)
    at_proj = parts * rows_each
    at_one = at_proj + rows_each
    at_two = at_one + wide_parts * rows_each
    cells = WIN * WIN
    padded, wide = slots_of(cells)
    windows = (SIDE // WIN) ** 2
    per = lanes // size
    group_lanes = per * wide
    share = features // devices
    pack = lanes // share
    share_one = hidden // devices
    pack_one = lanes // share_one
    span = 2 * WIN - 1
    strips = -(-span * WIN // 16) * 16

    own_s[...] = jnp.zeros_like(own_s)
    at = 0
    for ref in (again_ref, aoff_ref, bqv_ref, bproj_ref, mgain_ref, moff_ref, b2_ref):
        piece = ref[...].astype(f32)
        if ref.shape[0] == LAYERS and len(ref.shape) == 3:
            for layer in range(LAYERS):
                own_s[at : at + ref.shape[1], 0:share] = piece[layer]
                at += ref.shape[1]
        else:
            own_s[at : at + LAYERS, 0:share] = piece
            at += LAYERS
    row_at = lax.broadcasted_iota(jnp.int32, (lanes, lanes), 0)
    lane_at = lax.broadcasted_iota(jnp.int32, (lanes, lanes), 1)
    spot = share * lax.rem(me, pack)
    place = jnp.where((lane_at == row_at + spot) & (row_at < share), 1.0, 0.0).astype(bf16)
    kinds = dot_nn(own_s[...].astype(bf16), place)
    spot = share_one * lax.rem(me, pack_one)
    place = jnp.where((lane_at == row_at + spot) & (row_at < share_one), 1.0, 0.0).astype(bf16)
    own_s[...] = jnp.zeros_like(own_s)
    own_s[0:LAYERS, 0:share_one] = b1_ref[...].astype(f32)
    firsts = dot_nn(own_s[...].astype(bf16), place)
    own_s[...] = jnp.zeros_like(own_s)
    for layer in range(LAYERS):
        own_s[layer * 8 : layer * 8 + table_each, 0:heads] = rel_ref[layer].astype(f32)
        own_s[layer * 8 + table_each : layer * 8 + table_each + 1, :] = firsts[layer : layer + 1]
    sm[z, y, x, c, :, 0:lanes] = kinds.astype(bf16)
    sm[z, y, x, c, :, lanes : 2 * lanes] = own_s[...].astype(bf16)
    for layer in range(LAYERS):
        for part in range(parts):
            w[layer, z, y, x, c, pl.ds(part * rows_each, rows_each), :] = (
                wqkv_ref[layer, :, part * features : (part + 1) * features]
            )
        w[layer, z, y, x, c, pl.ds(at_proj, rows_each), :] = wproj_ref[layer]
        for part in range(wide_parts):
            w[layer, z, y, x, c, pl.ds(at_one + part * rows_each, rows_each), :] = (
                w1_ref[layer, :, part * features : (part + 1) * features]
            )
        w[layer, z, y, x, c, pl.ds(at_two, deep), :] = w2_ref[layer]

    own = {"z": z, "y": y, "x": x}

    def view(where, span, picks):
        big, small = where
        layer, low, count, _ = span
        if layer is None:
            return small.at[picks]
        return big.at[(layer,) + picks + (pl.ds(low, count),)]

    def gather(n, stage):
        span = gspans[n]
        route = span[3]
        if stage:
            links.arrive("g", (stage - 1, n))
        got = route[:stage]
        picks = tuple(every if axis in got else own[axis] for axis in "zyx") + (c,)
        ref = view((w, sm), span, picks)
        if stage == 3:
            links.send((stage, n), "g", line + 1, ref, ref, links.sibling)
        elif route[stage] == "z":
            for k, peer in enumerate(links.along):
                links.send((stage, n), "g", k, ref, ref, peer)
        else:
            peer = links.across[route[stage]]
            links.send((stage, n), "g", line - 1 + "yx".index(route[stage]), ref, ref, peer)

    def merge(n, stage):
        span = rspans[n]
        order = span[3]
        closed = order[:stage]
        counts = [1 if axis in closed else 2 for axis in "yx"]

        def one(zi, carry):
            for a in range(counts[0]):
                for b in range(counts[1]):
                    at = (zi, a if counts[0] == 2 else y, b if counts[1] == 2 else x, c)
                    here = view((g, sg), span, at)
                    if stage == 0:
                        total = here[...] + view((land_c, sland_c), span, (zi, a, b))[...]
                    elif stage == 1:
                        total = here[...] + view((land_1, sland_1), span, (zi, a + b))[...]
                    elif order[1] == "z":
                        total = here[...].astype(f32)
                        for k in range(line - 1):
                            landed = view((land_2, sland_2), span, (2 * k + a + b,))
                            total = total + landed[...].astype(f32)
                        total = total.astype(bf16)
                    else:
                        total = here[...] + view((land_2, sland_2), span, (zi,))[...]
                    here[...] = total
            return carry

        if "z" in closed:
            one(z, 0)
        else:
            lax.fori_loop(0, line, one, 0)

    def scatter(n, stage):
        span = rspans[n]
        layer, low, count, order = span
        if stage:
            links.arrive("r", (stage - 1, n))
        if stage == 0:
            source = view((g, sg), span, (every, every, every, 1 - c))
            target = view((land_c, sland_c), span, (every, every, every))
            links.send((0, n), "r", line + 1, source, target, links.sibling)
            return
        if stage < 4:
            merge(n, stage - 1)
            axis = order[stage - 1]
            closed = order[: stage - 1]
            where = {a: own[a] if a in closed else every for a in "zyx"}
            if axis == "z":
                for k, peer in enumerate(links.along):
                    where["z"] = lax.rem(z + k + 1, line)
                    source = view((g, sg), span, (where["z"], where["y"], where["x"], c))
                    if stage == 2:
                        target = view((land_2, sland_2), span, (pl.ds(2 * k, 2),))
                    else:
                        target = view((land_3, sland_3), span, (k,))
                    links.send((stage, n), "r", k, source, target, peer)
                return
            where[axis] = 1 - own[axis]
            source = view((g, sg), span, (where["z"], where["y"], where["x"], c))
            if stage == 1:
                target = view((land_1, sland_1), span, (every, every))
            elif stage == 2:
                target = view((land_2, sland_2), span, (pl.ds(0, line),))
            else:
                target = view((land_3, sland_3), span, (0,))
            slot = line - 1 + "yx".index(axis)
            links.send((stage, n), "r", slot, source, target, links.across[axis])
            return
        landed = line - 1 if order[2] == "z" else 1
        if layer is None:
            total = sg[z, y, x, c].astype(f32)
            for k in range(landed):
                total = total + sland_3[k].astype(f32)
            small_out(total)
            return
        for unit in range(low, low + count, rows_each):
            rows = pl.ds(unit, rows_each)
            total = g[layer, z, y, x, c, rows, :].astype(f32)
            for k in range(landed):
                total = total + land_3[layer, k, rows, :].astype(f32)
            if unit < at_proj:
                part = unit // rows_each
                gwqkv_ref[layer, :, part * features : (part + 1) * features] = total
            elif unit < at_one:
                gwproj_ref[layer] = total
            elif unit < at_two:
                part = (unit - at_one) // rows_each
                gw1_ref[layer, :, part * features : (part + 1) * features] = total
            else:
                gw2_ref[layer, unit - at_two : unit - at_two + rows_each, :] = total

    def small_out(total):
        picked = jnp.where(lax.broadcasted_iota(jnp.int32, (16, lanes), 1) // share == lax.rem(me, pack),
                           total[:, 0:lanes], 0.0)
        folded = picked[:, 0:share]
        for n in range(1, pack):
            folded = folded + picked[:, n * share : (n + 1) * share]
        at = 0
        for ref in (gagain_ref, gaoff_ref, gbqv_ref, gbproj_ref, gmgain_ref, gmoff_ref, gb2_ref):
            if len(ref.shape) == 3:
                for layer in range(LAYERS):
                    ref[layer] = folded[at : at + ref.shape[1]]
                    at += ref.shape[1]
            else:
                ref[...] = folded[at : at + LAYERS]
                at += LAYERS
        tail = total[:, lanes : 2 * lanes]
        for layer in range(LAYERS):
            grel_ref[layer] = tail[layer * 8 : layer * 8 + table_each, 0:heads]
            row = tail[layer * 8 + table_each : layer * 8 + table_each + 1]
            keep = lax.broadcasted_iota(jnp.int32, (1, lanes), 1) // share_one
            row = jnp.where(keep == lax.rem(me, pack_one), row, 0.0)
            folded_row = row[:, 0:share_one]
            for n in range(1, pack_one):
                folded_row = folded_row + row[:, n * share_one : (n + 1) * share_one]
            gb1_ref[layer : layer + 1, :] = folded_row

    def qkv_part(layer, part):
        block = w[layer, :, :, :, :, part * rows_each : (part + 1) * rows_each, :]
        return block.reshape(features, features)

    def proj_of(layer):
        return w[layer, :, :, :, :, at_proj : at_proj + rows_each, :].reshape(features, features)

    def one_of(layer, part):
        low = at_one + part * rows_each
        return w[layer, :, :, :, :, low : low + rows_each, :].reshape(features, features)

    def two_of(layer, part):
        return w[layer, part, :, :, :, at_two : at_two + deep, :].reshape(features, features)

    def put(layer, low, value):
        g[layer, :, :, :, :, low : low + rows_each, :] = value.astype(bf16).reshape(
            line, 2, 2, 2, rows_each, features
        )

    agenda = list(agenda)

    def go():
        for way, n, stage in agenda.pop(0):
            (gather if way == 0 else scatter)(n, stage)

    def have(layer, low, high):
        for n, span in enumerate(gspans):
            if span[0] == layer and (layer is None or low <= span[1] < high):
                links.arrive("g", (3, n))

    links.greet()
    go()

    stream = dot_nn(plain_ref[...], x_ref[0])
    xs[0] = stream
    qkv_s[:, :, 48:64, :] = jnp.zeros((LAYERS, windows, 16, parts * features), bf16)
    dmix_s[:, 48:64, :] = jnp.zeros((windows, 16, features), bf16)
    strip_s[...] = jnp.zeros_like(strip_s)

    go()
    have(None, 0, 0)
    small = sm[...].reshape(devices, 16, 2 * lanes).astype(f32)
    for tile in range(features // lanes):
        block = small[tile * pack : (tile + 1) * pack, :, 0:lanes]
        kinds_s[:, tile * lanes : (tile + 1) * lanes] = jnp.sum(block, axis=0)
    for tile in range(hidden // lanes):
        total = small[tile * pack_one, :, lanes : 2 * lanes]
        for n in range(1, pack_one):
            total = total + small[tile * pack_one + n, :, lanes : 2 * lanes]
        for layer in range(LAYERS):
            at = layer * 8 + table_each
            b1_s[layer : layer + 1, tile * lanes : (tile + 1) * lanes] = total[at : at + 1]

    def kind(n):
        return kinds_s[n : n + 1, :]

    lane_row = lane_ref[0:1, :]
    lane_col = lane_ref[1:2, :]
    for layer in range(LAYERS):
        table = small[:, layer * 8 : (layer + 1) * 8, lanes : 2 * lanes]
        table = table.reshape(devices * 8, lanes).astype(bf16)
        spread = dot_nn(table, expand_ref[...]).astype(bf16)
        strip = jnp.zeros((strips, heads * wide), f32)
        for col in range(WIN):
            found = dot_nn(onehot_ref[col * strips : (col + 1) * strips, :], spread)
            strip = jnp.where(lane_col == col, found, strip)
        strip_s[0:strips, :] = strip
        bias = jnp.zeros((padded, heads * wide), f32)
        for row in range(WIN):
            low = (WIN - 1 - row) * WIN
            bias = jnp.where(lane_row == row, strip_s[low : low + padded, :], bias)
        key_at = lax.broadcasted_iota(jnp.int32, (padded, heads * wide), 0)
        bias_s[layer] = jnp.where(key_at < cells, bias, outside_fill)

    keeps = [head_mask(one, size) for one in range(per)]

    def diagonal(block):
        return stack_rows([block * keep for keep in keeps])

    def undiagonal(block):
        total = block[0:padded] * keeps[0].astype(f32)
        for n in range(1, per):
            total = total + block[n * wide : n * wide + padded] * keeps[n].astype(f32)
        return total

    def both_halves(group):
        groups = heads // per
        go()
        lax.fori_loop(0, groups // 2, group, 0)
        go()
        lax.fori_loop(groups // 2, groups, group, 0)

    def attention_forward(layer):
        rows = xs[layer]
        go()
        have(layer, 0, at_proj)
        unit, _ = normalize(rows)
        xn = (unit * kind(layer) + kind(LAYERS + layer)).astype(bf16)
        xn_s[layer] = xn
        for part in range(parts):
            block = dot_nn(xn, qkv_part(layer, part))
            if part != 1:
                block = block + kind(2 * LAYERS + 2 * layer + part // 2)
            for window in range(windows):
                qkv_s[layer, window, 0:padded, part * features : (part + 1) * features] = (
                    block[window * padded : (window + 1) * padded].astype(bf16)
                )

        def group(n, carry):
            start = pl.multiple_of(n * lanes, lanes)
            bias = bias_s[layer, :, pl.ds(pl.multiple_of(n * group_lanes, lanes), group_lanes)]
            for window in range(windows):
                query = qkv_s[layer, window, :, pl.ds(start, lanes)]
                key = qkv_s[layer, window, 0:padded, pl.ds(pl.multiple_of(features + start, lanes), lanes)]
                value = qkv_s[layer, window, 0:padded, pl.ds(pl.multiple_of(2 * features + start, lanes), lanes)]
                scores = dot_nt(key, diagonal(query)) * scaling + bias
                if layer % 2:
                    scores = scores + mask_ref[window]
                raised = jnp.exp(scores - jnp.max(scores, axis=0, keepdims=True))
                probs = raised * (1.0 / jnp.sum(raised, axis=0, keepdims=True))
                probs_s[layer, n, window] = probs
                mixed = undiagonal(dot_tn(probs.astype(bf16), value))
                mixf_s[window * padded : (window + 1) * padded, pl.ds(start, lanes)] = mixed
            return carry

        both_halves(group)
        go()
        have(layer, at_proj, at_one)
        mixed = mixf_s[...].astype(bf16)
        mixed_s[layer] = mixed
        mid_s[layer] = rows + dot_nn(mixed, proj_of(layer)) + kind(4 * LAYERS + layer)

    def mlp_forward(layer):
        go()
        have(layer, at_one, at_two)
        middle = mid_s[layer]
        unit, _ = normalize(middle)
        yn = (unit * kind(5 * LAYERS + layer) + kind(6 * LAYERS + layer)).astype(bf16)
        yn_s[layer] = yn
        for part in range(wide_parts):
            cols = slice(part * features, (part + 1) * features)
            pre = dot_nn(yn, one_of(layer, part)) + b1_s[layer : layer + 1, cols]
            cumul = 0.5 * (1.0 + lax.erf(pre * half_root))
            slope_s[layer, :, cols] = cumul + pre * (jnp.exp(-0.5 * pre * pre) * inv_root_tau)
            act_s[layer, :, cols] = (pre * cumul).astype(bf16)

    def mlp_rest(layer):
        total = mid_s[layer] + kind(7 * LAYERS + layer)
        for part in range(wide_parts):
            cols = slice(part * features, (part + 1) * features)
            total = total + dot_nn(act_s[layer, :, cols], two_of(layer, part))
        return total

    attention_forward(0)
    mlp_forward(0)
    go()
    have(0, at_two, at_two + deep)
    xs[1] = permute_f32(forth_ref[...], mlp_rest(0))
    attention_forward(1)
    mlp_forward(1)
    active = count_ref[0] > 0

    def mlp_backward(layer, grad):
        low = grad.astype(bf16)
        kg_s[7 * LAYERS + layer : 7 * LAYERS + layer + 1, :] = jnp.sum(grad, axis=0, keepdims=True)
        go()
        for part in range(wide_parts):
            cols = slice(part * features, (part + 1) * features)
            g[layer, part, :, :, :, at_two : at_two + deep, :] = (
                dot_tn(act_s[layer, :, cols], low).astype(bf16).reshape(2, 2, 2, deep, features)
            )
        go()
        if layer == LAYERS - 1:
            have(layer, at_two, at_two + deep)
        yn = yn_s[layer]
        g_yn = jnp.zeros_like(grad)
        for part in range(wide_parts):
            cols = slice(part * features, (part + 1) * features)
            g_pre = dot_nt(low, two_of(layer, part)) * slope_s[layer, :, cols]
            b1g_s[layer : layer + 1, cols] = jnp.sum(g_pre, axis=0, keepdims=True)
            pre_low = g_pre.astype(bf16)
            put(layer, at_one + part * rows_each, dot_tn(yn, pre_low))
            g_yn = g_yn + dot_nt(pre_low, one_of(layer, part))
        back, g_gain, g_off = norm_pull(mid_s[layer], kind(5 * LAYERS + layer), g_yn)
        kg_s[5 * LAYERS + layer : 5 * LAYERS + layer + 1, :] = g_gain
        kg_s[6 * LAYERS + layer : 6 * LAYERS + layer + 1, :] = g_off
        g_mid = grad + back
        kg_s[4 * LAYERS + layer : 4 * LAYERS + layer + 1, :] = jnp.sum(g_mid, axis=0, keepdims=True)
        return g_mid

    def attention_backward(layer, g_mid):
        go()
        low = g_mid.astype(bf16)
        put(layer, at_proj, dot_tn(mixed_s[layer], low))
        d_mix = dot_nt(low, proj_of(layer))
        for window in range(windows):
            dmix_s[window, 0:padded, :] = d_mix[window * padded : (window + 1) * padded].astype(bf16)

        def group(n, carry):
            start = pl.multiple_of(n * lanes, lanes)
            k_at = pl.multiple_of(features + start, lanes)
            v_at = pl.multiple_of(2 * features + start, lanes)
            total = jnp.zeros((padded, group_lanes), f32)
            for window in range(windows):
                here = slice(window * padded, (window + 1) * padded)
                query = diagonal(qkv_s[layer, window, :, pl.ds(start, lanes)])
                key = qkv_s[layer, window, 0:padded, pl.ds(k_at, lanes)]
                value = qkv_s[layer, window, 0:padded, pl.ds(v_at, lanes)]
                d_out = diagonal(dmix_s[window, :, pl.ds(start, lanes)])
                probs = probs_s[layer, n, window]
                d_probs = dot_nt(value, d_out)
                dqkv_s[here, pl.ds(v_at, lanes)] = dot_nn(probs.astype(bf16), d_out)
                weighed = probs * d_probs
                d_scores = weighed - probs * jnp.sum(weighed, axis=0, keepdims=True)
                total = total + d_scores
                scores_low = d_scores.astype(bf16)
                dqkv_s[here, pl.ds(k_at, lanes)] = dot_nn(scores_low, query) * scaling
                dqkv_s[here, pl.ds(start, lanes)] = undiagonal(dot_tn(scores_low, key)) * scaling
            dsum_s[:, pl.ds(pl.multiple_of(n * group_lanes, lanes), group_lanes)] = total
            return carry

        both_halves(group)
        go()
        for n, part in ((0, 0), (1, 2)):
            column = jnp.sum(dqkv_s[:, part * features : (part + 1) * features], axis=0, keepdims=True)
            at = 2 * LAYERS + 2 * layer + n
            kg_s[at : at + 1, :] = column
        xn = xn_s[layer]
        g_xn = jnp.zeros_like(g_mid)
        for part in range(parts):
            block = dqkv_s[:, part * features : (part + 1) * features].astype(bf16)
            put(layer, part * rows_each, dot_tn(xn, block))
            g_xn = g_xn + dot_nt(block, qkv_part(layer, part))
        go()
        back, g_gain, g_off = norm_pull(xs[layer], kind(layer), g_xn)
        kg_s[layer : layer + 1, :] = g_gain
        kg_s[LAYERS + layer : LAYERS + layer + 1, :] = g_off
        strip_s[...] = jnp.zeros_like(strip_s)
        for row in range(WIN):
            at = (WIN - 1 - row) * WIN
            strip_s[at : at + padded, :] = strip_s[at : at + padded, :] + jnp.where(
                lane_row == row, dsum_s[...], 0.0
            )
        by_col = dot_nn(strip_s[0:strips, :].astype(bf16), collect_ref[...])
        col_at = lax.broadcasted_iota(jnp.int32, (1, lanes), 1) // heads
        stacked = stack_rows([jnp.where(col_at == col, by_col, 0.0).astype(bf16) for col in range(WIN)])
        table = dot_nn(onehot_t_ref[...], stacked)
        high = table.astype(bf16)
        rest = (table - high.astype(f32)).astype(bf16)
        table = dot_nn(high, fold_ref[...]) + dot_nn(rest, fold_ref[...])
        rg_s[:, layer * 8 : (layer + 1) * 8, :] = table.reshape(devices, 8, lanes)
        return g_mid + back

    grad = jnp.where(active, dot_nn(shifted_ref[...], cot_ref[0]), 0.0)
    g_x = attention_backward(1, mlp_backward(1, grad))
    grad = permute_f32(back_ref[...], g_x)
    g_x = attention_backward(0, mlp_backward(0, grad))
    for tile in range(hidden // lanes):
        for n in range(pack_one):
            for layer in range(LAYERS):
                at = layer * 8 + table_each
                rg_s[tile * pack_one + n, at : at + 1, :] = (
                    b1g_s[layer : layer + 1, tile * lanes : (tile + 1) * lanes]
                )
    for tile in range(features // lanes):
        block = kg_s[:, tile * lanes : (tile + 1) * lanes].astype(bf16)
        for n in range(pack):
            device = tile * pack + n
            sg[device // 8, (device // 4) % 2, (device // 2) % 2, device % 2, :, 0:lanes] = block
    sg[:, :, :, :, :, lanes : 2 * lanes] = rg_s[...].astype(bf16).reshape(line, 2, 2, 2, 16, lanes)
    go()
    gin_ref[0] = permute_f32(plain_t_ref[...], g_x)
    go()
    out_ref[0] = jnp.where(active, permute_f32(shifted_t_ref[...], mlp_rest(1)), 0.0)
    go()
    links.finish()


def finish_kernel(*refs):
    count = len(refs) // 2
    for n, (source, target) in enumerate(zip(refs[:count], refs[count:])):
        if n < 2:
            target[...] = source[0][:, None, :]
        elif n == 6:
            for layer in range(LAYERS):
                target[:, layer, :] = source[layer]
        else:
            target[...] = source[...]


def whole(devices):
    def local(images, cotangent, counts, *shards):
        line = devices // 8
        rows_each, features = shards[5].shape[1:]
        hidden = shards[9].shape[2]
        deep = shards[11].shape[1]
        parts, wide_parts = shards[2].shape[2] // features, hidden // features
        heads = shards[4].shape[2]
        cells = WIN * WIN
        padded, wide = slots_of(cells)
        windows = (SIDE // WIN) ** 2
        total = windows * padded
        tokens = images.shape[1]
        at_one = (parts + 1) * rows_each
        at_two = at_one + wide_parts * rows_each
        depth = at_two + deep
        edges = (0, parts * rows_each, at_one, at_two, depth)

        def spans_of(pieces):
            spans = []
            for layer, part, start, stop, of, route in pieces:
                if layer is None:
                    spans.append((None, 0, 0, route))
                    continue
                rows = edges[part + 1] - edges[part]
                low = edges[part] + rows * start // of
                spans.append((layer, low, edges[part] + rows * stop // of - low, route))
            return tuple(spans)

        gspans, rspans = spans_of(GATHERED), spans_of(SCATTERED)
        consts = constants(heads, shards[4].shape[1], devices)
        args = [counts, images, cotangent, *shards, *consts]
        outs = [shaped(images.shape, f32), shaped(images.shape, f32)]
        outs += [shaped(s.shape, f32) for s in shards]
        vmem = pltpu.VMEM
        strips = -(-(2 * WIN - 1) * WIN // 16) * 16
        tall = (WIN - 1) * WIN + padded
        tall = max(-(-tall // 8) * 8, strips)
        scratch = [
            vmem((LAYERS, line, 2, 2, 2, depth, features), bf16),
            vmem((LAYERS, line, 2, 2, 2, depth, features), bf16),
            vmem((LAYERS, line, 2, 2, depth, features), bf16),
            vmem((LAYERS, line, 2, depth, features), bf16),
            vmem((LAYERS, 2 * line - 2, depth, features), bf16),
            vmem((LAYERS, line - 1, depth, features), bf16),
            vmem((line, 2, 2, 2, 16, 2 * lanes), bf16),
            vmem((line, 2, 2, 2, 16, 2 * lanes), bf16),
            vmem((line, 2, 2, 16, 2 * lanes), bf16),
            vmem((line, 2, 16, 2 * lanes), bf16),
            vmem((2 * line - 2, 16, 2 * lanes), bf16),
            vmem((line - 1, 16, 2 * lanes), bf16),
            vmem((LAYERS, total, features), f32),
            vmem((LAYERS, total, features), bf16),
            vmem((LAYERS, windows, wide, parts * features), bf16),
            vmem((LAYERS, heads * wide // (2 * lanes), windows, padded, 2 * lanes), f32),
            vmem((LAYERS, total, features), bf16),
            vmem((LAYERS, total, features), f32),
            vmem((LAYERS, total, features), bf16),
            vmem((LAYERS, total, hidden), f32),
            vmem((LAYERS, total, hidden), bf16),
            vmem((LAYERS, padded, heads * wide), f32),
            vmem((tall, heads * wide), f32),
            vmem((16, features), f32),
            vmem((8, hidden), f32),
            vmem((16, lanes), f32),
            vmem((total, features), f32),
            vmem((windows, wide, features), bf16),
            vmem((total, parts * features), f32),
            vmem((padded, heads * wide), f32),
            vmem((16, features), f32),
            vmem((8, hidden), f32),
            vmem((devices, 16, lanes), f32),
        ]
        scratch += [pltpu.SemaphoreType.DMA((len(gspans), line + 2))] * 2
        scratch += [pltpu.SemaphoreType.DMA((len(rspans), line + 2))] * 2
        space = pl.BlockSpec(memory_space=pltpu.VMEM)
        results = pl.pallas_call(
            functools.partial(all_kernel, line, gspans, rspans, AGENDA),
            out_shape=tuple(outs),
            in_specs=[pl.BlockSpec(memory_space=pltpu.SMEM)] + [space] * (len(args) - 1),
            out_specs=tuple([space] * len(outs)),
            scratch_shapes=scratch,
            compiler_params=pltpu.CompilerParams(
                collective_id=2, has_side_effects=True, vmem_limit_bytes=63 * 1024 * 1024
            ),
        )(*args)
        shapes = [r.shape for r in results]
        for n in (0, 1):
            shapes[n] = (tokens, 1, features)
        shapes[6] = (shapes[6][1], LAYERS, shapes[6][2])
        results = pl.pallas_call(
            finish_kernel,
            out_shape=tuple(shaped(s, f32) for s in shapes),
            in_specs=[space] * len(shapes),
            out_specs=tuple([space] * len(shapes)),
        )(*results)
        results = list(results)
        for n in (0, 1, 6):
            results[n] = jnp.transpose(results[n], (1, 0, 2))
        return tuple(results)

    return local


def fits_whole(devices, sizes):
    features, hidden, heads, table_rows, wide = sizes
    if devices % 8 or devices < 16 or features % devices or hidden % devices or table_rows % devices:
        return False
    rows_each, share_one, table_each = features // devices, hidden // devices, table_rows // devices
    return (
        rows_each % 16 == 0
        and lanes % rows_each == 0
        and lanes % share_one == 0
        and table_each <= 7
        and hidden * 8 == features * devices
        and lanes * heads == 4 * features
        and WIN * heads <= lanes
        and LAYERS == 2
        and share_one % (4 * 16) == 0
        and wide == 3 * features
    )


def solution(mesh):
    in_specs = (
        P("fsdp", None, None),
        P("fsdp", None, None),
        P("fsdp"),
        P(None, "fsdp"),
        P(None, "fsdp"),
        P(None, "fsdp", None),
        P(None, None, "fsdp"),
        P(None, "fsdp", None),
        P(None, "fsdp", None),
        P(None, "fsdp"),
        P(None, "fsdp"),
        P(None, "fsdp"),
        P(None, "fsdp", None),
        P(None, "fsdp"),
        P(None, "fsdp", None),
        P(None, "fsdp"),
    )
    out_specs = (
        P("fsdp", None, None),
        P("fsdp", None, None),
        P(None, "fsdp"),
        P(None, "fsdp"),
        P(None, "fsdp", None),
        P(None, None, "fsdp"),
        P(None, "fsdp", None),
        P(None, "fsdp", None),
        P(None, "fsdp"),
        P(None, "fsdp"),
        P(None, "fsdp"),
        P(None, "fsdp", None),
        P(None, "fsdp"),
        P(None, "fsdp", None),
        P(None, "fsdp"),
    )
    devices = mesh.shape["fsdp"]

    def step(images, cotangent, counts, *params):
        hidden, (_, table_rows, heads) = params[9].shape[2], params[4].shape
        sizes = (images.shape[2], hidden, heads, table_rows, params[2].shape[2])
        body = whole(devices) if fits_whole(devices, sizes) else local
        return jax.shard_map(
            body, mesh=mesh, in_specs=in_specs, out_specs=out_specs, check_vma=False
        )(images, cotangent, counts, *params)

    return step
```

```python
import functools

import jax
import jax.numpy as jnp
import numpy as np
from jax import lax
from jax.experimental import pallas as pl
from jax.experimental.pallas import tpu as pltpu
from jax.sharding import PartitionSpec as P

WIN = 7
SIDE = 14
LAYERS = 2
SHIFT = 3

norm_eps = 1e-05
mask_fill = -10000.0
outside_fill = -1e30
half_root = 0.7071067811865476
inv_root_tau = 0.3989422804014327
lanes = 128
bf16 = jnp.bfloat16
f32 = jnp.float32


def dot_nn(left, right):
    return lax.dot_general(left, right, (((1,), (0,)), ((), ())), preferred_element_type=f32)


def dot_nt(left, right):
    return lax.dot_general(left, right, (((1,), (1,)), ((), ())), preferred_element_type=f32)


def dot_tn(left, right):
    return lax.dot_general(left, right, (((0,), (0,)), ((), ())), preferred_element_type=f32)


def normalize(rows):
    centred = rows - jnp.mean(rows, axis=-1, keepdims=True)
    spread = jnp.mean(centred * centred, axis=-1, keepdims=True)
    inverse = lax.rsqrt(spread + norm_eps)
    return centred * inverse, inverse


def norm_pull(rows, gain, grad):
    unit, inverse = normalize(rows)
    g_gain = jnp.sum(grad * unit, axis=0, keepdims=True)
    g_bias = jnp.sum(grad, axis=0, keepdims=True)
    scaled = grad * gain
    back = inverse * (
        scaled
        - jnp.mean(scaled, axis=-1, keepdims=True)
        - unit * jnp.mean(scaled * unit, axis=-1, keepdims=True)
    )
    return back, g_gain, g_bias


def head_mask(local_head, head_size):
    lane = lax.broadcasted_iota(jnp.int32, (1, lanes), 1)
    return jnp.where(lane // head_size == local_head, 1.0, 0.0).astype(bf16)


def bias_kernel(pairs_ref, spread_ref, spread_t_ref, mask_ref, out_ref):
    def step(head, carry):
        rows = dot_nn(spread_ref[...], pairs_ref[head]).astype(bf16)
        out_ref[head] = dot_nn(rows, spread_t_ref[...]) + mask_ref[...]
        return carry

    lax.fori_loop(0, pairs_ref.shape[0], step, 0)


def attn_fwd_kernel(
    x_ref, gain_ref, off_ref, wqkv_ref, bqkv_ref, bias_ref, wproj_ref, bproj_ref,
    mid_ref, xn_ref, qkv_ref, key_t_ref, probs_ref, mixed_t_ref,
    val_t,
):
    rows = x_ref[...]
    features = rows.shape[1]
    heads = bias_ref.shape[0]
    size = features // heads
    scaling = size ** (-0.5)
    unit, _ = normalize(rows)
    xn = (unit * gain_ref[...] + off_ref[...]).astype(bf16)
    xn_ref[...] = xn
    for part in range(3):
        cols = pl.ds(part * features, features)
        block = dot_nn(xn, wqkv_ref[part]) + bqkv_ref[:, cols]
        qkv_ref[:, cols] = block.astype(bf16)
        if part == 1:
            key_t_ref[...] = block.T.astype(bf16)
        if part == 2:
            val_t[...] = block.T.astype(bf16)
    per = lanes // size

    def group(g, carry):
        start = pl.multiple_of(g * lanes, lanes)
        query = qkv_ref[:, pl.ds(start, lanes)]
        keys = qkv_ref[:, pl.ds(pl.multiple_of(features + start, lanes), lanes)]
        for one in range(per):
            head = g * per + one
            at = pl.ds(pl.multiple_of(head * size, size), size)
            scores = dot_nt(keys * head_mask(one, size), query) * scaling + bias_ref[head]
            peak = jnp.max(scores, axis=0, keepdims=True)
            raised = jnp.exp(scores - peak)
            total = jnp.sum(raised, axis=0, keepdims=True)
            probs = raised * (1.0 / total)
            probs_ref[head] = probs
            mixed_t_ref[at, :] = dot_nn(val_t[at, :], probs.astype(bf16)).astype(bf16)
        return carry

    lax.fori_loop(0, heads // per, group, 0)
    mixed = mixed_t_ref[...].astype(f32).T.astype(bf16)
    mid_ref[...] = rows + dot_nn(mixed, wproj_ref[...]) + bproj_ref[...]


def mlp_fwd_kernel(
    mid_ref, gain_ref, off_ref, w1_ref, b1_ref, w2_ref, b2_ref,
    out_ref, yn_ref, slope_ref, act_ref,
):
    middle = mid_ref[...]
    features = middle.shape[1]
    unit, _ = normalize(middle)
    yn = (unit * gain_ref[...] + off_ref[...]).astype(bf16)
    yn_ref[...] = yn
    total = middle + b2_ref[...]
    for chunk in range(w1_ref.shape[0]):
        cols = pl.ds(chunk * features, features)
        pre = dot_nn(yn, w1_ref[chunk]) + b1_ref[:, cols]
        cumul = 0.5 * (1.0 + lax.erf(pre * half_root))
        slope_ref[:, cols] = cumul + pre * (jnp.exp(-0.5 * pre * pre) * inv_root_tau)
        act = (pre * cumul).astype(bf16)
        act_ref[:, cols] = act
        total = total + dot_nn(act, w2_ref[cols, :])
    out_ref[...] = total


def mlp_bwd_kernel(
    g_ref, mid_ref, gain_ref, w1_ref, w2_ref, yn_ref, slope_ref, act_ref,
    gm_ref, gw1_ref, gw2_ref, gb1_ref, gb2_ref, ggain_ref, goff_ref, gbproj_ref,
):
    grad = g_ref[...]
    features = grad.shape[1]
    low = grad.astype(bf16)
    gb2_ref[...] = jnp.sum(grad, axis=0, keepdims=True)
    yn = yn_ref[...]
    g_yn = jnp.zeros_like(grad)
    for chunk in range(w1_ref.shape[0]):
        cols = pl.ds(chunk * features, features)
        gw2_ref[cols, :] = dot_tn(act_ref[:, cols], low).astype(bf16)
        g_pre = dot_nt(low, w2_ref[cols, :]) * slope_ref[:, cols]
        gb1_ref[:, cols] = jnp.sum(g_pre, axis=0, keepdims=True)
        pre_low = g_pre.astype(bf16)
        gw1_ref[chunk] = dot_tn(yn, pre_low).astype(bf16)
        g_yn = g_yn + dot_nt(pre_low, w1_ref[chunk])
    back, g_gain, g_off = norm_pull(mid_ref[...], gain_ref[...], g_yn)
    ggain_ref[...] = g_gain
    goff_ref[...] = g_off
    g_mid = grad + back
    gm_ref[...] = g_mid
    gbproj_ref[...] = jnp.sum(g_mid, axis=0, keepdims=True)


def attn_bwd_kernel(
    gm_ref, x_ref, gain_ref, wqkv_ref, wproj_ref, xn_ref, qkv_ref, key_t_ref, probs_ref,
    mixed_t_ref, spread_ref, spread_t_ref,
    gx_ref, gwqkv_ref, gwproj_ref, gqv_ref, gpairs_ref, ggain_ref, goff_ref,
    dmix, dq_t, dqkv,
):
    g_mid = gm_ref[...]
    features = g_mid.shape[1]
    heads = probs_ref.shape[0]
    size = features // heads
    scaling = size ** (-0.5)
    low = g_mid.astype(bf16)
    gwproj_ref[...] = dot_nn(mixed_t_ref[...], low).astype(bf16)
    dmix[...] = dot_nt(low, wproj_ref[...]).astype(bf16)
    per = lanes // size

    def group(g, carry):
        start = pl.multiple_of(g * lanes, lanes)
        k_at = pl.multiple_of(features + start, lanes)
        v_at = pl.multiple_of(2 * features + start, lanes)
        query = qkv_ref[:, pl.ds(start, lanes)]
        values = qkv_ref[:, pl.ds(v_at, lanes)]
        d_mix = dmix[:, pl.ds(start, lanes)]
        d_keys = jnp.zeros(query.shape, f32)
        d_values = jnp.zeros(query.shape, f32)
        for one in range(per):
            head = g * per + one
            at = pl.ds(pl.multiple_of(head * size, size), size)
            keep = head_mask(one, size)
            probs = probs_ref[head]
            d_probs = dot_nt(values * keep, d_mix)
            d_values = d_values + dot_nn(probs.astype(bf16), d_mix * keep)
            weighed = probs * d_probs
            d_scores = weighed - probs * jnp.sum(weighed, axis=0, keepdims=True)
            scores_low = d_scores.astype(bf16)
            d_keys = d_keys + dot_nn(scores_low, query * keep)
            dq_t[at, :] = dot_nn(key_t_ref[at, :], scores_low)
            folded = dot_nn(spread_t_ref[...], scores_low).astype(bf16)
            gpairs_ref[head] = dot_nn(folded, spread_ref[...])
        dqkv[:, pl.ds(k_at, lanes)] = (d_keys * scaling).astype(bf16)
        dqkv[:, pl.ds(v_at, lanes)] = d_values.astype(bf16)
        gqv_ref[1:2, pl.ds(start, lanes)] = jnp.sum(d_values, axis=0, keepdims=True)
        return carry

    lax.fori_loop(0, heads // per, group, 0)
    d_query = dq_t[...].T * scaling
    gqv_ref[0:1, :] = jnp.sum(d_query, axis=0, keepdims=True)
    dqkv[:, :features] = d_query.astype(bf16)
    xn = xn_ref[...]
    g_xn = jnp.zeros_like(g_mid)
    for part in range(3):
        cols = pl.ds(part * features, features)
        block = dqkv[:, cols]
        gwqkv_ref[part] = dot_tn(xn, block).astype(bf16)
        g_xn = g_xn + dot_nt(block, wqkv_ref[part])
    back, g_gain, g_off = norm_pull(x_ref[...], gain_ref[...], g_xn)
    ggain_ref[...] = g_gain
    goff_ref[...] = g_off
    gx_ref[...] = g_mid + back


def bit_of(index, place):
    return lax.rem(index // (1 << place), 2)


def peers_of(me, places):
    return [me + (1 - 2 * bit_of(me, place)) * (1 << place) for place in range(places)]


def greet(me, places):
    barrier = pltpu.get_barrier_semaphore()
    for peer in peers_of(me, places):
        pl.semaphore_signal(
            barrier, inc=1, device_id=(peer,), device_id_type=pl.DeviceIdType.MESH
        )
    pl.semaphore_wait(barrier, places)


def routes(places):
    high = list(range(places - 1, 2, -1))
    if places < 3:
        return [list(range(places - 1, -1, -1))]
    return [
        high + [2, 1, 0],
        high + [1, 2, 0],
        [2] + high + [1, 0],
        [1] + high + [2, 0],
    ]


def row_parts(total, count):
    units = total // 16
    sizes = [16 * (units // count + (1 if n < units % count else 0)) for n in range(count)]
    return [(sum(sizes[:n]), sizes[n]) for n in range(count)]


def region(places, free, me, lowest=0, forced=None):
    picks = []
    for place in range(places - 1, lowest - 1, -1):
        if forced is not None and place == forced[0]:
            picks.append(forced[1])
        elif place in free:
            picks.append(slice(None))
        else:
            picks.append(bit_of(me, place))
    return tuple(picks)


def gather_kernel(places, x_ref, out_ref, send_sem, recv_sem, own_sem):
    me = lax.axis_index("fsdp")
    peers = peers_of(me, places)
    greet(me, places)
    own = pltpu.make_async_copy(x_ref, out_ref.at[region(places, (), me)], own_sem)
    own.start()
    orders = routes(places)
    parts = row_parts(x_ref.shape[0], len(orders))
    copies = [[] for _ in orders]
    for stage in range(places):
        for n, (order, (low, size)) in enumerate(zip(orders, parts)):
            rows = pl.ds(low, size)
            place = order[stage]
            if stage == 1 and n == 0:
                own.wait()
            if stage:
                copies[n][-1].wait_recv()
            here = region(places, order[:stage], me)
            target = out_ref.at[here + (rows,)]
            copy = pltpu.make_async_remote_copy(
                src_ref=x_ref.at[rows] if stage == 0 else target,
                dst_ref=target,
                send_sem=send_sem.at[n, stage],
                recv_sem=recv_sem.at[n, stage],
                device_id=(peers[place],),
                device_id_type=pl.DeviceIdType.MESH,
            )
            copy.start()
            copies[n].append(copy)
    for group in copies:
        group[-1].wait_recv()
    for group in copies:
        for copy in group:
            copy.wait_send()


def scatter_kernel(places, g_ref, out_ref, acc, *rest):
    landings, (send_sem, recv_sem) = rest[:places], rest[places:]
    me = lax.axis_index("fsdp")
    peers = peers_of(me, places)
    greet(me, places)
    orders = [order[::-1] for order in routes(places)]
    parts = row_parts(g_ref.shape[-2], len(orders))
    everything = set(range(places))
    copies = [[None] * places for _ in orders]

    def send(n, stage):
        order, (low, size) = orders[n], parts[n]
        rows = pl.ds(low, size)
        place = order[stage]
        free = everything - set(order[: stage + 1])
        away = (place, 1 - bit_of(me, place))
        if stage == 0:
            source = g_ref.at[region(places, free, me, 0, away) + (rows,)]
        else:
            source = acc.at[region(places, free, me, 1, away) + (rows,)]
        copy = pltpu.make_async_remote_copy(
            src_ref=source,
            dst_ref=landings[stage].at[(slice(None),) * len(free) + (rows,)],
            send_sem=send_sem.at[n, stage],
            recv_sem=recv_sem.at[n, stage],
            device_id=(peers[place],),
            device_id_type=pl.DeviceIdType.MESH,
        )
        copy.start()
        copies[n][stage] = copy

    def add(n, stage):
        order, (low, size) = orders[n], parts[n]
        rows = pl.ds(low, size)
        free = sorted(everything - set(order[: stage + 1]), reverse=True)
        copies[n][stage].wait_recv()

        def one(at, carry):
            values = {}
            for spot, place in enumerate(free):
                values[place] = lax.rem(at // (1 << (len(free) - 1 - spot)), 2)
            full = tuple(
                values[place] if place in values else bit_of(me, place)
                for place in range(places - 1, -1, -1)
            )
            kept = full[:-1] + (rows,)
            landed = landings[stage][tuple(values[place] for place in free) + (rows,)]
            if stage == 0:
                acc[kept] = g_ref[full + (rows,)] + landed
            elif stage < places - 1:
                acc[kept] = acc[kept] + landed
            else:
                out_ref[rows] = acc[kept].astype(f32) + landed.astype(f32)
            return carry

        lax.fori_loop(0, 1 << len(free), one, 0)

    for n in range(len(orders)):
        send(n, 0)
    for stage in range(places):
        for n in range(len(orders)):
            add(n, stage)
            if stage < places - 1:
                send(n, stage + 1)
    for group in copies:
        for copy in group:
            copy.wait_send()


def gather_all(shard, devices):
    places = devices.bit_length() - 1
    count = len(routes(places))
    out = pl.pallas_call(
        functools.partial(gather_kernel, places),
        out_shape=shaped((2,) * places + shard.shape, shard.dtype),
        in_specs=[pl.BlockSpec(memory_space=pltpu.VMEM)],
        out_specs=pl.BlockSpec(memory_space=pltpu.VMEM),
        scratch_shapes=[
            pltpu.SemaphoreType.DMA((count, places)),
            pltpu.SemaphoreType.DMA((count, places)),
            pltpu.SemaphoreType.DMA,
        ],
        compiler_params=pltpu.CompilerParams(
            collective_id=0, has_side_effects=True, vmem_limit_bytes=60 * 1024 * 1024
        ),
    )(shard)
    return out.reshape((devices,) + shard.shape)


def scatter_all(grads, devices):
    places = devices.bit_length() - 1
    count = len(routes(places))
    tail = grads.shape[1:]
    return pl.pallas_call(
        functools.partial(scatter_kernel, places),
        out_shape=shaped(tail, f32),
        in_specs=[pl.BlockSpec(memory_space=pltpu.VMEM)],
        out_specs=pl.BlockSpec(memory_space=pltpu.VMEM),
        scratch_shapes=[pltpu.VMEM((2,) * (places - 1) + tail, bf16)]
        + [pltpu.VMEM((2,) * (places - 1 - stage) + tail, bf16) for stage in range(places)]
        + [
            pltpu.SemaphoreType.DMA((count, places)),
            pltpu.SemaphoreType.DMA((count, places)),
        ],
        compiler_params=pltpu.CompilerParams(
            collective_id=1, has_side_effects=True, vmem_limit_bytes=60 * 1024 * 1024
        ),
    )(grads.reshape((2,) * places + tail))


def run(kernel, outs, args, scratch=(), flops=0):
    size = sum(a.size * a.dtype.itemsize for a in args)
    size += sum(a.size * a.dtype.itemsize for a in outs)
    return pl.pallas_call(
        kernel,
        out_shape=tuple(outs),
        in_specs=[pl.BlockSpec(memory_space=pltpu.VMEM)] * len(args),
        out_specs=tuple([pl.BlockSpec(memory_space=pltpu.VMEM)] * len(outs)),
        scratch_shapes=list(scratch),
        compiler_params=pltpu.CompilerParams(vmem_limit_bytes=60 * 1024 * 1024),
        cost_estimate=pl.CostEstimate(flops=flops, bytes_accessed=size, transcendentals=0),
    )(*args)


def shaped(shape, dtype):
    return jax.ShapeDtypeStruct(tuple(shape), dtype)


def offset_onehot(table_rows):
    places = jnp.arange(WIN * WIN, dtype=jnp.int32)
    row_at = places // WIN
    col_at = places % WIN
    index = (row_at[:, None] - row_at[None, :] + WIN - 1) * (2 * WIN - 1) + (
        col_at[:, None] - col_at[None, :] + WIN - 1
    )
    targets = jnp.arange(table_rows, dtype=jnp.int32)
    return (index.reshape(-1)[:, None] == targets[None, :]).astype(f32)


def token_places(shift_by):
    token = jnp.arange(SIDE * SIDE, dtype=jnp.int32)
    row = (token // SIDE - shift_by) % SIDE
    col = (token % SIDE - shift_by) % SIDE
    window = (row // WIN) * (SIDE // WIN) + col // WIN
    inside = (row % WIN) * WIN + col % WIN
    if shift_by:
        edges = SIDE - WIN, SIDE - shift_by
        a_row = (row >= edges[0]).astype(jnp.int32) + (row >= edges[1]).astype(jnp.int32)
        a_col = (col >= edges[0]).astype(jnp.int32) + (col >= edges[1]).astype(jnp.int32)
        label = 3 * a_row + a_col
    else:
        label = jnp.zeros_like(token)
    mask = jnp.where(label[:, None] == label[None, :], 0.0, mask_fill)
    mask = jnp.where(window[:, None] == window[None, :], mask, outside_fill).astype(f32)
    spread = (inside[:, None] == jnp.arange(WIN * WIN)[None, :]).astype(bf16)
    return mask, spread, spread.T


def local(
    images,
    cotangent,
    counts,
    *shards,
):
    devices = lax.axis_size("fsdp")
    gather_dims = (1, 1, 1, 2, 1, 1, 1, 1, 1, 1, 1, 1, 1)
    large_at = (2, 5, 9, 11)
    small_at = (0, 1, 3, 4, 6, 7, 8, 10, 12)
    flats = [tensor.reshape(-1) for tensor in shards]
    tokens, features = images.shape[1:]
    packed = jnp.concatenate([flats[n] for n in small_at])
    small_rows = 16 * -(-packed.shape[0] // (16 * features))
    packed = jnp.pad(packed, (0, small_rows * features - packed.shape[0]))
    blocks, spans = [packed.reshape(small_rows, features)], {}
    filled = small_rows
    for layer in range(LAYERS):
        for n in large_at:
            piece = shards[n][layer]
            rows, wide = piece.shape[0], piece.shape[1] // features
            piece = piece.reshape(rows, wide, features).transpose(1, 0, 2)
            blocks.append(piece.reshape(rows * wide, features))
            spans[n, layer] = (filled, rows, wide)
            filled += rows * wide
    spare = -filled % 16
    if spare:
        blocks.append(jnp.zeros((spare, features), bf16))
    gathered = gather_all(jnp.concatenate(blocks), devices)
    packed = gathered[:, :small_rows].reshape(devices, -1)
    weights = [None] * len(shards)
    at = 0
    for n in small_at:
        shape, axis_dim = shards[n].shape, gather_dims[n]
        size = flats[n].shape[0]
        piece = packed[:, at : at + size].reshape((devices,) + shape)
        piece = jnp.moveaxis(piece, 0, axis_dim)
        full = shape[:axis_dim] + (devices * shape[axis_dim],) + shape[axis_dim + 1 :]
        weights[n] = piece.reshape(full)
        at += size
    for n in large_at:
        weights[n] = [None] * LAYERS
        for layer in range(LAYERS):
            low, rows, wide = spans[n, layer]
            piece = gathered[:, low : low + rows * wide]
            piece = piece.reshape(devices, wide, rows, features).transpose(1, 0, 2, 3)
            piece = piece.reshape(wide, devices * rows, features)
            weights[n][layer] = piece if wide > 1 else piece[0]
    table = weights[4]
    heads = table.shape[-1]
    hidden = weights[10].shape[-1]
    cells = WIN * WIN
    onehot = offset_onehot(table.shape[1])
    pairs = jnp.einsum("pt,lth->lhp", onehot.astype(bf16), table, preferred_element_type=f32)
    pairs = pairs.reshape(LAYERS, heads, cells, cells).transpose(0, 1, 3, 2).astype(bf16)
    zero = jnp.zeros((features,), f32)

    def row(n, layer):
        return weights[n][layer].astype(f32).reshape(1, -1)

    active = counts[0] > 0
    current = images[0].astype(f32)
    saved = []
    for layer in range(LAYERS):
        mask, spread, spread_t = token_places(SHIFT if layer % 2 else 0)
        bias = run(
            bias_kernel,
            [shaped((heads, tokens, tokens), f32)],
            (pairs[layer], spread, spread_t, mask),
        )[0]
        b_qv = weights[3][layer].astype(f32)
        b_qkv = jnp.concatenate([b_qv[0], zero, b_qv[1]]).reshape(1, -1)
        attn = run(
            attn_fwd_kernel,
            [
                shaped((tokens, features), f32),
                shaped((tokens, features), bf16),
                shaped((tokens, 3 * features), bf16),
                shaped((features, tokens), bf16),
                shaped((heads, tokens, tokens), f32),
                shaped((features, tokens), bf16),
            ],
            (current, row(0, layer), row(1, layer), weights[2][layer], b_qkv, bias,
             weights[5][layer], row(6, layer)),
            [pltpu.VMEM((features, tokens), bf16)],
        )
        mlp = run(
            mlp_fwd_kernel,
            [
                shaped((tokens, features), f32),
                shaped((tokens, features), bf16),
                shaped((tokens, hidden), f32),
                shaped((tokens, hidden), bf16),
            ],
            (attn[0], row(7, layer), row(8, layer), weights[9][layer], row(10, layer),
             weights[11][layer], row(12, layer)),
        )
        saved.append((current, attn, mlp, spread, spread_t))
        current = mlp[0]
    outs = jnp.where(active, current, 0.0)[None]
    grad = jnp.where(active, cotangent[0].astype(f32), 0.0)
    sums = [[None] * LAYERS for _ in shards]
    owned = [[None] * LAYERS for _ in shards]

    def scatter(value):
        return value

    for layer in reversed(range(LAYERS)):
        entry, attn, mlp, spread, spread_t = saved[layer]
        g_mid, g_w1, g_w2, *rest = run(
            mlp_bwd_kernel,
            [
                shaped((tokens, features), f32),
                shaped((hidden // features, features, features), bf16),
                shaped((hidden, features), bf16),
                shaped((1, hidden), f32),
                shaped((1, features), f32),
                shaped((1, features), f32),
                shaped((1, features), f32),
                shaped((1, features), f32),
            ],
            (grad, attn[0], row(7, layer), weights[9][layer], weights[11][layer], *mlp[1:]),
        )
        sums[10][layer], sums[12][layer], sums[7][layer], sums[8][layer], sums[6][layer] = rest
        owned[11][layer] = scatter(g_w2)
        owned[9][layer] = scatter(g_w1)
        grad, g_qkv, g_proj, g_qv, g_pairs, g_gain, g_off = run(
            attn_bwd_kernel,
            [
                shaped((tokens, features), f32),
                shaped((3, features, features), bf16),
                shaped((features, features), bf16),
                shaped((2, features), f32),
                shaped((heads, cells, cells), f32),
                shaped((1, features), f32),
                shaped((1, features), f32),
            ],
            (g_mid, entry, row(0, layer), weights[2][layer], weights[5][layer], *attn[1:],
             spread, spread_t),
            [
                pltpu.VMEM((tokens, features), bf16),
                pltpu.VMEM((features, tokens), f32),
                pltpu.VMEM((tokens, 3 * features), bf16),
            ],
        )
        owned[5][layer] = scatter(g_proj)
        owned[2][layer] = scatter(g_qkv)
        sums[0][layer], sums[1][layer], sums[3][layer] = g_gain, g_off, g_qv
        per_pair = g_pairs.transpose(0, 2, 1).reshape(heads, cells * cells)
        sums[4][layer] = jnp.dot(per_pair, onehot, precision=lax.Precision.HIGHEST).T
    parts = []
    for n in small_at:
        shape, axis_dim = shards[n].shape, gather_dims[n]
        both = jnp.stack(sums[n])
        both = both.reshape(shape[:axis_dim] + (devices,) + shape[axis_dim:])
        parts.append(jnp.moveaxis(both, axis_dim, 0).reshape(devices, -1))
    packed = jnp.concatenate(parts, axis=1).astype(bf16)
    packed = jnp.pad(packed, ((0, 0), (0, small_rows * features - packed.shape[1])))
    blocks = [packed.reshape(devices, small_rows, features)]
    for layer in range(LAYERS):
        for n in large_at:
            low, rows, wide = spans[n, layer]
            piece = owned[n][layer].reshape(wide, devices, rows, features)
            blocks.append(piece.transpose(1, 0, 2, 3).reshape(devices, rows * wide, features))
    if spare:
        blocks.append(jnp.zeros((devices, spare, features), bf16))
    reduced = scatter_all(jnp.concatenate(blocks, axis=1), devices)
    summed = reduced[:small_rows].reshape(-1)
    at = 0
    for n in small_at:
        size = flats[n].shape[0]
        owned[n] = summed[at : at + size].reshape(shards[n].shape)
        at += size
    for n in large_at:
        for layer in range(LAYERS):
            low, rows, wide = spans[n, layer]
            piece = reduced[low : low + rows * wide].reshape(wide, rows, features)
            owned[n][layer] = piece.transpose(1, 0, 2).reshape(rows, wide * features)
        owned[n] = jnp.stack(owned[n])
    return (outs, grad[None], *owned)


GATHERED = (
    (None, 0, 0, 0, 1, 'hlxy'),
    (0, 0, 0, 1, 3, 'hlxy'),
    (0, 0, 1, 2, 3, 'hlyx'),
    (0, 0, 2, 3, 3, 'hlxy'),
    (0, 1, 0, 1, 1, 'hlyx'),
    (0, 2, 0, 1, 4, 'hyxl'),
    (0, 2, 1, 2, 4, 'hlxy'),
    (0, 2, 2, 3, 4, 'hylx'),
    (0, 2, 3, 4, 4, 'hlxy'),
    (0, 3, 0, 1, 4, 'yxhl'),
    (0, 3, 1, 2, 4, 'hxly'),
    (0, 3, 2, 4, 4, 'hlyx'),
    (1, 0, 0, 2, 3, 'hlxy'),
    (1, 0, 2, 3, 3, 'hlyx'),
    (1, 1, 0, 1, 1, 'hyxl'),
    (1, 2, 0, 1, 4, 'hlyx'),
    (1, 2, 1, 2, 4, 'hlyx'),
    (1, 2, 2, 3, 4, 'xyhl'),
    (1, 2, 3, 4, 4, 'hlyx'),
    (1, 3, 0, 2, 4, 'yxhl'),
    (1, 3, 2, 4, 4, 'xhly'),
)
SCATTERED = (
    (1, 3, 0, 2, 4, 'lxhy'),
    (1, 3, 2, 4, 4, 'xylh'),
    (1, 2, 0, 2, 4, 'lhyx'),
    (1, 2, 2, 4, 4, 'ylhx'),
    (1, 1, 0, 1, 1, 'xlhy'),
    (1, 0, 0, 1, 3, 'xylh'),
    (0, 3, 0, 2, 4, 'xlhy'),
    (1, 0, 1, 3, 3, 'yxlh'),
    (0, 3, 2, 4, 4, 'yxlh'),
    (0, 0, 0, 2, 3, 'xylh'),
    (0, 2, 0, 2, 4, 'xylh'),
    (0, 2, 2, 4, 4, 'lyxh'),
    (0, 1, 0, 1, 1, 'ylxh'),
    (0, 0, 2, 3, 3, 'yxlh'),
    (None, 0, 0, 0, 1, 'xylh'),
)
AGENDA = (
    (
        (0, 3, 0), (0, 2, 0), (0, 20, 0), (0, 10, 0), (0, 4, 0), (0, 17, 0),
        (0, 0, 0), (0, 8, 0), (0, 3, 1), (0, 15, 0), (0, 2, 1), (0, 17, 1),
        (0, 19, 0), (0, 10, 1), (0, 6, 0), (0, 4, 1), (0, 5, 0), (0, 9, 0),
        (0, 0, 1), (0, 11, 0), (0, 8, 1), (0, 3, 2), (0, 1, 0), (0, 15, 1),
        (0, 7, 0), (0, 2, 2), (0, 13, 0), (0, 19, 1), (0, 6, 1), (0, 4, 2),
        (0, 0, 2), (0, 18, 0), (0, 5, 1), (0, 9, 1), (0, 8, 2), (0, 3, 3),
        (0, 11, 1), (0, 2, 3), (0, 7, 1), (0, 14, 0), (0, 15, 2), (0, 1, 1),
        (0, 6, 2), (0, 12, 0), (0, 10, 2), (0, 16, 0),
    ),
    (
        (0, 5, 2), (0, 18, 1), (0, 11, 2), (0, 14, 1), (0, 4, 3), (0, 1, 2),
        (0, 17, 2), (0, 3, 4), (0, 12, 1), (0, 16, 1), (0, 7, 2), (0, 6, 3),
        (0, 20, 1), (0, 11, 3), (0, 18, 2), (0, 12, 2), (0, 13, 1), (0, 5, 3),
        (0, 0, 3), (0, 1, 3), (0, 9, 2), (0, 6, 4), (0, 17, 3), (0, 19, 2),
        (0, 2, 4), (0, 8, 3), (0, 10, 3), (0, 1, 4), (0, 20, 2), (0, 7, 3),
        (0, 13, 2), (0, 16, 2), (0, 5, 4), (0, 14, 2), (0, 15, 3), (0, 0, 4),
        (0, 8, 4), (0, 9, 3),
    ),
    (
        (0, 12, 3),
    ),
    (
        (0, 10, 4), (0, 11, 4), (0, 13, 3), (0, 7, 4), (0, 4, 4), (0, 18, 3),
        (0, 16, 3), (0, 14, 3),
    ),
    (
        (0, 20, 3), (0, 19, 3),
    ),
    (),
    (
        (0, 9, 4),
    ),
    (
        (0, 13, 4), (0, 12, 4), (0, 14, 4), (0, 17, 4),
    ),
    (
        (0, 15, 4), (0, 18, 4),
    ),
    (),
    (
        (0, 16, 4),
    ),
    (),
    (
        (0, 20, 4), (0, 19, 4),
    ),
    (),
    (
        (1, 0, 0), (1, 1, 0),
    ),
    (
        (1, 3, 0), (1, 0, 1), (1, 1, 1), (1, 2, 0),
    ),
    (
        (1, 4, 0), (1, 3, 1),
    ),
    (
        (1, 4, 1), (1, 2, 1),
    ),
    (),
    (
        (1, 1, 2), (1, 5, 0), (1, 7, 0), (1, 0, 2),
    ),
    (
        (1, 5, 1),
    ),
    (
        (1, 4, 2), (1, 3, 2), (1, 6, 0), (1, 7, 1),
    ),
    (
        (1, 6, 1), (1, 10, 0), (1, 2, 2), (1, 8, 0), (1, 1, 3), (1, 11, 0),
        (1, 5, 2), (1, 8, 1), (1, 10, 1), (1, 11, 1),
    ),
    (
        (1, 4, 3), (1, 12, 0),
    ),
    (),
    (
        (1, 7, 2), (1, 5, 3), (1, 12, 1),
    ),
    (
        (1, 9, 0), (1, 1, 4), (1, 6, 2), (1, 13, 0), (1, 3, 3), (1, 11, 2),
        (1, 9, 1), (1, 10, 2), (1, 13, 1), (1, 7, 3), (1, 0, 3), (1, 8, 2),
        (1, 12, 2), (1, 5, 4), (1, 6, 3),
    ),
    (
        (1, 10, 3), (1, 14, 0), (1, 4, 4), (1, 7, 4), (1, 9, 2), (1, 11, 3),
        (1, 2, 3), (1, 14, 1),
    ),
    (
        (1, 13, 2), (1, 8, 3), (1, 11, 4), (1, 0, 4), (1, 3, 4), (1, 12, 3),
        (1, 1, 5), (1, 9, 3), (1, 14, 2), (1, 10, 4), (1, 5, 5), (1, 13, 3),
        (1, 8, 4), (1, 4, 5), (1, 2, 4), (1, 14, 3), (1, 9, 4), (1, 12, 4),
        (1, 3, 5), (1, 0, 5), (1, 11, 5), (1, 13, 4), (1, 6, 4), (1, 2, 5),
        (1, 14, 4), (1, 10, 5),
    ),
    (
        (1, 12, 5), (1, 9, 5), (1, 7, 5), (1, 8, 5), (1, 13, 5), (1, 6, 5),
        (1, 14, 5),
    ),
)


def stack_rows(parts):
    return jnp.concatenate(parts, axis=0)


def permute_f32(matrix, rows):
    high = rows.astype(bf16)
    rest = rows - high.astype(f32)
    middle = rest.astype(bf16)
    low = (rest - middle.astype(f32)).astype(bf16)
    return dot_nn(matrix, high) + (dot_nn(matrix, middle) + dot_nn(matrix, low))


def slots_of(window):
    padded = -(-window // 8) * 8
    lanes_each = 64
    return padded, lanes_each


def places_in_windows(shift_by):
    token = np.arange(SIDE * SIDE)
    row = (token // SIDE - shift_by) % SIDE
    col = (token % SIDE - shift_by) % SIDE
    window = (row // WIN) * (SIDE // WIN) + col // WIN
    inside = (row % WIN) * WIN + col % WIN
    edges = SIDE - WIN, SIDE - shift_by
    a_row = (row >= edges[0]).astype(int) + (row >= edges[1]).astype(int)
    a_col = (col >= edges[0]).astype(int) + (col >= edges[1]).astype(int)
    return window, inside, 3 * a_row + a_col


def constants(heads, per_device_rows, devices):
    cells = WIN * WIN
    padded, wide = slots_of(cells)
    windows = (SIDE // WIN) ** 2
    tokens = SIDE * SIDE
    total = windows * padded
    perms = []
    for shift_by in (0, SHIFT):
        window, inside, label = places_in_windows(shift_by)
        perm = np.zeros((total, tokens), np.float32)
        perm[window * padded + inside, np.arange(tokens)] = 1.0
        perms.append(perm)
    mask = np.zeros((windows, padded, wide), np.float32)
    labels = np.zeros((windows, cells), int)
    labels[window, inside] = label
    mask[:, :cells, :cells] = np.where(labels[:, :, None] == labels[:, None, :], 0.0, mask_fill)
    group = 2 * lanes // wide
    mask = np.tile(mask, (1, 1, group))
    span = 2 * WIN - 1
    strips = -(-span * WIN // 16) * 16
    onehot = np.zeros((WIN, strips, devices * 8), np.float32)
    for c_q in range(WIN):
        for d_r in range(span):
            for c_k in range(WIN):
                t = d_r * span + c_q - c_k + WIN - 1
                spot = (t // per_device_rows) * 8 + t % per_device_rows
                onehot[c_q, (span - 1 - d_r) * WIN + c_k, spot] = 1.0
    onehot = onehot.reshape(WIN * strips, devices * 8)
    query = np.arange(heads * wide) % wide
    head = np.arange(heads * wide) // wide
    lane_row = np.where(query < cells, query // WIN, -1)
    lane_col = np.where(query < cells, query % WIN, -1)
    lane_of = np.zeros((8, heads * wide), np.int32)
    lane_of[0], lane_of[1] = lane_row, lane_col
    expand = np.zeros((lanes, heads * wide), np.float32)
    expand[head, np.arange(heads * wide)] = 1.0
    collect = np.zeros((heads * wide, lanes), np.float32)
    real = query < cells
    collect[np.arange(heads * wide)[real], (lane_col * heads + head)[real]] = 1.0
    fold = np.zeros((lanes, lanes), np.float32)
    for lane in range(WIN * heads):
        fold[lane, lane % heads] = 1.0
    plain, shifted = perms
    low = [plain, shifted, shifted @ plain.T, plain @ shifted.T, plain.T, shifted.T,
           onehot, onehot.T, expand, collect, fold]
    return [jnp.asarray(a, bf16) for a in low] + [jnp.asarray(lane_of), jnp.asarray(mask)]


AXES = "hlyxc"


class Links:
    def __init__(self, sems):
        me = lax.axis_index("fsdp")
        self.me = me
        self.own, self.peer = {}, {}
        for place, axis in enumerate(reversed(AXES)):
            bit = bit_of(me, place)
            self.own[axis] = bit
            self.peer[axis] = me + (1 - 2 * bit) * (1 << place)
        self.sems = sems
        self.copies = {}

    def greet(self):
        barrier = pltpu.get_barrier_semaphore()
        for axis in AXES:
            pl.semaphore_signal(
                barrier, inc=1, device_id=(self.peer[axis],), device_id_type=pl.DeviceIdType.MESH
            )

    def greeted(self):
        pl.semaphore_wait(pltpu.get_barrier_semaphore(), len(AXES))

    def send(self, key, way, source, target, axis):
        send_sem, recv_sem = self.sems[way]
        copy = pltpu.make_async_remote_copy(
            src_ref=source,
            dst_ref=target,
            send_sem=send_sem.at[key[1], key[0]],
            recv_sem=recv_sem.at[key[1], key[0]],
            device_id=(self.peer[axis],),
            device_id_type=pl.DeviceIdType.MESH,
        )
        copy.start()
        self.copies[(way,) + key] = copy

    def arrive(self, way, key):
        self.copies[(way,) + key].wait_recv()

    def finish(self):
        for copy in self.copies.values():
            copy.wait_send()


def all_kernel(
    gspans, rspans, agenda,
    count_ref, x_ref, cot_ref, again_ref, aoff_ref, wqkv_ref, bqv_ref, rel_ref, wproj_ref, bproj_ref,
    mgain_ref, moff_ref, w1_ref, b1_ref, w2_ref, b2_ref,
    plain_ref, shifted_ref, forth_ref, back_ref, plain_t_ref, shifted_t_ref,
    onehot_ref, onehot_t_ref, expand_ref, collect_ref, fold_ref, lane_ref, mask_ref,
    out_ref, gin_ref, gagain_ref, gaoff_ref, gwqkv_ref, gbqv_ref, grel_ref, gwproj_ref, gbproj_ref,
    gmgain_ref, gmoff_ref, gw1_ref, gb1_ref, gw2_ref, gb2_ref,
    w, g, land_0, land_1, land_2, land_3, land_4, sm, sg, sland_0, sland_1, sland_2, sland_3, sland_4,
    xs, xn_s, qkv_s, probs_s, mixed_s, mid_s, yn_s, slope_s, act_s,
    bias_s, strip_s, kinds_s, b1_s, own_s, mixf_s, dmix_s, dqkv_s, dsum_s, kg_s, b1g_s, rg_s,
    gs_send, gs_recv, rs_send, rs_recv,
):
    links = Links({"g": (gs_send, gs_recv), "r": (rs_send, rs_recv)})
    me = links.me
    every = slice(None)
    home = tuple(links.own[axis] for axis in AXES)
    devices = 1 << len(AXES)
    lands = ((land_0, sland_0), (land_1, sland_1), (land_2, sland_2), (land_3, sland_3), (land_4, sland_4))
    rows_each = wqkv_ref.shape[1]
    features = wproj_ref.shape[2]
    hidden = w1_ref.shape[2]
    parts = wqkv_ref.shape[2] // features
    wide_parts = hidden // features
    deep = w2_ref.shape[1]
    table_each = rel_ref.shape[0]
    heads = rel_ref.shape[2]
    size = features // heads
    scaling = size ** (-0.5)
    at_proj = parts * rows_each
    at_one = at_proj + rows_each
    at_two = at_one + wide_parts * rows_each
    cells = WIN * WIN
    padded, wide = slots_of(cells)
    windows = (SIDE // WIN) ** 2
    per = lanes // size
    group_lanes = per * wide
    share = features // devices
    pack = lanes // share
    share_one = hidden // devices
    pack_one = lanes // share_one
    span = 2 * WIN - 1
    strips = -(-span * WIN // 16) * 16

    links.greet()
    own_s[...] = jnp.zeros_like(own_s)
    at = 0
    for ref in (again_ref, aoff_ref, bqv_ref, bproj_ref, mgain_ref, moff_ref, b2_ref):
        piece = ref[...].astype(f32)
        if ref.shape[0] == LAYERS and len(ref.shape) == 3:
            for layer in range(LAYERS):
                own_s[at : at + ref.shape[1], 0:share] = piece[layer]
                at += ref.shape[1]
        else:
            own_s[at : at + LAYERS, 0:share] = piece
            at += LAYERS
    row_at = lax.broadcasted_iota(jnp.int32, (lanes, lanes), 0)
    lane_at = lax.broadcasted_iota(jnp.int32, (lanes, lanes), 1)
    spot = share * lax.rem(me, pack)
    place = jnp.where((lane_at == row_at + spot) & (row_at < share), 1.0, 0.0).astype(bf16)
    kinds = dot_nn(own_s[...].astype(bf16), place)
    spot = share_one * lax.rem(me, pack_one)
    place = jnp.where((lane_at == row_at + spot) & (row_at < share_one), 1.0, 0.0).astype(bf16)
    own_s[...] = jnp.zeros_like(own_s)
    own_s[0:LAYERS, 0:share_one] = b1_ref[...].astype(f32)
    firsts = dot_nn(own_s[...].astype(bf16), place)
    own_s[...] = jnp.zeros_like(own_s)
    tables = rel_ref[...].astype(f32)
    for layer in range(LAYERS):
        own_s[layer * 8 : layer * 8 + table_each, 0:heads] = tables[:, layer, :]
        own_s[layer * 8 + table_each : layer * 8 + table_each + 1, :] = firsts[layer : layer + 1]
    sm[home + (every, slice(0, lanes))] = kinds.astype(bf16)
    sm[home + (every, slice(lanes, 2 * lanes))] = own_s[...].astype(bf16)
    for layer in range(LAYERS):
        for part in range(parts):
            w[(layer,) + home + (pl.ds(part * rows_each, rows_each), every)] = (
                wqkv_ref[layer, :, part * features : (part + 1) * features]
            )
        w[(layer,) + home + (pl.ds(at_proj, rows_each), every)] = wproj_ref[layer]
        for part in range(wide_parts):
            w[(layer,) + home + (pl.ds(at_one + part * rows_each, rows_each), every)] = (
                w1_ref[layer, :, part * features : (part + 1) * features]
            )
        w[(layer,) + home + (pl.ds(at_two, deep), every)] = w2_ref[layer]

    def view(where, span, picks):
        big, small = where
        layer, low, count, _ = span
        if layer is None:
            return small.at[picks]
        return big.at[(layer,) + picks + (pl.ds(low, count),)]

    def gather(n, stage):
        span = gspans[n]
        route = span[3] + AXES[-1]
        if stage:
            links.arrive("g", (stage - 1, n))
        got = route[:stage]
        ref = view((w, sm), span, tuple(every if a in got else links.own[a] for a in AXES))
        links.send((stage, n), "g", ref, ref, route[stage])

    def merge(n, stage):
        span = rspans[n]
        closed = (AXES[-1] + span[3])[: stage + 1]
        opened = [axis for axis in AXES if axis not in closed]

        def one(at, carry):
            bits = {axis: bit_of(at, k) for k, axis in enumerate(reversed(opened))}
            here = view((g, sg), span, tuple(bits.get(a, links.own[a]) for a in AXES))
            there = view(lands[stage], span, tuple(bits[a] for a in opened))
            here[...] = here[...] + there[...]
            return carry

        lax.fori_loop(0, 1 << len(opened), one, 0)

    def scatter(n, stage):
        span = rspans[n]
        layer, low, count, _ = span
        order = AXES[-1] + span[3]
        if stage:
            links.arrive("r", (stage - 1, n))
        if stage < len(AXES):
            if stage:
                merge(n, stage - 1)
            axis, closed = order[stage], order[:stage]
            where = {a: links.own[a] if a in closed else every for a in AXES}
            where[axis] = 1 - links.own[axis]
            source = view((g, sg), span, tuple(where[a] for a in AXES))
            target = view(lands[stage], span, (every,) * (len(AXES) - 1 - stage))
            links.send((stage, n), "r", source, target, axis)
            return
        if layer is None:
            small_out(sg[home].astype(f32) + sland_4[...].astype(f32))
            return
        for unit in range(low, low + count, rows_each):
            rows = pl.ds(unit, rows_each)
            total = g[(layer,) + home + (rows,)].astype(f32) + land_4[layer, rows, :].astype(f32)
            if unit < at_proj:
                part = unit // rows_each
                gwqkv_ref[layer, :, part * features : (part + 1) * features] = total
            elif unit < at_one:
                gwproj_ref[layer] = total
            elif unit < at_two:
                part = (unit - at_one) // rows_each
                gw1_ref[layer, :, part * features : (part + 1) * features] = total
            else:
                gw2_ref[layer, unit - at_two : unit - at_two + rows_each, :] = total

    def small_out(total):
        picked = jnp.where(lax.broadcasted_iota(jnp.int32, (16, lanes), 1) // share == lax.rem(me, pack),
                           total[:, 0:lanes], 0.0)
        folded = picked[:, 0:share]
        for n in range(1, pack):
            folded = folded + picked[:, n * share : (n + 1) * share]
        at = 0
        for ref in (gagain_ref, gaoff_ref, gbqv_ref, gbproj_ref, gmgain_ref, gmoff_ref, gb2_ref):
            if len(ref.shape) == 3:
                for layer in range(LAYERS):
                    ref[layer] = folded[at : at + ref.shape[1]]
                    at += ref.shape[1]
            else:
                ref[...] = folded[at : at + LAYERS]
                at += LAYERS
        tail = total[:, lanes : 2 * lanes]
        for layer in range(LAYERS):
            grel_ref[layer] = tail[layer * 8 : layer * 8 + table_each, 0:heads]
            row = tail[layer * 8 + table_each : layer * 8 + table_each + 1]
            keep = lax.broadcasted_iota(jnp.int32, (1, lanes), 1) // share_one
            row = jnp.where(keep == lax.rem(me, pack_one), row, 0.0)
            folded_row = row[:, 0:share_one]
            for n in range(1, pack_one):
                folded_row = folded_row + row[:, n * share_one : (n + 1) * share_one]
            gb1_ref[layer : layer + 1, :] = folded_row

    def qkv_part(layer, part):
        block = w[layer, :, :, :, :, :, part * rows_each : (part + 1) * rows_each, :]
        return block.reshape(features, features)

    def proj_of(layer):
        return w[layer, :, :, :, :, :, at_proj : at_proj + rows_each, :].reshape(features, features)

    def one_of(layer, part):
        low = at_one + part * rows_each
        return w[layer, :, :, :, :, :, low : low + rows_each, :].reshape(features, features)

    def two_of(layer, part):
        return w[layer, part // 2, part % 2, :, :, :, at_two : at_two + deep, :].reshape(features, features)

    def put(layer, low, value):
        g[layer, :, :, :, :, :, low : low + rows_each, :] = value.astype(bf16).reshape(
            2, 2, 2, 2, 2, rows_each, features
        )

    agenda = list(agenda)

    def go():
        for way, n, stage in agenda.pop(0):
            (gather if way == 0 else scatter)(n, stage)

    def have(layer, low, high):
        for n, span in enumerate(gspans):
            if span[0] == layer and (layer is None or low <= span[1] < high):
                links.arrive("g", (4, n))

    links.greeted()
    go()

    stream = dot_nn(plain_ref[...], x_ref[0])
    xs[0] = stream
    qkv_s[:, :, 48:64, :] = jnp.zeros((LAYERS, windows, 16, parts * features), bf16)
    dmix_s[:, 48:64, :] = jnp.zeros((windows, 16, features), bf16)
    strip_s[...] = jnp.zeros_like(strip_s)

    go()
    have(None, 0, 0)
    small = sm[...].reshape(devices, 16, 2 * lanes).astype(f32)
    for tile in range(features // lanes):
        block = small[tile * pack : (tile + 1) * pack, :, 0:lanes]
        kinds_s[:, tile * lanes : (tile + 1) * lanes] = jnp.sum(block, axis=0)
    for tile in range(hidden // lanes):
        total = small[tile * pack_one, :, lanes : 2 * lanes]
        for n in range(1, pack_one):
            total = total + small[tile * pack_one + n, :, lanes : 2 * lanes]
        for layer in range(LAYERS):
            at = layer * 8 + table_each
            b1_s[layer : layer + 1, tile * lanes : (tile + 1) * lanes] = total[at : at + 1]

    def kind(n):
        return kinds_s[n : n + 1, :]

    lane_row = lane_ref[0:1, :]
    lane_col = lane_ref[1:2, :]
    for layer in range(LAYERS):
        table = small[:, layer * 8 : (layer + 1) * 8, lanes : 2 * lanes]
        table = table.reshape(devices * 8, lanes).astype(bf16)
        spread = dot_nn(table, expand_ref[...]).astype(bf16)
        strip = jnp.zeros((strips, heads * wide), f32)
        for col in range(WIN):
            found = dot_nn(onehot_ref[col * strips : (col + 1) * strips, :], spread)
            strip = jnp.where(lane_col == col, found, strip)
        strip_s[0:strips, :] = strip
        bias = jnp.zeros((padded, heads * wide), f32)
        for row in range(WIN):
            low = (WIN - 1 - row) * WIN
            bias = jnp.where(lane_row == row, strip_s[low : low + padded, :], bias)
        key_at = lax.broadcasted_iota(jnp.int32, (padded, heads * wide), 0)
        bias_s[layer] = jnp.where(key_at < cells, bias, outside_fill)

    keeps = [head_mask(one, size) for one in range(per)]

    def diagonal(block):
        return stack_rows([block * keep for keep in keeps])

    def undiagonal(block):
        total = block[0:padded] * keeps[0].astype(f32)
        for n in range(1, per):
            total = total + block[n * wide : n * wide + padded] * keeps[n].astype(f32)
        return total

    def both_halves(group):
        groups = heads // per
        go()
        lax.fori_loop(0, groups // 2, group, 0)
        go()
        lax.fori_loop(groups // 2, groups, group, 0)

    def attention_forward(layer):
        rows = xs[layer]
        go()
        have(layer, 0, at_proj)
        unit, _ = normalize(rows)
        xn = (unit * kind(layer) + kind(LAYERS + layer)).astype(bf16)
        xn_s[layer] = xn
        for part in range(parts):
            block = dot_nn(xn, qkv_part(layer, part))
            if part != 1:
                block = block + kind(2 * LAYERS + 2 * layer + part // 2)
            for window in range(windows):
                qkv_s[layer, window, 0:padded, part * features : (part + 1) * features] = (
                    block[window * padded : (window + 1) * padded].astype(bf16)
                )

        def group(n, carry):
            start = pl.multiple_of(n * lanes, lanes)
            bias = bias_s[layer, :, pl.ds(pl.multiple_of(n * group_lanes, lanes), group_lanes)]
            for window in range(windows):
                query = qkv_s[layer, window, :, pl.ds(start, lanes)]
                key = qkv_s[layer, window, 0:padded, pl.ds(pl.multiple_of(features + start, lanes), lanes)]
                value = qkv_s[layer, window, 0:padded, pl.ds(pl.multiple_of(2 * features + start, lanes), lanes)]
                scores = dot_nt(key, diagonal(query)) * scaling + bias
                if layer % 2:
                    scores = scores + mask_ref[window]
                raised = jnp.exp(scores - jnp.max(scores, axis=0, keepdims=True))
                probs = raised * (1.0 / jnp.sum(raised, axis=0, keepdims=True))
                probs_s[layer, n, window] = probs
                mixed = undiagonal(dot_tn(probs.astype(bf16), value))
                mixf_s[window * padded : (window + 1) * padded, pl.ds(start, lanes)] = mixed
            return carry

        both_halves(group)
        go()
        have(layer, at_proj, at_one)
        mixed = mixf_s[...].astype(bf16)
        mixed_s[layer] = mixed
        mid_s[layer] = rows + dot_nn(mixed, proj_of(layer)) + kind(4 * LAYERS + layer)

    def mlp_forward(layer):
        go()
        have(layer, at_one, at_two)
        middle = mid_s[layer]
        unit, _ = normalize(middle)
        yn = (unit * kind(5 * LAYERS + layer) + kind(6 * LAYERS + layer)).astype(bf16)
        yn_s[layer] = yn
        for part in range(wide_parts):
            cols = slice(part * features, (part + 1) * features)
            pre = dot_nn(yn, one_of(layer, part)) + b1_s[layer : layer + 1, cols]
            cumul = 0.5 * (1.0 + lax.erf(pre * half_root))
            slope_s[layer, :, cols] = cumul + pre * (jnp.exp(-0.5 * pre * pre) * inv_root_tau)
            act_s[layer, :, cols] = (pre * cumul).astype(bf16)

    def mlp_rest(layer):
        total = mid_s[layer] + kind(7 * LAYERS + layer)
        for part in range(wide_parts):
            cols = slice(part * features, (part + 1) * features)
            total = total + dot_nn(act_s[layer, :, cols], two_of(layer, part))
        return total

    attention_forward(0)
    mlp_forward(0)
    go()
    have(0, at_two, at_two + deep)
    xs[1] = permute_f32(forth_ref[...], mlp_rest(0))
    attention_forward(1)
    mlp_forward(1)
    active = count_ref[0] > 0

    def mlp_backward(layer, grad):
        low = grad.astype(bf16)
        kg_s[7 * LAYERS + layer : 7 * LAYERS + layer + 1, :] = jnp.sum(grad, axis=0, keepdims=True)
        go()
        for part in range(wide_parts):
            cols = slice(part * features, (part + 1) * features)
            g[layer, part // 2, part % 2, :, :, :, at_two : at_two + deep, :] = (
                dot_tn(act_s[layer, :, cols], low).astype(bf16).reshape(2, 2, 2, deep, features)
            )
        go()
        if layer == LAYERS - 1:
            have(layer, at_two, at_two + deep)
        yn = yn_s[layer]
        g_yn = jnp.zeros_like(grad)
        for part in range(wide_parts):
            cols = slice(part * features, (part + 1) * features)
            g_pre = dot_nt(low, two_of(layer, part)) * slope_s[layer, :, cols]
            b1g_s[layer : layer + 1, cols] = jnp.sum(g_pre, axis=0, keepdims=True)
            pre_low = g_pre.astype(bf16)
            put(layer, at_one + part * rows_each, dot_tn(yn, pre_low))
            g_yn = g_yn + dot_nt(pre_low, one_of(layer, part))
        back, g_gain, g_off = norm_pull(mid_s[layer], kind(5 * LAYERS + layer), g_yn)
        kg_s[5 * LAYERS + layer : 5 * LAYERS + layer + 1, :] = g_gain
        kg_s[6 * LAYERS + layer : 6 * LAYERS + layer + 1, :] = g_off
        g_mid = grad + back
        kg_s[4 * LAYERS + layer : 4 * LAYERS + layer + 1, :] = jnp.sum(g_mid, axis=0, keepdims=True)
        return g_mid

    def attention_backward(layer, g_mid):
        go()
        low = g_mid.astype(bf16)
        put(layer, at_proj, dot_tn(mixed_s[layer], low))
        d_mix = dot_nt(low, proj_of(layer))
        for window in range(windows):
            dmix_s[window, 0:padded, :] = d_mix[window * padded : (window + 1) * padded].astype(bf16)

        def group(n, carry):
            start = pl.multiple_of(n * lanes, lanes)
            k_at = pl.multiple_of(features + start, lanes)
            v_at = pl.multiple_of(2 * features + start, lanes)
            total = jnp.zeros((padded, group_lanes), f32)
            for window in range(windows):
                here = slice(window * padded, (window + 1) * padded)
                query = diagonal(qkv_s[layer, window, :, pl.ds(start, lanes)])
                key = qkv_s[layer, window, 0:padded, pl.ds(k_at, lanes)]
                value = qkv_s[layer, window, 0:padded, pl.ds(v_at, lanes)]
                d_out = diagonal(dmix_s[window, :, pl.ds(start, lanes)])
                probs = probs_s[layer, n, window]
                d_probs = dot_nt(value, d_out)
                dqkv_s[here, pl.ds(v_at, lanes)] = dot_nn(probs.astype(bf16), d_out)
                weighed = probs * d_probs
                d_scores = weighed - probs * jnp.sum(weighed, axis=0, keepdims=True)
                total = total + d_scores
                scores_low = d_scores.astype(bf16)
                dqkv_s[here, pl.ds(k_at, lanes)] = dot_nn(scores_low, query) * scaling
                dqkv_s[here, pl.ds(start, lanes)] = undiagonal(dot_tn(scores_low, key)) * scaling
            dsum_s[:, pl.ds(pl.multiple_of(n * group_lanes, lanes), group_lanes)] = total
            return carry

        both_halves(group)
        go()
        for n, part in ((0, 0), (1, 2)):
            column = jnp.sum(dqkv_s[:, part * features : (part + 1) * features], axis=0, keepdims=True)
            at = 2 * LAYERS + 2 * layer + n
            kg_s[at : at + 1, :] = column
        xn = xn_s[layer]
        g_xn = jnp.zeros_like(g_mid)
        for part in range(parts):
            block = dqkv_s[:, part * features : (part + 1) * features].astype(bf16)
            put(layer, part * rows_each, dot_tn(xn, block))
            g_xn = g_xn + dot_nt(block, qkv_part(layer, part))
        go()
        back, g_gain, g_off = norm_pull(xs[layer], kind(layer), g_xn)
        kg_s[layer : layer + 1, :] = g_gain
        kg_s[LAYERS + layer : LAYERS + layer + 1, :] = g_off
        strip_s[...] = jnp.zeros_like(strip_s)
        for row in range(WIN):
            at = (WIN - 1 - row) * WIN
            strip_s[at : at + padded, :] = strip_s[at : at + padded, :] + jnp.where(
                lane_row == row, dsum_s[...], 0.0
            )
        by_col = dot_nn(strip_s[0:strips, :].astype(bf16), collect_ref[...])
        col_at = lax.broadcasted_iota(jnp.int32, (1, lanes), 1) // heads
        stacked = stack_rows([jnp.where(col_at == col, by_col, 0.0).astype(bf16) for col in range(WIN)])
        table = dot_nn(onehot_t_ref[...], stacked)
        high = table.astype(bf16)
        rest = (table - high.astype(f32)).astype(bf16)
        table = dot_nn(high, fold_ref[...]) + dot_nn(rest, fold_ref[...])
        rg_s[:, layer * 8 : (layer + 1) * 8, :] = table.reshape(devices, 8, lanes)
        return g_mid + back

    grad = jnp.where(active, dot_nn(shifted_ref[...], cot_ref[0]), 0.0)
    g_x = attention_backward(1, mlp_backward(1, grad))
    grad = permute_f32(back_ref[...], g_x)
    g_x = attention_backward(0, mlp_backward(0, grad))
    for tile in range(hidden // lanes):
        for n in range(pack_one):
            for layer in range(LAYERS):
                at = layer * 8 + table_each
                rg_s[tile * pack_one + n, at : at + 1, :] = (
                    b1g_s[layer : layer + 1, tile * lanes : (tile + 1) * lanes]
                )
    for tile in range(features // lanes):
        block = kg_s[:, tile * lanes : (tile + 1) * lanes].astype(bf16)
        for n in range(pack):
            device = tile * pack + n
            sg[device // 16, (device // 8) % 2, (device // 4) % 2, (device // 2) % 2, device % 2, :, 0:lanes] = block
    sg[:, :, :, :, :, :, lanes : 2 * lanes] = rg_s[...].astype(bf16).reshape(2, 2, 2, 2, 2, 16, lanes)
    go()
    gin_ref[0] = permute_f32(plain_t_ref[...], g_x)
    go()
    out_ref[0] = jnp.where(active, permute_f32(shifted_t_ref[...], mlp_rest(1)), 0.0)
    go()
    links.finish()


def finish_kernel(*refs):
    count = len(refs) // 2
    for n, (source, target) in enumerate(zip(refs[:count], refs[count:])):
        if n < 2:
            target[...] = source[0][:, None, :]
        elif n == 6:
            for layer in range(LAYERS):
                target[:, layer, :] = source[layer]
        else:
            target[...] = source[...]


def whole(devices):
    def local(images, cotangent, counts, *shards):
        twos = (2,) * len(AXES)
        rows_each, features = shards[5].shape[1:]
        hidden = shards[9].shape[2]
        deep = shards[11].shape[1]
        parts, wide_parts = shards[2].shape[2] // features, hidden // features
        heads = shards[4].shape[2]
        cells = WIN * WIN
        padded, wide = slots_of(cells)
        windows = (SIDE // WIN) ** 2
        total = windows * padded
        tokens = images.shape[1]
        at_one = (parts + 1) * rows_each
        at_two = at_one + wide_parts * rows_each
        depth = at_two + deep
        edges = (0, parts * rows_each, at_one, at_two, depth)

        def spans_of(pieces):
            spans = []
            for layer, part, start, stop, of, route in pieces:
                if layer is None:
                    spans.append((None, 0, 0, route))
                    continue
                rows = edges[part + 1] - edges[part]
                low = edges[part] + rows * start // of
                spans.append((layer, low, edges[part] + rows * stop // of - low, route))
            return tuple(spans)

        gspans, rspans = spans_of(GATHERED), spans_of(SCATTERED)
        consts = constants(heads, shards[4].shape[1], devices)
        held = list(shards)
        held[4] = jnp.transpose(held[4], (1, 0, 2))
        args = [counts, images, cotangent, *held, *consts]
        outs = [shaped(images.shape, f32), shaped(images.shape, f32)]
        outs += [shaped(s.shape, f32) for s in shards]
        vmem = pltpu.VMEM
        strips = -(-(2 * WIN - 1) * WIN // 16) * 16
        tall = (WIN - 1) * WIN + padded
        tall = max(-(-tall // 8) * 8, strips)
        scratch = [
            *[vmem((LAYERS,) + twos + (depth, features), bf16)] * 2,
            *[vmem((LAYERS,) + twos[n:] + (depth, features), bf16) for n in range(1, len(AXES) + 1)],
            *[vmem(twos + (16, 2 * lanes), bf16)] * 2,
            *[vmem(twos[n:] + (16, 2 * lanes), bf16) for n in range(1, len(AXES) + 1)],
            vmem((LAYERS, total, features), f32),
            vmem((LAYERS, total, features), bf16),
            vmem((LAYERS, windows, wide, parts * features), bf16),
            vmem((LAYERS, heads * wide // (2 * lanes), windows, padded, 2 * lanes), f32),
            vmem((LAYERS, total, features), bf16),
            vmem((LAYERS, total, features), f32),
            vmem((LAYERS, total, features), bf16),
            vmem((LAYERS, total, hidden), f32),
            vmem((LAYERS, total, hidden), bf16),
            vmem((LAYERS, padded, heads * wide), f32),
            vmem((tall, heads * wide), f32),
            vmem((16, features), f32),
            vmem((8, hidden), f32),
            vmem((16, lanes), f32),
            vmem((total, features), f32),
            vmem((windows, wide, features), bf16),
            vmem((total, parts * features), f32),
            vmem((padded, heads * wide), f32),
            vmem((16, features), f32),
            vmem((8, hidden), f32),
            vmem((devices, 16, lanes), f32),
        ]
        scratch += [pltpu.SemaphoreType.DMA((len(gspans), len(AXES)))] * 2
        scratch += [pltpu.SemaphoreType.DMA((len(rspans), len(AXES)))] * 2
        space = pl.BlockSpec(memory_space=pltpu.VMEM)
        results = pl.pallas_call(
            functools.partial(all_kernel, gspans, rspans, AGENDA),
            out_shape=tuple(outs),
            in_specs=[pl.BlockSpec(memory_space=pltpu.SMEM)] + [space] * (len(args) - 1),
            out_specs=tuple([space] * len(outs)),
            scratch_shapes=scratch,
            compiler_params=pltpu.CompilerParams(
                collective_id=2, has_side_effects=True, vmem_limit_bytes=63 * 1024 * 1024
            ),
        )(*args)
        shapes = [r.shape for r in results]
        for n in (0, 1):
            shapes[n] = (tokens, 1, features)
        shapes[6] = (shapes[6][1], LAYERS, shapes[6][2])
        results = pl.pallas_call(
            finish_kernel,
            out_shape=tuple(shaped(s, f32) for s in shapes),
            in_specs=[space] * len(shapes),
            out_specs=tuple([space] * len(shapes)),
        )(*results)
        results = list(results)
        for n in (0, 1, 6):
            results[n] = jnp.transpose(results[n], (1, 0, 2))
        return tuple(results)

    return local


def fits_whole(devices, sizes):
    features, hidden, heads, table_rows, wide = sizes
    if devices != 1 << len(AXES) or features % devices or hidden % devices or table_rows % devices:
        return False
    rows_each, share_one, table_each = features // devices, hidden // devices, table_rows // devices
    return (
        rows_each % 16 == 0
        and lanes % rows_each == 0
        and lanes % share_one == 0
        and table_each <= 7
        and hidden * 8 == features * devices
        and lanes * heads == 4 * features
        and WIN * heads <= lanes
        and LAYERS == 2
        and share_one % (4 * 16) == 0
        and wide == 3 * features
    )


def solution(mesh):
    in_specs = (
        P("fsdp", None, None),
        P("fsdp", None, None),
        P("fsdp"),
        P(None, "fsdp"),
        P(None, "fsdp"),
        P(None, "fsdp", None),
        P(None, None, "fsdp"),
        P(None, "fsdp", None),
        P(None, "fsdp", None),
        P(None, "fsdp"),
        P(None, "fsdp"),
        P(None, "fsdp"),
        P(None, "fsdp", None),
        P(None, "fsdp"),
        P(None, "fsdp", None),
        P(None, "fsdp"),
    )
    out_specs = (
        P("fsdp", None, None),
        P("fsdp", None, None),
        P(None, "fsdp"),
        P(None, "fsdp"),
        P(None, "fsdp", None),
        P(None, None, "fsdp"),
        P(None, "fsdp", None),
        P(None, "fsdp", None),
        P(None, "fsdp"),
        P(None, "fsdp"),
        P(None, "fsdp"),
        P(None, "fsdp", None),
        P(None, "fsdp"),
        P(None, "fsdp", None),
        P(None, "fsdp"),
    )
    devices = mesh.shape["fsdp"]

    def step(images, cotangent, counts, *params):
        hidden, (_, table_rows, heads) = params[9].shape[2], params[4].shape
        sizes = (images.shape[2], hidden, heads, table_rows, params[2].shape[2])
        body = whole(devices) if fits_whole(devices, sizes) else local
        return jax.shard_map(
            body, mesh=mesh, in_specs=in_specs, out_specs=out_specs, check_vma=False
        )(images, cotangent, counts, *params)

    return step
```

```python
import functools

import jax
import jax.numpy as jnp
import numpy as np
from jax import lax
from jax.experimental import pallas as pl
from jax.experimental.pallas import tpu as pltpu
from jax.sharding import PartitionSpec as P

WIN = 7
SIDE = 14
LAYERS = 2
SHIFT = 3

norm_eps = 1e-05
mask_fill = -10000.0
outside_fill = -1e30
half_root = 0.7071067811865476
inv_root_tau = 0.3989422804014327
lanes = 128
bf16 = jnp.bfloat16
f32 = jnp.float32


def dot_nn(left, right):
    return lax.dot_general(left, right, (((1,), (0,)), ((), ())), preferred_element_type=f32)


def dot_nt(left, right):
    return lax.dot_general(left, right, (((1,), (1,)), ((), ())), preferred_element_type=f32)


def dot_tn(left, right):
    return lax.dot_general(left, right, (((0,), (0,)), ((), ())), preferred_element_type=f32)


def normalize(rows):
    centred = rows - jnp.mean(rows, axis=-1, keepdims=True)
    spread = jnp.mean(centred * centred, axis=-1, keepdims=True)
    inverse = lax.rsqrt(spread + norm_eps)
    return centred * inverse, inverse


def norm_pull(rows, gain, grad):
    unit, inverse = normalize(rows)
    g_gain = jnp.sum(grad * unit, axis=0, keepdims=True)
    g_bias = jnp.sum(grad, axis=0, keepdims=True)
    scaled = grad * gain
    back = inverse * (
        scaled
        - jnp.mean(scaled, axis=-1, keepdims=True)
        - unit * jnp.mean(scaled * unit, axis=-1, keepdims=True)
    )
    return back, g_gain, g_bias


def head_mask(local_head, head_size):
    lane = lax.broadcasted_iota(jnp.int32, (1, lanes), 1)
    return jnp.where(lane // head_size == local_head, 1.0, 0.0).astype(bf16)


def bias_kernel(pairs_ref, spread_ref, spread_t_ref, mask_ref, out_ref):
    def step(head, carry):
        rows = dot_nn(spread_ref[...], pairs_ref[head]).astype(bf16)
        out_ref[head] = dot_nn(rows, spread_t_ref[...]) + mask_ref[...]
        return carry

    lax.fori_loop(0, pairs_ref.shape[0], step, 0)


def attn_fwd_kernel(
    x_ref, gain_ref, off_ref, wqkv_ref, bqkv_ref, bias_ref, wproj_ref, bproj_ref,
    mid_ref, xn_ref, qkv_ref, key_t_ref, probs_ref, mixed_t_ref,
    val_t,
):
    rows = x_ref[...]
    features = rows.shape[1]
    heads = bias_ref.shape[0]
    size = features // heads
    scaling = size ** (-0.5)
    unit, _ = normalize(rows)
    xn = (unit * gain_ref[...] + off_ref[...]).astype(bf16)
    xn_ref[...] = xn
    for part in range(3):
        cols = pl.ds(part * features, features)
        block = dot_nn(xn, wqkv_ref[part]) + bqkv_ref[:, cols]
        qkv_ref[:, cols] = block.astype(bf16)
        if part == 1:
            key_t_ref[...] = block.T.astype(bf16)
        if part == 2:
            val_t[...] = block.T.astype(bf16)
    per = lanes // size

    def group(g, carry):
        start = pl.multiple_of(g * lanes, lanes)
        query = qkv_ref[:, pl.ds(start, lanes)]
        keys = qkv_ref[:, pl.ds(pl.multiple_of(features + start, lanes), lanes)]
        for one in range(per):
            head = g * per + one
            at = pl.ds(pl.multiple_of(head * size, size), size)
            scores = dot_nt(keys * head_mask(one, size), query) * scaling + bias_ref[head]
            peak = jnp.max(scores, axis=0, keepdims=True)
            raised = jnp.exp(scores - peak)
            total = jnp.sum(raised, axis=0, keepdims=True)
            probs = raised * (1.0 / total)
            probs_ref[head] = probs
            mixed_t_ref[at, :] = dot_nn(val_t[at, :], probs.astype(bf16)).astype(bf16)
        return carry

    lax.fori_loop(0, heads // per, group, 0)
    mixed = mixed_t_ref[...].astype(f32).T.astype(bf16)
    mid_ref[...] = rows + dot_nn(mixed, wproj_ref[...]) + bproj_ref[...]


def mlp_fwd_kernel(
    mid_ref, gain_ref, off_ref, w1_ref, b1_ref, w2_ref, b2_ref,
    out_ref, yn_ref, slope_ref, act_ref,
):
    middle = mid_ref[...]
    features = middle.shape[1]
    unit, _ = normalize(middle)
    yn = (unit * gain_ref[...] + off_ref[...]).astype(bf16)
    yn_ref[...] = yn
    total = middle + b2_ref[...]
    for chunk in range(w1_ref.shape[0]):
        cols = pl.ds(chunk * features, features)
        pre = dot_nn(yn, w1_ref[chunk]) + b1_ref[:, cols]
        cumul = 0.5 * (1.0 + lax.erf(pre * half_root))
        slope_ref[:, cols] = cumul + pre * (jnp.exp(-0.5 * pre * pre) * inv_root_tau)
        act = (pre * cumul).astype(bf16)
        act_ref[:, cols] = act
        total = total + dot_nn(act, w2_ref[cols, :])
    out_ref[...] = total


def mlp_bwd_kernel(
    g_ref, mid_ref, gain_ref, w1_ref, w2_ref, yn_ref, slope_ref, act_ref,
    gm_ref, gw1_ref, gw2_ref, gb1_ref, gb2_ref, ggain_ref, goff_ref, gbproj_ref,
):
    grad = g_ref[...]
    features = grad.shape[1]
    low = grad.astype(bf16)
    gb2_ref[...] = jnp.sum(grad, axis=0, keepdims=True)
    yn = yn_ref[...]
    g_yn = jnp.zeros_like(grad)
    for chunk in range(w1_ref.shape[0]):
        cols = pl.ds(chunk * features, features)
        gw2_ref[cols, :] = dot_tn(act_ref[:, cols], low).astype(bf16)
        g_pre = dot_nt(low, w2_ref[cols, :]) * slope_ref[:, cols]
        gb1_ref[:, cols] = jnp.sum(g_pre, axis=0, keepdims=True)
        pre_low = g_pre.astype(bf16)
        gw1_ref[chunk] = dot_tn(yn, pre_low).astype(bf16)
        g_yn = g_yn + dot_nt(pre_low, w1_ref[chunk])
    back, g_gain, g_off = norm_pull(mid_ref[...], gain_ref[...], g_yn)
    ggain_ref[...] = g_gain
    goff_ref[...] = g_off
    g_mid = grad + back
    gm_ref[...] = g_mid
    gbproj_ref[...] = jnp.sum(g_mid, axis=0, keepdims=True)


def attn_bwd_kernel(
    gm_ref, x_ref, gain_ref, wqkv_ref, wproj_ref, xn_ref, qkv_ref, key_t_ref, probs_ref,
    mixed_t_ref, spread_ref, spread_t_ref,
    gx_ref, gwqkv_ref, gwproj_ref, gqv_ref, gpairs_ref, ggain_ref, goff_ref,
    dmix, dq_t, dqkv,
):
    g_mid = gm_ref[...]
    features = g_mid.shape[1]
    heads = probs_ref.shape[0]
    size = features // heads
    scaling = size ** (-0.5)
    low = g_mid.astype(bf16)
    gwproj_ref[...] = dot_nn(mixed_t_ref[...], low).astype(bf16)
    dmix[...] = dot_nt(low, wproj_ref[...]).astype(bf16)
    per = lanes // size

    def group(g, carry):
        start = pl.multiple_of(g * lanes, lanes)
        k_at = pl.multiple_of(features + start, lanes)
        v_at = pl.multiple_of(2 * features + start, lanes)
        query = qkv_ref[:, pl.ds(start, lanes)]
        values = qkv_ref[:, pl.ds(v_at, lanes)]
        d_mix = dmix[:, pl.ds(start, lanes)]
        d_keys = jnp.zeros(query.shape, f32)
        d_values = jnp.zeros(query.shape, f32)
        for one in range(per):
            head = g * per + one
            at = pl.ds(pl.multiple_of(head * size, size), size)
            keep = head_mask(one, size)
            probs = probs_ref[head]
            d_probs = dot_nt(values * keep, d_mix)
            d_values = d_values + dot_nn(probs.astype(bf16), d_mix * keep)
            weighed = probs * d_probs
            d_scores = weighed - probs * jnp.sum(weighed, axis=0, keepdims=True)
            scores_low = d_scores.astype(bf16)
            d_keys = d_keys + dot_nn(scores_low, query * keep)
            dq_t[at, :] = dot_nn(key_t_ref[at, :], scores_low)
            folded = dot_nn(spread_t_ref[...], scores_low).astype(bf16)
            gpairs_ref[head] = dot_nn(folded, spread_ref[...])
        dqkv[:, pl.ds(k_at, lanes)] = (d_keys * scaling).astype(bf16)
        dqkv[:, pl.ds(v_at, lanes)] = d_values.astype(bf16)
        gqv_ref[1:2, pl.ds(start, lanes)] = jnp.sum(d_values, axis=0, keepdims=True)
        return carry

    lax.fori_loop(0, heads // per, group, 0)
    d_query = dq_t[...].T * scaling
    gqv_ref[0:1, :] = jnp.sum(d_query, axis=0, keepdims=True)
    dqkv[:, :features] = d_query.astype(bf16)
    xn = xn_ref[...]
    g_xn = jnp.zeros_like(g_mid)
    for part in range(3):
        cols = pl.ds(part * features, features)
        block = dqkv[:, cols]
        gwqkv_ref[part] = dot_tn(xn, block).astype(bf16)
        g_xn = g_xn + dot_nt(block, wqkv_ref[part])
    back, g_gain, g_off = norm_pull(x_ref[...], gain_ref[...], g_xn)
    ggain_ref[...] = g_gain
    goff_ref[...] = g_off
    gx_ref[...] = g_mid + back


def bit_of(index, place):
    return lax.rem(index // (1 << place), 2)


def peers_of(me, places):
    return [me + (1 - 2 * bit_of(me, place)) * (1 << place) for place in range(places)]


def greet(me, places):
    barrier = pltpu.get_barrier_semaphore()
    for peer in peers_of(me, places):
        pl.semaphore_signal(
            barrier, inc=1, device_id=(peer,), device_id_type=pl.DeviceIdType.MESH
        )
    pl.semaphore_wait(barrier, places)


def routes(places):
    high = list(range(places - 1, 2, -1))
    if places < 3:
        return [list(range(places - 1, -1, -1))]
    return [
        high + [2, 1, 0],
        high + [1, 2, 0],
        [2] + high + [1, 0],
        [1] + high + [2, 0],
    ]


def row_parts(total, count):
    units = total // 16
    sizes = [16 * (units // count + (1 if n < units % count else 0)) for n in range(count)]
    return [(sum(sizes[:n]), sizes[n]) for n in range(count)]


def region(places, free, me, lowest=0, forced=None):
    picks = []
    for place in range(places - 1, lowest - 1, -1):
        if forced is not None and place == forced[0]:
            picks.append(forced[1])
        elif place in free:
            picks.append(slice(None))
        else:
            picks.append(bit_of(me, place))
    return tuple(picks)


def gather_kernel(places, x_ref, out_ref, send_sem, recv_sem, own_sem):
    me = lax.axis_index("fsdp")
    peers = peers_of(me, places)
    greet(me, places)
    own = pltpu.make_async_copy(x_ref, out_ref.at[region(places, (), me)], own_sem)
    own.start()
    orders = routes(places)
    parts = row_parts(x_ref.shape[0], len(orders))
    copies = [[] for _ in orders]
    for stage in range(places):
        for n, (order, (low, size)) in enumerate(zip(orders, parts)):
            rows = pl.ds(low, size)
            place = order[stage]
            if stage == 1 and n == 0:
                own.wait()
            if stage:
                copies[n][-1].wait_recv()
            here = region(places, order[:stage], me)
            target = out_ref.at[here + (rows,)]
            copy = pltpu.make_async_remote_copy(
                src_ref=x_ref.at[rows] if stage == 0 else target,
                dst_ref=target,
                send_sem=send_sem.at[n, stage],
                recv_sem=recv_sem.at[n, stage],
                device_id=(peers[place],),
                device_id_type=pl.DeviceIdType.MESH,
            )
            copy.start()
            copies[n].append(copy)
    for group in copies:
        group[-1].wait_recv()
    for group in copies:
        for copy in group:
            copy.wait_send()


def scatter_kernel(places, g_ref, out_ref, acc, *rest):
    landings, (send_sem, recv_sem) = rest[:places], rest[places:]
    me = lax.axis_index("fsdp")
    peers = peers_of(me, places)
    greet(me, places)
    orders = [order[::-1] for order in routes(places)]
    parts = row_parts(g_ref.shape[-2], len(orders))
    everything = set(range(places))
    copies = [[None] * places for _ in orders]

    def send(n, stage):
        order, (low, size) = orders[n], parts[n]
        rows = pl.ds(low, size)
        place = order[stage]
        free = everything - set(order[: stage + 1])
        away = (place, 1 - bit_of(me, place))
        if stage == 0:
            source = g_ref.at[region(places, free, me, 0, away) + (rows,)]
        else:
            source = acc.at[region(places, free, me, 1, away) + (rows,)]
        copy = pltpu.make_async_remote_copy(
            src_ref=source,
            dst_ref=landings[stage].at[(slice(None),) * len(free) + (rows,)],
            send_sem=send_sem.at[n, stage],
            recv_sem=recv_sem.at[n, stage],
            device_id=(peers[place],),
            device_id_type=pl.DeviceIdType.MESH,
        )
        copy.start()
        copies[n][stage] = copy

    def add(n, stage):
        order, (low, size) = orders[n], parts[n]
        rows = pl.ds(low, size)
        free = sorted(everything - set(order[: stage + 1]), reverse=True)
        copies[n][stage].wait_recv()

        def one(at, carry):
            values = {}
            for spot, place in enumerate(free):
                values[place] = lax.rem(at // (1 << (len(free) - 1 - spot)), 2)
            full = tuple(
                values[place] if place in values else bit_of(me, place)
                for place in range(places - 1, -1, -1)
            )
            kept = full[:-1] + (rows,)
            landed = landings[stage][tuple(values[place] for place in free) + (rows,)]
            if stage == 0:
                acc[kept] = g_ref[full + (rows,)] + landed
            elif stage < places - 1:
                acc[kept] = acc[kept] + landed
            else:
                out_ref[rows] = acc[kept].astype(f32) + landed.astype(f32)
            return carry

        lax.fori_loop(0, 1 << len(free), one, 0)

    for n in range(len(orders)):
        send(n, 0)
    for stage in range(places):
        for n in range(len(orders)):
            add(n, stage)
            if stage < places - 1:
                send(n, stage + 1)
    for group in copies:
        for copy in group:
            copy.wait_send()


def gather_all(shard, devices):
    places = devices.bit_length() - 1
    count = len(routes(places))
    out = pl.pallas_call(
        functools.partial(gather_kernel, places),
        out_shape=shaped((2,) * places + shard.shape, shard.dtype),
        in_specs=[pl.BlockSpec(memory_space=pltpu.VMEM)],
        out_specs=pl.BlockSpec(memory_space=pltpu.VMEM),
        scratch_shapes=[
            pltpu.SemaphoreType.DMA((count, places)),
            pltpu.SemaphoreType.DMA((count, places)),
            pltpu.SemaphoreType.DMA,
        ],
        compiler_params=pltpu.CompilerParams(
            collective_id=0, has_side_effects=True, vmem_limit_bytes=60 * 1024 * 1024
        ),
    )(shard)
    return out.reshape((devices,) + shard.shape)


def scatter_all(grads, devices):
    places = devices.bit_length() - 1
    count = len(routes(places))
    tail = grads.shape[1:]
    return pl.pallas_call(
        functools.partial(scatter_kernel, places),
        out_shape=shaped(tail, f32),
        in_specs=[pl.BlockSpec(memory_space=pltpu.VMEM)],
        out_specs=pl.BlockSpec(memory_space=pltpu.VMEM),
        scratch_shapes=[pltpu.VMEM((2,) * (places - 1) + tail, bf16)]
        + [pltpu.VMEM((2,) * (places - 1 - stage) + tail, bf16) for stage in range(places)]
        + [
            pltpu.SemaphoreType.DMA((count, places)),
            pltpu.SemaphoreType.DMA((count, places)),
        ],
        compiler_params=pltpu.CompilerParams(
            collective_id=1, has_side_effects=True, vmem_limit_bytes=60 * 1024 * 1024
        ),
    )(grads.reshape((2,) * places + tail))


def run(kernel, outs, args, scratch=(), flops=0):
    size = sum(a.size * a.dtype.itemsize for a in args)
    size += sum(a.size * a.dtype.itemsize for a in outs)
    return pl.pallas_call(
        kernel,
        out_shape=tuple(outs),
        in_specs=[pl.BlockSpec(memory_space=pltpu.VMEM)] * len(args),
        out_specs=tuple([pl.BlockSpec(memory_space=pltpu.VMEM)] * len(outs)),
        scratch_shapes=list(scratch),
        compiler_params=pltpu.CompilerParams(vmem_limit_bytes=60 * 1024 * 1024),
        cost_estimate=pl.CostEstimate(flops=flops, bytes_accessed=size, transcendentals=0),
    )(*args)


def shaped(shape, dtype):
    return jax.ShapeDtypeStruct(tuple(shape), dtype)


def offset_onehot(table_rows):
    places = jnp.arange(WIN * WIN, dtype=jnp.int32)
    row_at = places // WIN
    col_at = places % WIN
    index = (row_at[:, None] - row_at[None, :] + WIN - 1) * (2 * WIN - 1) + (
        col_at[:, None] - col_at[None, :] + WIN - 1
    )
    targets = jnp.arange(table_rows, dtype=jnp.int32)
    return (index.reshape(-1)[:, None] == targets[None, :]).astype(f32)


def token_places(shift_by):
    token = jnp.arange(SIDE * SIDE, dtype=jnp.int32)
    row = (token // SIDE - shift_by) % SIDE
    col = (token % SIDE - shift_by) % SIDE
    window = (row // WIN) * (SIDE // WIN) + col // WIN
    inside = (row % WIN) * WIN + col % WIN
    if shift_by:
        edges = SIDE - WIN, SIDE - shift_by
        a_row = (row >= edges[0]).astype(jnp.int32) + (row >= edges[1]).astype(jnp.int32)
        a_col = (col >= edges[0]).astype(jnp.int32) + (col >= edges[1]).astype(jnp.int32)
        label = 3 * a_row + a_col
    else:
        label = jnp.zeros_like(token)
    mask = jnp.where(label[:, None] == label[None, :], 0.0, mask_fill)
    mask = jnp.where(window[:, None] == window[None, :], mask, outside_fill).astype(f32)
    spread = (inside[:, None] == jnp.arange(WIN * WIN)[None, :]).astype(bf16)
    return mask, spread, spread.T


def local(
    images,
    cotangent,
    counts,
    *shards,
):
    devices = lax.axis_size("fsdp")
    gather_dims = (1, 1, 1, 2, 1, 1, 1, 1, 1, 1, 1, 1, 1)
    large_at = (2, 5, 9, 11)
    small_at = (0, 1, 3, 4, 6, 7, 8, 10, 12)
    flats = [tensor.reshape(-1) for tensor in shards]
    tokens, features = images.shape[1:]
    packed = jnp.concatenate([flats[n] for n in small_at])
    small_rows = 16 * -(-packed.shape[0] // (16 * features))
    packed = jnp.pad(packed, (0, small_rows * features - packed.shape[0]))
    blocks, spans = [packed.reshape(small_rows, features)], {}
    filled = small_rows
    for layer in range(LAYERS):
        for n in large_at:
            piece = shards[n][layer]
            rows, wide = piece.shape[0], piece.shape[1] // features
            piece = piece.reshape(rows, wide, features).transpose(1, 0, 2)
            blocks.append(piece.reshape(rows * wide, features))
            spans[n, layer] = (filled, rows, wide)
            filled += rows * wide
    spare = -filled % 16
    if spare:
        blocks.append(jnp.zeros((spare, features), bf16))
    gathered = gather_all(jnp.concatenate(blocks), devices)
    packed = gathered[:, :small_rows].reshape(devices, -1)
    weights = [None] * len(shards)
    at = 0
    for n in small_at:
        shape, axis_dim = shards[n].shape, gather_dims[n]
        size = flats[n].shape[0]
        piece = packed[:, at : at + size].reshape((devices,) + shape)
        piece = jnp.moveaxis(piece, 0, axis_dim)
        full = shape[:axis_dim] + (devices * shape[axis_dim],) + shape[axis_dim + 1 :]
        weights[n] = piece.reshape(full)
        at += size
    for n in large_at:
        weights[n] = [None] * LAYERS
        for layer in range(LAYERS):
            low, rows, wide = spans[n, layer]
            piece = gathered[:, low : low + rows * wide]
            piece = piece.reshape(devices, wide, rows, features).transpose(1, 0, 2, 3)
            piece = piece.reshape(wide, devices * rows, features)
            weights[n][layer] = piece if wide > 1 else piece[0]
    table = weights[4]
    heads = table.shape[-1]
    hidden = weights[10].shape[-1]
    cells = WIN * WIN
    onehot = offset_onehot(table.shape[1])
    pairs = jnp.einsum("pt,lth->lhp", onehot.astype(bf16), table, preferred_element_type=f32)
    pairs = pairs.reshape(LAYERS, heads, cells, cells).transpose(0, 1, 3, 2).astype(bf16)
    zero = jnp.zeros((features,), f32)

    def row(n, layer):
        return weights[n][layer].astype(f32).reshape(1, -1)

    active = counts[0] > 0
    current = images[0].astype(f32)
    saved = []
    for layer in range(LAYERS):
        mask, spread, spread_t = token_places(SHIFT if layer % 2 else 0)
        bias = run(
            bias_kernel,
            [shaped((heads, tokens, tokens), f32)],
            (pairs[layer], spread, spread_t, mask),
        )[0]
        b_qv = weights[3][layer].astype(f32)
        b_qkv = jnp.concatenate([b_qv[0], zero, b_qv[1]]).reshape(1, -1)
        attn = run(
            attn_fwd_kernel,
            [
                shaped((tokens, features), f32),
                shaped((tokens, features), bf16),
                shaped((tokens, 3 * features), bf16),
                shaped((features, tokens), bf16),
                shaped((heads, tokens, tokens), f32),
                shaped((features, tokens), bf16),
            ],
            (current, row(0, layer), row(1, layer), weights[2][layer], b_qkv, bias,
             weights[5][layer], row(6, layer)),
            [pltpu.VMEM((features, tokens), bf16)],
        )
        mlp = run(
            mlp_fwd_kernel,
            [
                shaped((tokens, features), f32),
                shaped((tokens, features), bf16),
                shaped((tokens, hidden), f32),
                shaped((tokens, hidden), bf16),
            ],
            (attn[0], row(7, layer), row(8, layer), weights[9][layer], row(10, layer),
             weights[11][layer], row(12, layer)),
        )
        saved.append((current, attn, mlp, spread, spread_t))
        current = mlp[0]
    outs = jnp.where(active, current, 0.0)[None]
    grad = jnp.where(active, cotangent[0].astype(f32), 0.0)
    sums = [[None] * LAYERS for _ in shards]
    owned = [[None] * LAYERS for _ in shards]

    def scatter(value):
        return value

    for layer in reversed(range(LAYERS)):
        entry, attn, mlp, spread, spread_t = saved[layer]
        g_mid, g_w1, g_w2, *rest = run(
            mlp_bwd_kernel,
            [
                shaped((tokens, features), f32),
                shaped((hidden // features, features, features), bf16),
                shaped((hidden, features), bf16),
                shaped((1, hidden), f32),
                shaped((1, features), f32),
                shaped((1, features), f32),
                shaped((1, features), f32),
                shaped((1, features), f32),
            ],
            (grad, attn[0], row(7, layer), weights[9][layer], weights[11][layer], *mlp[1:]),
        )
        sums[10][layer], sums[12][layer], sums[7][layer], sums[8][layer], sums[6][layer] = rest
        owned[11][layer] = scatter(g_w2)
        owned[9][layer] = scatter(g_w1)
        grad, g_qkv, g_proj, g_qv, g_pairs, g_gain, g_off = run(
            attn_bwd_kernel,
            [
                shaped((tokens, features), f32),
                shaped((3, features, features), bf16),
                shaped((features, features), bf16),
                shaped((2, features), f32),
                shaped((heads, cells, cells), f32),
                shaped((1, features), f32),
                shaped((1, features), f32),
            ],
            (g_mid, entry, row(0, layer), weights[2][layer], weights[5][layer], *attn[1:],
             spread, spread_t),
            [
                pltpu.VMEM((tokens, features), bf16),
                pltpu.VMEM((features, tokens), f32),
                pltpu.VMEM((tokens, 3 * features), bf16),
            ],
        )
        owned[5][layer] = scatter(g_proj)
        owned[2][layer] = scatter(g_qkv)
        sums[0][layer], sums[1][layer], sums[3][layer] = g_gain, g_off, g_qv
        per_pair = g_pairs.transpose(0, 2, 1).reshape(heads, cells * cells)
        sums[4][layer] = jnp.dot(per_pair, onehot, precision=lax.Precision.HIGHEST).T
    parts = []
    for n in small_at:
        shape, axis_dim = shards[n].shape, gather_dims[n]
        both = jnp.stack(sums[n])
        both = both.reshape(shape[:axis_dim] + (devices,) + shape[axis_dim:])
        parts.append(jnp.moveaxis(both, axis_dim, 0).reshape(devices, -1))
    packed = jnp.concatenate(parts, axis=1).astype(bf16)
    packed = jnp.pad(packed, ((0, 0), (0, small_rows * features - packed.shape[1])))
    blocks = [packed.reshape(devices, small_rows, features)]
    for layer in range(LAYERS):
        for n in large_at:
            low, rows, wide = spans[n, layer]
            piece = owned[n][layer].reshape(wide, devices, rows, features)
            blocks.append(piece.transpose(1, 0, 2, 3).reshape(devices, rows * wide, features))
    if spare:
        blocks.append(jnp.zeros((devices, spare, features), bf16))
    reduced = scatter_all(jnp.concatenate(blocks, axis=1), devices)
    summed = reduced[:small_rows].reshape(-1)
    at = 0
    for n in small_at:
        size = flats[n].shape[0]
        owned[n] = summed[at : at + size].reshape(shards[n].shape)
        at += size
    for n in large_at:
        for layer in range(LAYERS):
            low, rows, wide = spans[n, layer]
            piece = reduced[low : low + rows * wide].reshape(wide, rows, features)
            owned[n][layer] = piece.transpose(1, 0, 2).reshape(rows, wide * features)
        owned[n] = jnp.stack(owned[n])
    return (outs, grad[None], *owned)


GATHERED = (
    (None, 0, 0, 0, 1, 'hlxy'),
    (0, 0, 0, 1, 3, 'xyhl'),
    (0, 0, 1, 2, 3, 'hlyx'),
    (0, 0, 2, 3, 3, 'hlyx'),
    (0, 1, 0, 1, 1, 'hxly'),
    (0, 2, 0, 1, 4, 'hlxy'),
    (0, 2, 1, 2, 4, 'hlyx'),
    (0, 2, 2, 3, 4, 'hlxy'),
    (0, 2, 3, 4, 4, 'hlxy'),
    (0, 3, 0, 1, 4, 'xhyl'),
    (0, 3, 1, 2, 4, 'hlxy'),
    (0, 3, 2, 4, 4, 'hlxy'),
    (1, 0, 0, 2, 3, 'hylx'),
    (1, 0, 2, 3, 3, 'yhlx'),
    (1, 1, 0, 1, 1, 'hlxy'),
    (1, 2, 0, 1, 4, 'hlyx'),
    (1, 2, 1, 2, 4, 'hlyx'),
    (1, 2, 2, 3, 4, 'yhlx'),
    (1, 2, 3, 4, 4, 'xyhl'),
    (1, 3, 0, 2, 4, 'xyhl'),
    (1, 3, 2, 4, 4, 'hxly'),
)
SCATTERED = (
    (1, 3, 0, 2, 4, 'ylxh'),
    (1, 3, 2, 4, 4, 'lxhy'),
    (1, 2, 0, 2, 4, 'xlhy'),
    (1, 2, 2, 4, 4, 'ylxh'),
    (1, 1, 0, 1, 1, 'lxyh'),
    (1, 0, 0, 1, 3, 'yxlh'),
    (0, 3, 0, 2, 4, 'xlyh'),
    (1, 0, 1, 3, 3, 'lhyx'),
    (0, 3, 2, 4, 4, 'ylxh'),
    (0, 0, 0, 2, 3, 'yxlh'),
    (0, 2, 0, 2, 4, 'yxlh'),
    (0, 2, 2, 4, 4, 'xylh'),
    (0, 1, 0, 1, 1, 'xylh'),
    (0, 0, 2, 3, 3, 'yxlh'),
    (None, 0, 0, 0, 1, 'ylxh'),
)
AGENDA = (
    (
        (0, 3, 0), (0, 5, 0), (0, 1, 0), (0, 18, 0), (0, 0, 0), (0, 19, 0),
        (0, 2, 0), (0, 13, 0), (0, 16, 0), (0, 20, 0), (0, 3, 1), (0, 4, 0),
        (0, 5, 1), (0, 1, 1), (0, 8, 0), (0, 17, 0), (0, 2, 1), (0, 19, 1),
        (0, 15, 0), (0, 0, 1), (0, 11, 0), (0, 16, 1), (0, 3, 2), (0, 9, 0),
        (0, 18, 1), (0, 12, 0), (0, 4, 1), (0, 5, 2), (0, 20, 1), (0, 2, 2),
        (0, 8, 1), (0, 6, 0), (0, 15, 1), (0, 13, 1), (0, 3, 3), (0, 16, 2),
        (0, 4, 2), (0, 0, 2), (0, 7, 0), (0, 5, 3), (0, 8, 2), (0, 6, 1),
        (0, 15, 2), (0, 10, 0), (0, 11, 1), (0, 1, 2), (0, 12, 1), (0, 2, 3),
        (0, 6, 2), (0, 4, 3), (0, 13, 2), (0, 14, 0), (0, 11, 2), (0, 7, 1),
        (0, 17, 1), (0, 10, 1), (0, 18, 2), (0, 8, 3), (0, 13, 3), (0, 7, 2),
        (0, 1, 3), (0, 9, 1), (0, 5, 4), (0, 12, 2), (0, 0, 3), (0, 3, 4),
        (0, 10, 2), (0, 14, 1),
    ),
    (
        (0, 6, 3), (0, 11, 3), (0, 8, 4), (0, 19, 2), (0, 0, 4), (0, 17, 2),
        (0, 20, 2), (0, 9, 2), (0, 16, 3), (0, 2, 4), (0, 14, 2), (0, 1, 4),
        (0, 12, 3), (0, 4, 4), (0, 7, 3),
    ),
    (
        (0, 10, 3), (0, 11, 4), (0, 13, 4),
    ),
    (
        (0, 9, 3), (0, 6, 4),
    ),
    (
        (0, 16, 4),
    ),
    (
        (0, 7, 4), (0, 18, 3), (0, 15, 3), (0, 17, 3), (0, 14, 3), (0, 20, 3),
        (0, 10, 4),
    ),
    (
        (0, 19, 3), (0, 9, 4), (0, 12, 4),
    ),
    (),
    (
        (0, 18, 4), (0, 14, 4), (0, 15, 4),
    ),
    (),
    (
        (0, 17, 4),
    ),
    (),
    (
        (0, 19, 4), (0, 20, 4),
    ),
    (),
    (
        (1, 0, 0), (1, 1, 0),
    ),
    (
        (1, 0, 1), (1, 1, 1), (1, 3, 0), (1, 2, 0),
    ),
    (
        (1, 4, 0),
    ),
    (
        (1, 3, 1), (1, 2, 1), (1, 4, 1),
    ),
    (),
    (
        (1, 7, 0), (1, 5, 0), (1, 1, 2), (1, 0, 2),
    ),
    (),
    (
        (1, 8, 0), (1, 7, 1), (1, 5, 1), (1, 4, 2),
    ),
    (
        (1, 11, 0), (1, 8, 1), (1, 2, 2), (1, 10, 0), (1, 0, 3),
    ),
    (
        (1, 11, 1), (1, 1, 3), (1, 6, 0), (1, 3, 2),
    ),
    (
        (1, 10, 1),
    ),
    (
        (1, 12, 0), (1, 4, 3), (1, 6, 1), (1, 7, 2),
    ),
    (
        (1, 9, 0), (1, 13, 0), (1, 8, 2), (1, 9, 1), (1, 2, 3), (1, 11, 2),
        (1, 5, 2),
    ),
    (
        (1, 10, 2), (1, 6, 2), (1, 14, 0), (1, 3, 3), (1, 14, 1), (1, 12, 1),
        (1, 0, 4), (1, 5, 3), (1, 3, 4), (1, 8, 3), (1, 10, 3), (1, 13, 1),
        (1, 9, 2), (1, 4, 4), (1, 1, 4), (1, 5, 4), (1, 11, 3), (1, 12, 2),
        (1, 6, 3), (1, 10, 4), (1, 14, 2), (1, 7, 3),
    ),
    (
        (1, 8, 4), (1, 13, 2), (1, 9, 3), (1, 5, 5), (1, 2, 4), (1, 11, 4),
        (1, 3, 5), (1, 12, 3), (1, 14, 3), (1, 6, 4), (1, 13, 3), (1, 9, 4),
        (1, 10, 5), (1, 7, 4), (1, 14, 4), (1, 0, 5), (1, 4, 5), (1, 1, 5),
        (1, 11, 5), (1, 12, 4), (1, 13, 4), (1, 6, 5),
    ),
    (
        (1, 9, 5), (1, 12, 5), (1, 8, 5), (1, 14, 5), (1, 2, 5), (1, 7, 5),
        (1, 13, 5),
    ),
)


def stack_rows(parts):
    return jnp.concatenate(parts, axis=0)


def permute_f32(matrix, rows):
    high = rows.astype(bf16)
    rest = rows - high.astype(f32)
    middle = rest.astype(bf16)
    low = (rest - middle.astype(f32)).astype(bf16)
    return dot_nn(matrix, high) + (dot_nn(matrix, middle) + dot_nn(matrix, low))


def slots_of(window):
    padded = -(-window // 8) * 8
    lanes_each = 64
    return padded, lanes_each


def places_in_windows(shift_by):
    token = np.arange(SIDE * SIDE)
    row = (token // SIDE - shift_by) % SIDE
    col = (token % SIDE - shift_by) % SIDE
    window = (row // WIN) * (SIDE // WIN) + col // WIN
    inside = (row % WIN) * WIN + col % WIN
    edges = SIDE - WIN, SIDE - shift_by
    a_row = (row >= edges[0]).astype(int) + (row >= edges[1]).astype(int)
    a_col = (col >= edges[0]).astype(int) + (col >= edges[1]).astype(int)
    return window, inside, 3 * a_row + a_col


def constants(heads, per_device_rows, devices):
    cells = WIN * WIN
    padded, wide = slots_of(cells)
    windows = (SIDE // WIN) ** 2
    tokens = SIDE * SIDE
    total = windows * padded
    perms = []
    for shift_by in (0, SHIFT):
        window, inside, label = places_in_windows(shift_by)
        perm = np.zeros((total, tokens), np.float32)
        perm[window * padded + inside, np.arange(tokens)] = 1.0
        perms.append(perm)
    mask = np.zeros((windows, padded, wide), np.float32)
    labels = np.zeros((windows, cells), int)
    labels[window, inside] = label
    mask[:, :cells, :cells] = np.where(labels[:, :, None] == labels[:, None, :], 0.0, mask_fill)
    group = 2 * lanes // wide
    mask = np.tile(mask, (1, 1, group))
    span = 2 * WIN - 1
    strips = -(-span * WIN // 16) * 16
    onehot = np.zeros((WIN, strips, devices * 8), np.float32)
    for c_q in range(WIN):
        for d_r in range(span):
            for c_k in range(WIN):
                t = d_r * span + c_q - c_k + WIN - 1
                spot = (t // per_device_rows) * 8 + t % per_device_rows
                onehot[c_q, (span - 1 - d_r) * WIN + c_k, spot] = 1.0
    onehot = onehot.reshape(WIN * strips, devices * 8)
    query = np.arange(heads * wide) % wide
    head = np.arange(heads * wide) // wide
    lane_row = np.where(query < cells, query // WIN, -1)
    lane_col = np.where(query < cells, query % WIN, -1)
    lane_of = np.zeros((8, heads * wide), np.int32)
    lane_of[0], lane_of[1] = lane_row, lane_col
    expand = np.zeros((lanes, heads * wide), np.float32)
    expand[head, np.arange(heads * wide)] = 1.0
    collect = np.zeros((heads * wide, lanes), np.float32)
    real = query < cells
    collect[np.arange(heads * wide)[real], (lane_col * heads + head)[real]] = 1.0
    fold = np.zeros((lanes, lanes), np.float32)
    for lane in range(WIN * heads):
        fold[lane, lane % heads] = 1.0
    plain, shifted = perms
    low = [plain, shifted, shifted @ plain.T, plain @ shifted.T, plain.T, shifted.T,
           onehot, onehot.T, expand, collect, fold]
    return [jnp.asarray(a, bf16) for a in low] + [jnp.asarray(lane_of), jnp.asarray(mask)]


AXES = "hlyxc"


class Links:
    def __init__(self, sems):
        me = lax.axis_index("fsdp")
        self.me = me
        self.own, self.peer = {}, {}
        for place, axis in enumerate(reversed(AXES)):
            bit = bit_of(me, place)
            self.own[axis] = bit
            self.peer[axis] = me + (1 - 2 * bit) * (1 << place)
        self.sems = sems
        self.copies = {}

    def greet(self):
        barrier = pltpu.get_barrier_semaphore()
        for axis in AXES:
            pl.semaphore_signal(
                barrier, inc=1, device_id=(self.peer[axis],), device_id_type=pl.DeviceIdType.MESH
            )

    def greeted(self):
        pl.semaphore_wait(pltpu.get_barrier_semaphore(), len(AXES))

    def send(self, key, way, source, target, axis):
        send_sem, recv_sem = self.sems[way]
        copy = pltpu.make_async_remote_copy(
            src_ref=source,
            dst_ref=target,
            send_sem=send_sem.at[key[1], key[0]],
            recv_sem=recv_sem.at[key[1], key[0]],
            device_id=(self.peer[axis],),
            device_id_type=pl.DeviceIdType.MESH,
        )
        copy.start()
        self.copies[(way,) + key] = copy

    def arrive(self, way, key):
        self.copies[(way,) + key].wait_recv()

    def finish(self):
        for copy in self.copies.values():
            copy.wait_send()


def all_kernel(
    gspans, rspans, agenda,
    count_ref, x_ref, cot_ref, again_ref, aoff_ref, wqkv_ref, bqv_ref, rel_ref, wproj_ref, bproj_ref,
    mgain_ref, moff_ref, w1_ref, b1_ref, w2_ref, b2_ref,
    plain_ref, shifted_ref, forth_ref, back_ref, plain_t_ref, shifted_t_ref,
    onehot_ref, onehot_t_ref, expand_ref, collect_ref, fold_ref, lane_ref, mask_ref,
    out_ref, gin_ref, gagain_ref, gaoff_ref, gwqkv_ref, gbqv_ref, grel_ref, gwproj_ref, gbproj_ref,
    gmgain_ref, gmoff_ref, gw1_ref, gb1_ref, gw2_ref, gb2_ref,
    w, g, land_0, land_1, land_2, land_3, land_4, sm, sg, sland_0, sland_1, sland_2, sland_3, sland_4,
    xs, xn_s, qkv_s, probs_s, mixed_s, mid_s, yn_s, slope_s, act_s,
    bias_s, strip_s, kinds_s, b1_s, own_s, mixf_s, dmix_s, dqkv_s, dsum_s, kg_s, b1g_s, rg_s,
    gs_send, gs_recv, rs_send, rs_recv,
):
    links = Links({"g": (gs_send, gs_recv), "r": (rs_send, rs_recv)})
    me = links.me
    every = slice(None)
    home = tuple(links.own[axis] for axis in AXES)
    devices = 1 << len(AXES)
    lands = ((land_0, sland_0), (land_1, sland_1), (land_2, sland_2), (land_3, sland_3), (land_4, sland_4))
    rows_each = wqkv_ref.shape[1]
    features = wproj_ref.shape[2]
    hidden = w1_ref.shape[2]
    parts = wqkv_ref.shape[2] // features
    wide_parts = hidden // features
    deep = w2_ref.shape[1]
    table_each = rel_ref.shape[0]
    heads = rel_ref.shape[2]
    size = features // heads
    scaling = size ** (-0.5)
    at_proj = parts * rows_each
    at_one = at_proj + rows_each
    at_two = at_one + wide_parts * rows_each
    cells = WIN * WIN
    padded, wide = slots_of(cells)
    windows = (SIDE // WIN) ** 2
    per = lanes // size
    group_lanes = per * wide
    share = features // devices
    pack = lanes // share
    share_one = hidden // devices
    pack_one = lanes // share_one
    span = 2 * WIN - 1
    strips = -(-span * WIN // 16) * 16

    links.greet()
    own_s[...] = jnp.zeros_like(own_s)
    at = 0
    for ref in (again_ref, aoff_ref, bqv_ref, bproj_ref, mgain_ref, moff_ref, b2_ref):
        piece = ref[...].astype(f32)
        if ref.shape[0] == LAYERS and len(ref.shape) == 3:
            for layer in range(LAYERS):
                own_s[at : at + ref.shape[1], 0:share] = piece[layer]
                at += ref.shape[1]
        else:
            own_s[at : at + LAYERS, 0:share] = piece
            at += LAYERS
    row_at = lax.broadcasted_iota(jnp.int32, (lanes, lanes), 0)
    lane_at = lax.broadcasted_iota(jnp.int32, (lanes, lanes), 1)
    spot = share * lax.rem(me, pack)
    place = jnp.where((lane_at == row_at + spot) & (row_at < share), 1.0, 0.0).astype(bf16)
    kinds = dot_nn(own_s[...].astype(bf16), place)
    spot = share_one * lax.rem(me, pack_one)
    place = jnp.where((lane_at == row_at + spot) & (row_at < share_one), 1.0, 0.0).astype(bf16)
    own_s[...] = jnp.zeros_like(own_s)
    own_s[0:LAYERS, 0:share_one] = b1_ref[...].astype(f32)
    firsts = dot_nn(own_s[...].astype(bf16), place)
    own_s[...] = jnp.zeros_like(own_s)
    tables = rel_ref[...].astype(f32)
    for layer in range(LAYERS):
        own_s[layer * 8 : layer * 8 + table_each, 0:heads] = tables[:, layer, :]
        own_s[layer * 8 + table_each : layer * 8 + table_each + 1, :] = firsts[layer : layer + 1]
    sm[home + (every, slice(0, lanes))] = kinds.astype(bf16)
    sm[home + (every, slice(lanes, 2 * lanes))] = own_s[...].astype(bf16)
    for layer in range(LAYERS):
        for part in range(parts):
            w[(layer,) + home + (pl.ds(part * rows_each, rows_each), every)] = (
                wqkv_ref[layer, :, part * features : (part + 1) * features]
            )
        w[(layer,) + home + (pl.ds(at_proj, rows_each), every)] = wproj_ref[layer]
        for part in range(wide_parts):
            w[(layer,) + home + (pl.ds(at_one + part * rows_each, rows_each), every)] = (
                w1_ref[layer, :, part * features : (part + 1) * features]
            )
        w[(layer,) + home + (pl.ds(at_two, deep), every)] = w2_ref[layer]

    def view(where, span, picks):
        big, small = where
        layer, low, count, _ = span
        if layer is None:
            return small.at[picks]
        return big.at[(layer,) + picks + (pl.ds(low, count),)]

    def gather(n, stage):
        span = gspans[n]
        route = span[3] + AXES[-1]
        if stage:
            links.arrive("g", (stage - 1, n))
        got = route[:stage]
        ref = view((w, sm), span, tuple(every if a in got else links.own[a] for a in AXES))
        links.send((stage, n), "g", ref, ref, route[stage])

    def merge(n, stage):
        span = rspans[n]
        closed = (AXES[-1] + span[3])[: stage + 1]
        opened = [axis for axis in AXES if axis not in closed]

        fixed = min(2, len(opened))

        def one(at, carry):
            for inner in range(1 << fixed):
                bits = {
                    axis: (inner >> k) % 2 if k < fixed else bit_of(at, k - fixed)
                    for k, axis in enumerate(reversed(opened))
                }
                here = view((g, sg), span, tuple(bits.get(a, links.own[a]) for a in AXES))
                there = view(lands[stage], span, tuple(bits[a] for a in opened))
                here[...] = here[...] + there[...]
            return carry

        if len(opened) == fixed:
            one(0, 0)
        else:
            lax.fori_loop(0, 1 << (len(opened) - fixed), one, 0)

    def scatter(n, stage):
        span = rspans[n]
        layer, low, count, _ = span
        order = AXES[-1] + span[3]
        if stage:
            links.arrive("r", (stage - 1, n))
        if stage < len(AXES):
            if stage:
                merge(n, stage - 1)
            axis, closed = order[stage], order[:stage]
            where = {a: links.own[a] if a in closed else every for a in AXES}
            where[axis] = 1 - links.own[axis]
            source = view((g, sg), span, tuple(where[a] for a in AXES))
            target = view(lands[stage], span, (every,) * (len(AXES) - 1 - stage))
            links.send((stage, n), "r", source, target, axis)
            return
        if layer is None:
            small_out(sg[home].astype(f32) + sland_4[...].astype(f32))
            return
        for unit in range(low, low + count, rows_each):
            rows = pl.ds(unit, rows_each)
            total = g[(layer,) + home + (rows,)].astype(f32) + land_4[layer, rows, :].astype(f32)
            if unit < at_proj:
                part = unit // rows_each
                gwqkv_ref[layer, :, part * features : (part + 1) * features] = total
            elif unit < at_one:
                gwproj_ref[layer] = total
            elif unit < at_two:
                part = (unit - at_one) // rows_each
                gw1_ref[layer, :, part * features : (part + 1) * features] = total
            else:
                gw2_ref[layer, unit - at_two : unit - at_two + rows_each, :] = total

    def small_out(total):
        picked = jnp.where(lax.broadcasted_iota(jnp.int32, (16, lanes), 1) // share == lax.rem(me, pack),
                           total[:, 0:lanes], 0.0)
        folded = picked[:, 0:share]
        for n in range(1, pack):
            folded = folded + picked[:, n * share : (n + 1) * share]
        at = 0
        for ref in (gagain_ref, gaoff_ref, gbqv_ref, gbproj_ref, gmgain_ref, gmoff_ref, gb2_ref):
            if len(ref.shape) == 3:
                for layer in range(LAYERS):
                    ref[layer] = folded[at : at + ref.shape[1]]
                    at += ref.shape[1]
            else:
                ref[...] = folded[at : at + LAYERS]
                at += LAYERS
        tail = total[:, lanes : 2 * lanes]
        for layer in range(LAYERS):
            grel_ref[layer] = tail[layer * 8 : layer * 8 + table_each, 0:heads]
            row = tail[layer * 8 + table_each : layer * 8 + table_each + 1]
            keep = lax.broadcasted_iota(jnp.int32, (1, lanes), 1) // share_one
            row = jnp.where(keep == lax.rem(me, pack_one), row, 0.0)
            folded_row = row[:, 0:share_one]
            for n in range(1, pack_one):
                folded_row = folded_row + row[:, n * share_one : (n + 1) * share_one]
            gb1_ref[layer : layer + 1, :] = folded_row

    def qkv_part(layer, part):
        block = w[layer, :, :, :, :, :, part * rows_each : (part + 1) * rows_each, :]
        return block.reshape(features, features)

    def proj_of(layer):
        return w[layer, :, :, :, :, :, at_proj : at_proj + rows_each, :].reshape(features, features)

    def one_of(layer, part):
        low = at_one + part * rows_each
        return w[layer, :, :, :, :, :, low : low + rows_each, :].reshape(features, features)

    def two_of(layer, part):
        return w[layer, part // 2, part % 2, :, :, :, at_two : at_two + deep, :].reshape(features, features)

    def put(layer, low, value):
        g[layer, :, :, :, :, :, low : low + rows_each, :] = value.astype(bf16).reshape(
            2, 2, 2, 2, 2, rows_each, features
        )

    agenda = list(agenda)

    def go():
        for way, n, stage in agenda.pop(0):
            (gather if way == 0 else scatter)(n, stage)

    def have(layer, low, high):
        for n, span in enumerate(gspans):
            if span[0] == layer and (layer is None or low <= span[1] < high):
                links.arrive("g", (4, n))

    links.greeted()
    go()

    stream = dot_nn(plain_ref[...], x_ref[0])
    xs[0] = stream
    qkv_s[:, :, 48:64, :] = jnp.zeros((LAYERS, windows, 16, parts * features), bf16)
    dmix_s[:, 48:64, :] = jnp.zeros((windows, 16, features), bf16)
    strip_s[...] = jnp.zeros_like(strip_s)

    go()
    have(None, 0, 0)
    small = sm[...].reshape(devices, 16, 2 * lanes).astype(f32)
    for tile in range(features // lanes):
        block = small[tile * pack : (tile + 1) * pack, :, 0:lanes]
        kinds_s[:, tile * lanes : (tile + 1) * lanes] = jnp.sum(block, axis=0)
    for tile in range(hidden // lanes):
        total = small[tile * pack_one, :, lanes : 2 * lanes]
        for n in range(1, pack_one):
            total = total + small[tile * pack_one + n, :, lanes : 2 * lanes]
        for layer in range(LAYERS):
            at = layer * 8 + table_each
            b1_s[layer : layer + 1, tile * lanes : (tile + 1) * lanes] = total[at : at + 1]

    def kind(n):
        return kinds_s[n : n + 1, :]

    lane_row = lane_ref[0:1, :]
    lane_col = lane_ref[1:2, :]
    for layer in range(LAYERS):
        table = small[:, layer * 8 : (layer + 1) * 8, lanes : 2 * lanes]
        table = table.reshape(devices * 8, lanes).astype(bf16)
        spread = dot_nn(table, expand_ref[...]).astype(bf16)
        strip = jnp.zeros((strips, heads * wide), f32)
        for col in range(WIN):
            found = dot_nn(onehot_ref[col * strips : (col + 1) * strips, :], spread)
            strip = jnp.where(lane_col == col, found, strip)
        strip_s[0:strips, :] = strip
        bias = jnp.zeros((padded, heads * wide), f32)
        for row in range(WIN):
            low = (WIN - 1 - row) * WIN
            bias = jnp.where(lane_row == row, strip_s[low : low + padded, :], bias)
        key_at = lax.broadcasted_iota(jnp.int32, (padded, heads * wide), 0)
        bias_s[layer] = jnp.where(key_at < cells, bias, outside_fill)

    keeps = [head_mask(one, size) for one in range(per)]

    def diagonal(block):
        return stack_rows([block * keep for keep in keeps])

    def undiagonal(block):
        total = block[0:padded] * keeps[0].astype(f32)
        for n in range(1, per):
            total = total + block[n * wide : n * wide + padded] * keeps[n].astype(f32)
        return total

    def both_halves(group):
        groups = heads // per
        go()
        lax.fori_loop(0, groups // 2, group, 0)
        go()
        lax.fori_loop(groups // 2, groups, group, 0)

    def attention_forward(layer):
        rows = xs[layer]
        go()
        have(layer, 0, at_proj)
        unit, _ = normalize(rows)
        xn = (unit * kind(layer) + kind(LAYERS + layer)).astype(bf16)
        xn_s[layer] = xn
        for part in range(parts):
            block = dot_nn(xn, qkv_part(layer, part))
            if part != 1:
                block = block + kind(2 * LAYERS + 2 * layer + part // 2)
            for window in range(windows):
                qkv_s[layer, window, 0:padded, part * features : (part + 1) * features] = (
                    block[window * padded : (window + 1) * padded].astype(bf16)
                )

        def group(n, carry):
            start = pl.multiple_of(n * lanes, lanes)
            bias = bias_s[layer, :, pl.ds(pl.multiple_of(n * group_lanes, lanes), group_lanes)]
            for window in range(windows):
                query = qkv_s[layer, window, :, pl.ds(start, lanes)]
                key = qkv_s[layer, window, 0:padded, pl.ds(pl.multiple_of(features + start, lanes), lanes)]
                value = qkv_s[layer, window, 0:padded, pl.ds(pl.multiple_of(2 * features + start, lanes), lanes)]
                scores = dot_nt(key, diagonal(query)) * scaling + bias
                if layer % 2:
                    scores = scores + mask_ref[window]
                raised = jnp.exp(scores - jnp.max(scores, axis=0, keepdims=True))
                probs = raised * (1.0 / jnp.sum(raised, axis=0, keepdims=True))
                probs_s[layer, n, window] = probs
                mixed = undiagonal(dot_tn(probs.astype(bf16), value))
                mixf_s[window * padded : (window + 1) * padded, pl.ds(start, lanes)] = mixed
            return carry

        both_halves(group)
        go()
        have(layer, at_proj, at_one)
        mixed = mixf_s[...].astype(bf16)
        mixed_s[layer] = mixed
        mid_s[layer] = rows + dot_nn(mixed, proj_of(layer)) + kind(4 * LAYERS + layer)

    def mlp_forward(layer):
        go()
        have(layer, at_one, at_two)
        middle = mid_s[layer]
        unit, _ = normalize(middle)
        yn = (unit * kind(5 * LAYERS + layer) + kind(6 * LAYERS + layer)).astype(bf16)
        yn_s[layer] = yn
        for part in range(wide_parts):
            cols = slice(part * features, (part + 1) * features)
            pre = dot_nn(yn, one_of(layer, part)) + b1_s[layer : layer + 1, cols]
            cumul = 0.5 * (1.0 + lax.erf(pre * half_root))
            slope_s[layer, :, cols] = cumul + pre * (jnp.exp(-0.5 * pre * pre) * inv_root_tau)
            act_s[layer, :, cols] = (pre * cumul).astype(bf16)

    def mlp_rest(layer):
        total = mid_s[layer] + kind(7 * LAYERS + layer)
        for part in range(wide_parts):
            cols = slice(part * features, (part + 1) * features)
            total = total + dot_nn(act_s[layer, :, cols], two_of(layer, part))
        return total

    attention_forward(0)
    mlp_forward(0)
    go()
    have(0, at_two, at_two + deep)
    xs[1] = permute_f32(forth_ref[...], mlp_rest(0))
    attention_forward(1)
    mlp_forward(1)
    active = count_ref[0] > 0

    def mlp_backward(layer, grad):
        low = grad.astype(bf16)
        kg_s[7 * LAYERS + layer : 7 * LAYERS + layer + 1, :] = jnp.sum(grad, axis=0, keepdims=True)
        go()
        for part in range(wide_parts):
            cols = slice(part * features, (part + 1) * features)
            g[layer, part // 2, part % 2, :, :, :, at_two : at_two + deep, :] = (
                dot_tn(act_s[layer, :, cols], low).astype(bf16).reshape(2, 2, 2, deep, features)
            )
        go()
        if layer == LAYERS - 1:
            have(layer, at_two, at_two + deep)
        yn = yn_s[layer]
        g_yn = jnp.zeros_like(grad)
        for part in range(wide_parts):
            cols = slice(part * features, (part + 1) * features)
            g_pre = dot_nt(low, two_of(layer, part)) * slope_s[layer, :, cols]
            b1g_s[layer : layer + 1, cols] = jnp.sum(g_pre, axis=0, keepdims=True)
            pre_low = g_pre.astype(bf16)
            put(layer, at_one + part * rows_each, dot_tn(yn, pre_low))
            g_yn = g_yn + dot_nt(pre_low, one_of(layer, part))
        back, g_gain, g_off = norm_pull(mid_s[layer], kind(5 * LAYERS + layer), g_yn)
        kg_s[5 * LAYERS + layer : 5 * LAYERS + layer + 1, :] = g_gain
        kg_s[6 * LAYERS + layer : 6 * LAYERS + layer + 1, :] = g_off
        g_mid = grad + back
        kg_s[4 * LAYERS + layer : 4 * LAYERS + layer + 1, :] = jnp.sum(g_mid, axis=0, keepdims=True)
        return g_mid

    def attention_backward(layer, g_mid):
        go()
        low = g_mid.astype(bf16)
        put(layer, at_proj, dot_tn(mixed_s[layer], low))
        d_mix = dot_nt(low, proj_of(layer))
        for window in range(windows):
            dmix_s[window, 0:padded, :] = d_mix[window * padded : (window + 1) * padded].astype(bf16)

        def group(n, carry):
            start = pl.multiple_of(n * lanes, lanes)
            k_at = pl.multiple_of(features + start, lanes)
            v_at = pl.multiple_of(2 * features + start, lanes)
            total = jnp.zeros((padded, group_lanes), f32)
            for window in range(windows):
                here = slice(window * padded, (window + 1) * padded)
                query = diagonal(qkv_s[layer, window, :, pl.ds(start, lanes)])
                key = qkv_s[layer, window, 0:padded, pl.ds(k_at, lanes)]
                value = qkv_s[layer, window, 0:padded, pl.ds(v_at, lanes)]
                d_out = diagonal(dmix_s[window, :, pl.ds(start, lanes)])
                probs = probs_s[layer, n, window]
                d_probs = dot_nt(value, d_out)
                dqkv_s[here, pl.ds(v_at, lanes)] = dot_nn(probs.astype(bf16), d_out)
                weighed = probs * d_probs
                d_scores = weighed - probs * jnp.sum(weighed, axis=0, keepdims=True)
                total = total + d_scores
                scores_low = d_scores.astype(bf16)
                dqkv_s[here, pl.ds(k_at, lanes)] = dot_nn(scores_low, query) * scaling
                dqkv_s[here, pl.ds(start, lanes)] = undiagonal(dot_tn(scores_low, key)) * scaling
            dsum_s[:, pl.ds(pl.multiple_of(n * group_lanes, lanes), group_lanes)] = total
            return carry

        both_halves(group)
        go()
        for n, part in ((0, 0), (1, 2)):
            column = jnp.sum(dqkv_s[:, part * features : (part + 1) * features], axis=0, keepdims=True)
            at = 2 * LAYERS + 2 * layer + n
            kg_s[at : at + 1, :] = column
        xn = xn_s[layer]
        g_xn = jnp.zeros_like(g_mid)
        for part in range(parts):
            block = dqkv_s[:, part * features : (part + 1) * features].astype(bf16)
            put(layer, part * rows_each, dot_tn(xn, block))
            g_xn = g_xn + dot_nt(block, qkv_part(layer, part))
        go()
        back, g_gain, g_off = norm_pull(xs[layer], kind(layer), g_xn)
        kg_s[layer : layer + 1, :] = g_gain
        kg_s[LAYERS + layer : LAYERS + layer + 1, :] = g_off
        strip_s[...] = jnp.zeros_like(strip_s)
        for row in range(WIN):
            at = (WIN - 1 - row) * WIN
            strip_s[at : at + padded, :] = strip_s[at : at + padded, :] + jnp.where(
                lane_row == row, dsum_s[...], 0.0
            )
        by_col = dot_nn(strip_s[0:strips, :].astype(bf16), collect_ref[...])
        col_at = lax.broadcasted_iota(jnp.int32, (1, lanes), 1) // heads
        stacked = stack_rows([jnp.where(col_at == col, by_col, 0.0).astype(bf16) for col in range(WIN)])
        table = dot_nn(onehot_t_ref[...], stacked)
        high = table.astype(bf16)
        rest = (table - high.astype(f32)).astype(bf16)
        table = dot_nn(high, fold_ref[...]) + dot_nn(rest, fold_ref[...])
        rg_s[:, layer * 8 : (layer + 1) * 8, :] = table.reshape(devices, 8, lanes)
        return g_mid + back

    grad = jnp.where(active, dot_nn(shifted_ref[...], cot_ref[0]), 0.0)
    g_x = attention_backward(1, mlp_backward(1, grad))
    grad = permute_f32(back_ref[...], g_x)
    g_x = attention_backward(0, mlp_backward(0, grad))
    for tile in range(hidden // lanes):
        for n in range(pack_one):
            for layer in range(LAYERS):
                at = layer * 8 + table_each
                rg_s[tile * pack_one + n, at : at + 1, :] = (
                    b1g_s[layer : layer + 1, tile * lanes : (tile + 1) * lanes]
                )
    for tile in range(features // lanes):
        block = kg_s[:, tile * lanes : (tile + 1) * lanes].astype(bf16)
        for n in range(pack):
            device = tile * pack + n
            sg[device // 16, (device // 8) % 2, (device // 4) % 2, (device // 2) % 2, device % 2, :, 0:lanes] = block
    sg[:, :, :, :, :, :, lanes : 2 * lanes] = rg_s[...].astype(bf16).reshape(2, 2, 2, 2, 2, 16, lanes)
    go()
    gin_ref[0] = permute_f32(plain_t_ref[...], g_x)
    go()
    out_ref[0] = jnp.where(active, permute_f32(shifted_t_ref[...], mlp_rest(1)), 0.0)
    go()
    links.finish()


def finish_kernel(*refs):
    count = len(refs) // 2
    for n, (source, target) in enumerate(zip(refs[:count], refs[count:])):
        if n < 2:
            target[...] = source[0][:, None, :]
        elif n == 6:
            for layer in range(LAYERS):
                target[:, layer, :] = source[layer]
        else:
            target[...] = source[...]


def whole(devices):
    def local(images, cotangent, counts, *shards):
        twos = (2,) * len(AXES)
        rows_each, features = shards[5].shape[1:]
        hidden = shards[9].shape[2]
        deep = shards[11].shape[1]
        parts, wide_parts = shards[2].shape[2] // features, hidden // features
        heads = shards[4].shape[2]
        cells = WIN * WIN
        padded, wide = slots_of(cells)
        windows = (SIDE // WIN) ** 2
        total = windows * padded
        tokens = images.shape[1]
        at_one = (parts + 1) * rows_each
        at_two = at_one + wide_parts * rows_each
        depth = at_two + deep
        edges = (0, parts * rows_each, at_one, at_two, depth)

        def spans_of(pieces):
            spans = []
            for layer, part, start, stop, of, route in pieces:
                if layer is None:
                    spans.append((None, 0, 0, route))
                    continue
                rows = edges[part + 1] - edges[part]
                low = edges[part] + rows * start // of
                spans.append((layer, low, edges[part] + rows * stop // of - low, route))
            return tuple(spans)

        gspans, rspans = spans_of(GATHERED), spans_of(SCATTERED)
        consts = constants(heads, shards[4].shape[1], devices)
        held = list(shards)
        held[4] = jnp.transpose(held[4], (1, 0, 2))
        args = [counts, images, cotangent, *held, *consts]
        outs = [shaped(images.shape, f32), shaped(images.shape, f32)]
        outs += [shaped(s.shape, f32) for s in shards]
        vmem = pltpu.VMEM
        strips = -(-(2 * WIN - 1) * WIN // 16) * 16
        tall = (WIN - 1) * WIN + padded
        tall = max(-(-tall // 8) * 8, strips)
        scratch = [
            *[vmem((LAYERS,) + twos + (depth, features), bf16)] * 2,
            *[vmem((LAYERS,) + twos[n:] + (depth, features), bf16) for n in range(1, len(AXES) + 1)],
            *[vmem(twos + (16, 2 * lanes), bf16)] * 2,
            *[vmem(twos[n:] + (16, 2 * lanes), bf16) for n in range(1, len(AXES) + 1)],
            vmem((LAYERS, total, features), f32),
            vmem((LAYERS, total, features), bf16),
            vmem((LAYERS, windows, wide, parts * features), bf16),
            vmem((LAYERS, heads * wide // (2 * lanes), windows, padded, 2 * lanes), f32),
            vmem((LAYERS, total, features), bf16),
            vmem((LAYERS, total, features), f32),
            vmem((LAYERS, total, features), bf16),
            vmem((LAYERS, total, hidden), f32),
            vmem((LAYERS, total, hidden), bf16),
            vmem((LAYERS, padded, heads * wide), f32),
            vmem((tall, heads * wide), f32),
            vmem((16, features), f32),
            vmem((8, hidden), f32),
            vmem((16, lanes), f32),
            vmem((total, features), f32),
            vmem((windows, wide, features), bf16),
            vmem((total, parts * features), f32),
            vmem((padded, heads * wide), f32),
            vmem((16, features), f32),
            vmem((8, hidden), f32),
            vmem((devices, 16, lanes), f32),
        ]
        scratch += [pltpu.SemaphoreType.DMA((len(gspans), len(AXES)))] * 2
        scratch += [pltpu.SemaphoreType.DMA((len(rspans), len(AXES)))] * 2
        space = pl.BlockSpec(memory_space=pltpu.VMEM)
        results = pl.pallas_call(
            functools.partial(all_kernel, gspans, rspans, AGENDA),
            out_shape=tuple(outs),
            in_specs=[pl.BlockSpec(memory_space=pltpu.SMEM)] + [space] * (len(args) - 1),
            out_specs=tuple([space] * len(outs)),
            scratch_shapes=scratch,
            compiler_params=pltpu.CompilerParams(
                collective_id=2, has_side_effects=True, vmem_limit_bytes=63 * 1024 * 1024
            ),
        )(*args)
        shapes = [r.shape for r in results]
        for n in (0, 1):
            shapes[n] = (tokens, 1, features)
        shapes[6] = (shapes[6][1], LAYERS, shapes[6][2])
        results = pl.pallas_call(
            finish_kernel,
            out_shape=tuple(shaped(s, f32) for s in shapes),
            in_specs=[space] * len(shapes),
            out_specs=tuple([space] * len(shapes)),
        )(*results)
        results = list(results)
        for n in (0, 1, 6):
            results[n] = jnp.transpose(results[n], (1, 0, 2))
        return tuple(results)

    return local


def fits_whole(devices, sizes):
    features, hidden, heads, table_rows, wide = sizes
    if devices != 1 << len(AXES) or features % devices or hidden % devices or table_rows % devices:
        return False
    rows_each, share_one, table_each = features // devices, hidden // devices, table_rows // devices
    return (
        rows_each % 16 == 0
        and lanes % rows_each == 0
        and lanes % share_one == 0
        and table_each <= 7
        and hidden * 8 == features * devices
        and lanes * heads == 4 * features
        and WIN * heads <= lanes
        and LAYERS == 2
        and share_one % (4 * 16) == 0
        and wide == 3 * features
    )


def solution(mesh):
    in_specs = (
        P("fsdp", None, None),
        P("fsdp", None, None),
        P("fsdp"),
        P(None, "fsdp"),
        P(None, "fsdp"),
        P(None, "fsdp", None),
        P(None, None, "fsdp"),
        P(None, "fsdp", None),
        P(None, "fsdp", None),
        P(None, "fsdp"),
        P(None, "fsdp"),
        P(None, "fsdp"),
        P(None, "fsdp", None),
        P(None, "fsdp"),
        P(None, "fsdp", None),
        P(None, "fsdp"),
    )
    out_specs = (
        P("fsdp", None, None),
        P("fsdp", None, None),
        P(None, "fsdp"),
        P(None, "fsdp"),
        P(None, "fsdp", None),
        P(None, None, "fsdp"),
        P(None, "fsdp", None),
        P(None, "fsdp", None),
        P(None, "fsdp"),
        P(None, "fsdp"),
        P(None, "fsdp"),
        P(None, "fsdp", None),
        P(None, "fsdp"),
        P(None, "fsdp", None),
        P(None, "fsdp"),
    )
    devices = mesh.shape["fsdp"]

    def step(images, cotangent, counts, *params):
        hidden, (_, table_rows, heads) = params[9].shape[2], params[4].shape
        sizes = (images.shape[2], hidden, heads, table_rows, params[2].shape[2])
        body = whole(devices) if fits_whole(devices, sizes) else local
        return jax.shard_map(
            body, mesh=mesh, in_specs=in_specs, out_specs=out_specs, check_vma=False
        )(images, cotangent, counts, *params)

    return step
```

```python
import functools

import jax
import jax.numpy as jnp
import numpy as np
from jax import lax
from jax.experimental import pallas as pl
from jax.experimental.pallas import tpu as pltpu
from jax.sharding import PartitionSpec as P

WIN = 7
SIDE = 14
LAYERS = 2
SHIFT = 3

norm_eps = 1e-05
mask_fill = -10000.0
outside_fill = -1e30
half_root = 0.7071067811865476
inv_root_tau = 0.3989422804014327
lanes = 128
bf16 = jnp.bfloat16
f32 = jnp.float32


def dot_nn(left, right):
    return lax.dot_general(left, right, (((1,), (0,)), ((), ())), preferred_element_type=f32)


def dot_nt(left, right):
    return lax.dot_general(left, right, (((1,), (1,)), ((), ())), preferred_element_type=f32)


def dot_tn(left, right):
    return lax.dot_general(left, right, (((0,), (0,)), ((), ())), preferred_element_type=f32)


def normalize(rows):
    centred = rows - jnp.mean(rows, axis=-1, keepdims=True)
    spread = jnp.mean(centred * centred, axis=-1, keepdims=True)
    inverse = lax.rsqrt(spread + norm_eps)
    return centred * inverse, inverse


def norm_pull(rows, gain, grad):
    unit, inverse = normalize(rows)
    g_gain = jnp.sum(grad * unit, axis=0, keepdims=True)
    g_bias = jnp.sum(grad, axis=0, keepdims=True)
    scaled = grad * gain
    back = inverse * (
        scaled
        - jnp.mean(scaled, axis=-1, keepdims=True)
        - unit * jnp.mean(scaled * unit, axis=-1, keepdims=True)
    )
    return back, g_gain, g_bias


def head_mask(local_head, head_size):
    lane = lax.broadcasted_iota(jnp.int32, (1, lanes), 1)
    return jnp.where(lane // head_size == local_head, 1.0, 0.0).astype(bf16)


def bias_kernel(pairs_ref, spread_ref, spread_t_ref, mask_ref, out_ref):
    def step(head, carry):
        rows = dot_nn(spread_ref[...], pairs_ref[head]).astype(bf16)
        out_ref[head] = dot_nn(rows, spread_t_ref[...]) + mask_ref[...]
        return carry

    lax.fori_loop(0, pairs_ref.shape[0], step, 0)


def attn_fwd_kernel(
    x_ref, gain_ref, off_ref, wqkv_ref, bqkv_ref, bias_ref, wproj_ref, bproj_ref,
    mid_ref, xn_ref, qkv_ref, key_t_ref, probs_ref, mixed_t_ref,
    val_t,
):
    rows = x_ref[...]
    features = rows.shape[1]
    heads = bias_ref.shape[0]
    size = features // heads
    scaling = size ** (-0.5)
    unit, _ = normalize(rows)
    xn = (unit * gain_ref[...] + off_ref[...]).astype(bf16)
    xn_ref[...] = xn
    for part in range(3):
        cols = pl.ds(part * features, features)
        block = dot_nn(xn, wqkv_ref[part]) + bqkv_ref[:, cols]
        qkv_ref[:, cols] = block.astype(bf16)
        if part == 1:
            key_t_ref[...] = block.T.astype(bf16)
        if part == 2:
            val_t[...] = block.T.astype(bf16)
    per = lanes // size

    def group(g, carry):
        start = pl.multiple_of(g * lanes, lanes)
        query = qkv_ref[:, pl.ds(start, lanes)]
        keys = qkv_ref[:, pl.ds(pl.multiple_of(features + start, lanes), lanes)]
        for one in range(per):
            head = g * per + one
            at = pl.ds(pl.multiple_of(head * size, size), size)
            scores = dot_nt(keys * head_mask(one, size), query) * scaling + bias_ref[head]
            peak = jnp.max(scores, axis=0, keepdims=True)
            raised = jnp.exp(scores - peak)
            total = jnp.sum(raised, axis=0, keepdims=True)
            probs = raised * (1.0 / total)
            probs_ref[head] = probs
            mixed_t_ref[at, :] = dot_nn(val_t[at, :], probs.astype(bf16)).astype(bf16)
        return carry

    lax.fori_loop(0, heads // per, group, 0)
    mixed = mixed_t_ref[...].astype(f32).T.astype(bf16)
    mid_ref[...] = rows + dot_nn(mixed, wproj_ref[...]) + bproj_ref[...]


def mlp_fwd_kernel(
    mid_ref, gain_ref, off_ref, w1_ref, b1_ref, w2_ref, b2_ref,
    out_ref, yn_ref, slope_ref, act_ref,
):
    middle = mid_ref[...]
    features = middle.shape[1]
    unit, _ = normalize(middle)
    yn = (unit * gain_ref[...] + off_ref[...]).astype(bf16)
    yn_ref[...] = yn
    total = middle + b2_ref[...]
    for chunk in range(w1_ref.shape[0]):
        cols = pl.ds(chunk * features, features)
        pre = dot_nn(yn, w1_ref[chunk]) + b1_ref[:, cols]
        cumul = 0.5 * (1.0 + lax.erf(pre * half_root))
        slope_ref[:, cols] = cumul + pre * (jnp.exp(-0.5 * pre * pre) * inv_root_tau)
        act = (pre * cumul).astype(bf16)
        act_ref[:, cols] = act
        total = total + dot_nn(act, w2_ref[cols, :])
    out_ref[...] = total


def mlp_bwd_kernel(
    g_ref, mid_ref, gain_ref, w1_ref, w2_ref, yn_ref, slope_ref, act_ref,
    gm_ref, gw1_ref, gw2_ref, gb1_ref, gb2_ref, ggain_ref, goff_ref, gbproj_ref,
):
    grad = g_ref[...]
    features = grad.shape[1]
    low = grad.astype(bf16)
    gb2_ref[...] = jnp.sum(grad, axis=0, keepdims=True)
    yn = yn_ref[...]
    g_yn = jnp.zeros_like(grad)
    for chunk in range(w1_ref.shape[0]):
        cols = pl.ds(chunk * features, features)
        gw2_ref[cols, :] = dot_tn(act_ref[:, cols], low).astype(bf16)
        g_pre = dot_nt(low, w2_ref[cols, :]) * slope_ref[:, cols]
        gb1_ref[:, cols] = jnp.sum(g_pre, axis=0, keepdims=True)
        pre_low = g_pre.astype(bf16)
        gw1_ref[chunk] = dot_tn(yn, pre_low).astype(bf16)
        g_yn = g_yn + dot_nt(pre_low, w1_ref[chunk])
    back, g_gain, g_off = norm_pull(mid_ref[...], gain_ref[...], g_yn)
    ggain_ref[...] = g_gain
    goff_ref[...] = g_off
    g_mid = grad + back
    gm_ref[...] = g_mid
    gbproj_ref[...] = jnp.sum(g_mid, axis=0, keepdims=True)


def attn_bwd_kernel(
    gm_ref, x_ref, gain_ref, wqkv_ref, wproj_ref, xn_ref, qkv_ref, key_t_ref, probs_ref,
    mixed_t_ref, spread_ref, spread_t_ref,
    gx_ref, gwqkv_ref, gwproj_ref, gqv_ref, gpairs_ref, ggain_ref, goff_ref,
    dmix, dq_t, dqkv,
):
    g_mid = gm_ref[...]
    features = g_mid.shape[1]
    heads = probs_ref.shape[0]
    size = features // heads
    scaling = size ** (-0.5)
    low = g_mid.astype(bf16)
    gwproj_ref[...] = dot_nn(mixed_t_ref[...], low).astype(bf16)
    dmix[...] = dot_nt(low, wproj_ref[...]).astype(bf16)
    per = lanes // size

    def group(g, carry):
        start = pl.multiple_of(g * lanes, lanes)
        k_at = pl.multiple_of(features + start, lanes)
        v_at = pl.multiple_of(2 * features + start, lanes)
        query = qkv_ref[:, pl.ds(start, lanes)]
        values = qkv_ref[:, pl.ds(v_at, lanes)]
        d_mix = dmix[:, pl.ds(start, lanes)]
        d_keys = jnp.zeros(query.shape, f32)
        d_values = jnp.zeros(query.shape, f32)
        for one in range(per):
            head = g * per + one
            at = pl.ds(pl.multiple_of(head * size, size), size)
            keep = head_mask(one, size)
            probs = probs_ref[head]
            d_probs = dot_nt(values * keep, d_mix)
            d_values = d_values + dot_nn(probs.astype(bf16), d_mix * keep)
            weighed = probs * d_probs
            d_scores = weighed - probs * jnp.sum(weighed, axis=0, keepdims=True)
            scores_low = d_scores.astype(bf16)
            d_keys = d_keys + dot_nn(scores_low, query * keep)
            dq_t[at, :] = dot_nn(key_t_ref[at, :], scores_low)
            folded = dot_nn(spread_t_ref[...], scores_low).astype(bf16)
            gpairs_ref[head] = dot_nn(folded, spread_ref[...])
        dqkv[:, pl.ds(k_at, lanes)] = (d_keys * scaling).astype(bf16)
        dqkv[:, pl.ds(v_at, lanes)] = d_values.astype(bf16)
        gqv_ref[1:2, pl.ds(start, lanes)] = jnp.sum(d_values, axis=0, keepdims=True)
        return carry

    lax.fori_loop(0, heads // per, group, 0)
    d_query = dq_t[...].T * scaling
    gqv_ref[0:1, :] = jnp.sum(d_query, axis=0, keepdims=True)
    dqkv[:, :features] = d_query.astype(bf16)
    xn = xn_ref[...]
    g_xn = jnp.zeros_like(g_mid)
    for part in range(3):
        cols = pl.ds(part * features, features)
        block = dqkv[:, cols]
        gwqkv_ref[part] = dot_tn(xn, block).astype(bf16)
        g_xn = g_xn + dot_nt(block, wqkv_ref[part])
    back, g_gain, g_off = norm_pull(x_ref[...], gain_ref[...], g_xn)
    ggain_ref[...] = g_gain
    goff_ref[...] = g_off
    gx_ref[...] = g_mid + back


def bit_of(index, place):
    return lax.rem(index // (1 << place), 2)


def peers_of(me, places):
    return [me + (1 - 2 * bit_of(me, place)) * (1 << place) for place in range(places)]


def greet(me, places):
    barrier = pltpu.get_barrier_semaphore()
    for peer in peers_of(me, places):
        pl.semaphore_signal(
            barrier, inc=1, device_id=(peer,), device_id_type=pl.DeviceIdType.MESH
        )
    pl.semaphore_wait(barrier, places)


def routes(places):
    high = list(range(places - 1, 2, -1))
    if places < 3:
        return [list(range(places - 1, -1, -1))]
    return [
        high + [2, 1, 0],
        high + [1, 2, 0],
        [2] + high + [1, 0],
        [1] + high + [2, 0],
    ]


def row_parts(total, count):
    units = total // 16
    sizes = [16 * (units // count + (1 if n < units % count else 0)) for n in range(count)]
    return [(sum(sizes[:n]), sizes[n]) for n in range(count)]


def region(places, free, me, lowest=0, forced=None):
    picks = []
    for place in range(places - 1, lowest - 1, -1):
        if forced is not None and place == forced[0]:
            picks.append(forced[1])
        elif place in free:
            picks.append(slice(None))
        else:
            picks.append(bit_of(me, place))
    return tuple(picks)


def gather_kernel(places, x_ref, out_ref, send_sem, recv_sem, own_sem):
    me = lax.axis_index("fsdp")
    peers = peers_of(me, places)
    greet(me, places)
    own = pltpu.make_async_copy(x_ref, out_ref.at[region(places, (), me)], own_sem)
    own.start()
    orders = routes(places)
    parts = row_parts(x_ref.shape[0], len(orders))
    copies = [[] for _ in orders]
    for stage in range(places):
        for n, (order, (low, size)) in enumerate(zip(orders, parts)):
            rows = pl.ds(low, size)
            place = order[stage]
            if stage == 1 and n == 0:
                own.wait()
            if stage:
                copies[n][-1].wait_recv()
            here = region(places, order[:stage], me)
            target = out_ref.at[here + (rows,)]
            copy = pltpu.make_async_remote_copy(
                src_ref=x_ref.at[rows] if stage == 0 else target,
                dst_ref=target,
                send_sem=send_sem.at[n, stage],
                recv_sem=recv_sem.at[n, stage],
                device_id=(peers[place],),
                device_id_type=pl.DeviceIdType.MESH,
            )
            copy.start()
            copies[n].append(copy)
    for group in copies:
        group[-1].wait_recv()
    for group in copies:
        for copy in group:
            copy.wait_send()


def scatter_kernel(places, g_ref, out_ref, acc, *rest):
    landings, (send_sem, recv_sem) = rest[:places], rest[places:]
    me = lax.axis_index("fsdp")
    peers = peers_of(me, places)
    greet(me, places)
    orders = [order[::-1] for order in routes(places)]
    parts = row_parts(g_ref.shape[-2], len(orders))
    everything = set(range(places))
    copies = [[None] * places for _ in orders]

    def send(n, stage):
        order, (low, size) = orders[n], parts[n]
        rows = pl.ds(low, size)
        place = order[stage]
        free = everything - set(order[: stage + 1])
        away = (place, 1 - bit_of(me, place))
        if stage == 0:
            source = g_ref.at[region(places, free, me, 0, away) + (rows,)]
        else:
            source = acc.at[region(places, free, me, 1, away) + (rows,)]
        copy = pltpu.make_async_remote_copy(
            src_ref=source,
            dst_ref=landings[stage].at[(slice(None),) * len(free) + (rows,)],
            send_sem=send_sem.at[n, stage],
            recv_sem=recv_sem.at[n, stage],
            device_id=(peers[place],),
            device_id_type=pl.DeviceIdType.MESH,
        )
        copy.start()
        copies[n][stage] = copy

    def add(n, stage):
        order, (low, size) = orders[n], parts[n]
        rows = pl.ds(low, size)
        free = sorted(everything - set(order[: stage + 1]), reverse=True)
        copies[n][stage].wait_recv()

        def one(at, carry):
            values = {}
            for spot, place in enumerate(free):
                values[place] = lax.rem(at // (1 << (len(free) - 1 - spot)), 2)
            full = tuple(
                values[place] if place in values else bit_of(me, place)
                for place in range(places - 1, -1, -1)
            )
            kept = full[:-1] + (rows,)
            landed = landings[stage][tuple(values[place] for place in free) + (rows,)]
            if stage == 0:
                acc[kept] = g_ref[full + (rows,)] + landed
            elif stage < places - 1:
                acc[kept] = acc[kept] + landed
            else:
                out_ref[rows] = acc[kept].astype(f32) + landed.astype(f32)
            return carry

        lax.fori_loop(0, 1 << len(free), one, 0)

    for n in range(len(orders)):
        send(n, 0)
    for stage in range(places):
        for n in range(len(orders)):
            add(n, stage)
            if stage < places - 1:
                send(n, stage + 1)
    for group in copies:
        for copy in group:
            copy.wait_send()


def gather_all(shard, devices):
    places = devices.bit_length() - 1
    count = len(routes(places))
    out = pl.pallas_call(
        functools.partial(gather_kernel, places),
        out_shape=shaped((2,) * places + shard.shape, shard.dtype),
        in_specs=[pl.BlockSpec(memory_space=pltpu.VMEM)],
        out_specs=pl.BlockSpec(memory_space=pltpu.VMEM),
        scratch_shapes=[
            pltpu.SemaphoreType.DMA((count, places)),
            pltpu.SemaphoreType.DMA((count, places)),
            pltpu.SemaphoreType.DMA,
        ],
        compiler_params=pltpu.CompilerParams(
            collective_id=0, has_side_effects=True, vmem_limit_bytes=60 * 1024 * 1024
        ),
    )(shard)
    return out.reshape((devices,) + shard.shape)


def scatter_all(grads, devices):
    places = devices.bit_length() - 1
    count = len(routes(places))
    tail = grads.shape[1:]
    return pl.pallas_call(
        functools.partial(scatter_kernel, places),
        out_shape=shaped(tail, f32),
        in_specs=[pl.BlockSpec(memory_space=pltpu.VMEM)],
        out_specs=pl.BlockSpec(memory_space=pltpu.VMEM),
        scratch_shapes=[pltpu.VMEM((2,) * (places - 1) + tail, bf16)]
        + [pltpu.VMEM((2,) * (places - 1 - stage) + tail, bf16) for stage in range(places)]
        + [
            pltpu.SemaphoreType.DMA((count, places)),
            pltpu.SemaphoreType.DMA((count, places)),
        ],
        compiler_params=pltpu.CompilerParams(
            collective_id=1, has_side_effects=True, vmem_limit_bytes=60 * 1024 * 1024
        ),
    )(grads.reshape((2,) * places + tail))


def run(kernel, outs, args, scratch=(), flops=0):
    size = sum(a.size * a.dtype.itemsize for a in args)
    size += sum(a.size * a.dtype.itemsize for a in outs)
    return pl.pallas_call(
        kernel,
        out_shape=tuple(outs),
        in_specs=[pl.BlockSpec(memory_space=pltpu.VMEM)] * len(args),
        out_specs=tuple([pl.BlockSpec(memory_space=pltpu.VMEM)] * len(outs)),
        scratch_shapes=list(scratch),
        compiler_params=pltpu.CompilerParams(vmem_limit_bytes=60 * 1024 * 1024),
        cost_estimate=pl.CostEstimate(flops=flops, bytes_accessed=size, transcendentals=0),
    )(*args)


def shaped(shape, dtype):
    return jax.ShapeDtypeStruct(tuple(shape), dtype)


def offset_onehot(table_rows):
    places = jnp.arange(WIN * WIN, dtype=jnp.int32)
    row_at = places // WIN
    col_at = places % WIN
    index = (row_at[:, None] - row_at[None, :] + WIN - 1) * (2 * WIN - 1) + (
        col_at[:, None] - col_at[None, :] + WIN - 1
    )
    targets = jnp.arange(table_rows, dtype=jnp.int32)
    return (index.reshape(-1)[:, None] == targets[None, :]).astype(f32)


def token_places(shift_by):
    token = jnp.arange(SIDE * SIDE, dtype=jnp.int32)
    row = (token // SIDE - shift_by) % SIDE
    col = (token % SIDE - shift_by) % SIDE
    window = (row // WIN) * (SIDE // WIN) + col // WIN
    inside = (row % WIN) * WIN + col % WIN
    if shift_by:
        edges = SIDE - WIN, SIDE - shift_by
        a_row = (row >= edges[0]).astype(jnp.int32) + (row >= edges[1]).astype(jnp.int32)
        a_col = (col >= edges[0]).astype(jnp.int32) + (col >= edges[1]).astype(jnp.int32)
        label = 3 * a_row + a_col
    else:
        label = jnp.zeros_like(token)
    mask = jnp.where(label[:, None] == label[None, :], 0.0, mask_fill)
    mask = jnp.where(window[:, None] == window[None, :], mask, outside_fill).astype(f32)
    spread = (inside[:, None] == jnp.arange(WIN * WIN)[None, :]).astype(bf16)
    return mask, spread, spread.T


def local(
    images,
    cotangent,
    counts,
    *shards,
):
    devices = lax.axis_size("fsdp")
    gather_dims = (1, 1, 1, 2, 1, 1, 1, 1, 1, 1, 1, 1, 1)
    large_at = (2, 5, 9, 11)
    small_at = (0, 1, 3, 4, 6, 7, 8, 10, 12)
    flats = [tensor.reshape(-1) for tensor in shards]
    tokens, features = images.shape[1:]
    packed = jnp.concatenate([flats[n] for n in small_at])
    small_rows = 16 * -(-packed.shape[0] // (16 * features))
    packed = jnp.pad(packed, (0, small_rows * features - packed.shape[0]))
    blocks, spans = [packed.reshape(small_rows, features)], {}
    filled = small_rows
    for layer in range(LAYERS):
        for n in large_at:
            piece = shards[n][layer]
            rows, wide = piece.shape[0], piece.shape[1] // features
            piece = piece.reshape(rows, wide, features).transpose(1, 0, 2)
            blocks.append(piece.reshape(rows * wide, features))
            spans[n, layer] = (filled, rows, wide)
            filled += rows * wide
    spare = -filled % 16
    if spare:
        blocks.append(jnp.zeros((spare, features), bf16))
    gathered = gather_all(jnp.concatenate(blocks), devices)
    packed = gathered[:, :small_rows].reshape(devices, -1)
    weights = [None] * len(shards)
    at = 0
    for n in small_at:
        shape, axis_dim = shards[n].shape, gather_dims[n]
        size = flats[n].shape[0]
        piece = packed[:, at : at + size].reshape((devices,) + shape)
        piece = jnp.moveaxis(piece, 0, axis_dim)
        full = shape[:axis_dim] + (devices * shape[axis_dim],) + shape[axis_dim + 1 :]
        weights[n] = piece.reshape(full)
        at += size
    for n in large_at:
        weights[n] = [None] * LAYERS
        for layer in range(LAYERS):
            low, rows, wide = spans[n, layer]
            piece = gathered[:, low : low + rows * wide]
            piece = piece.reshape(devices, wide, rows, features).transpose(1, 0, 2, 3)
            piece = piece.reshape(wide, devices * rows, features)
            weights[n][layer] = piece if wide > 1 else piece[0]
    table = weights[4]
    heads = table.shape[-1]
    hidden = weights[10].shape[-1]
    cells = WIN * WIN
    onehot = offset_onehot(table.shape[1])
    pairs = jnp.einsum("pt,lth->lhp", onehot.astype(bf16), table, preferred_element_type=f32)
    pairs = pairs.reshape(LAYERS, heads, cells, cells).transpose(0, 1, 3, 2).astype(bf16)
    zero = jnp.zeros((features,), f32)

    def row(n, layer):
        return weights[n][layer].astype(f32).reshape(1, -1)

    active = counts[0] > 0
    current = images[0].astype(f32)
    saved = []
    for layer in range(LAYERS):
        mask, spread, spread_t = token_places(SHIFT if layer % 2 else 0)
        bias = run(
            bias_kernel,
            [shaped((heads, tokens, tokens), f32)],
            (pairs[layer], spread, spread_t, mask),
        )[0]
        b_qv = weights[3][layer].astype(f32)
        b_qkv = jnp.concatenate([b_qv[0], zero, b_qv[1]]).reshape(1, -1)
        attn = run(
            attn_fwd_kernel,
            [
                shaped((tokens, features), f32),
                shaped((tokens, features), bf16),
                shaped((tokens, 3 * features), bf16),
                shaped((features, tokens), bf16),
                shaped((heads, tokens, tokens), f32),
                shaped((features, tokens), bf16),
            ],
            (current, row(0, layer), row(1, layer), weights[2][layer], b_qkv, bias,
             weights[5][layer], row(6, layer)),
            [pltpu.VMEM((features, tokens), bf16)],
        )
        mlp = run(
            mlp_fwd_kernel,
            [
                shaped((tokens, features), f32),
                shaped((tokens, features), bf16),
                shaped((tokens, hidden), f32),
                shaped((tokens, hidden), bf16),
            ],
            (attn[0], row(7, layer), row(8, layer), weights[9][layer], row(10, layer),
             weights[11][layer], row(12, layer)),
        )
        saved.append((current, attn, mlp, spread, spread_t))
        current = mlp[0]
    outs = jnp.where(active, current, 0.0)[None]
    grad = jnp.where(active, cotangent[0].astype(f32), 0.0)
    sums = [[None] * LAYERS for _ in shards]
    owned = [[None] * LAYERS for _ in shards]

    def scatter(value):
        return value

    for layer in reversed(range(LAYERS)):
        entry, attn, mlp, spread, spread_t = saved[layer]
        g_mid, g_w1, g_w2, *rest = run(
            mlp_bwd_kernel,
            [
                shaped((tokens, features), f32),
                shaped((hidden // features, features, features), bf16),
                shaped((hidden, features), bf16),
                shaped((1, hidden), f32),
                shaped((1, features), f32),
                shaped((1, features), f32),
                shaped((1, features), f32),
                shaped((1, features), f32),
            ],
            (grad, attn[0], row(7, layer), weights[9][layer], weights[11][layer], *mlp[1:]),
        )
        sums[10][layer], sums[12][layer], sums[7][layer], sums[8][layer], sums[6][layer] = rest
        owned[11][layer] = scatter(g_w2)
        owned[9][layer] = scatter(g_w1)
        grad, g_qkv, g_proj, g_qv, g_pairs, g_gain, g_off = run(
            attn_bwd_kernel,
            [
                shaped((tokens, features), f32),
                shaped((3, features, features), bf16),
                shaped((features, features), bf16),
                shaped((2, features), f32),
                shaped((heads, cells, cells), f32),
                shaped((1, features), f32),
                shaped((1, features), f32),
            ],
            (g_mid, entry, row(0, layer), weights[2][layer], weights[5][layer], *attn[1:],
             spread, spread_t),
            [
                pltpu.VMEM((tokens, features), bf16),
                pltpu.VMEM((features, tokens), f32),
                pltpu.VMEM((tokens, 3 * features), bf16),
            ],
        )
        owned[5][layer] = scatter(g_proj)
        owned[2][layer] = scatter(g_qkv)
        sums[0][layer], sums[1][layer], sums[3][layer] = g_gain, g_off, g_qv
        per_pair = g_pairs.transpose(0, 2, 1).reshape(heads, cells * cells)
        sums[4][layer] = jnp.dot(per_pair, onehot, precision=lax.Precision.HIGHEST).T
    parts = []
    for n in small_at:
        shape, axis_dim = shards[n].shape, gather_dims[n]
        both = jnp.stack(sums[n])
        both = both.reshape(shape[:axis_dim] + (devices,) + shape[axis_dim:])
        parts.append(jnp.moveaxis(both, axis_dim, 0).reshape(devices, -1))
    packed = jnp.concatenate(parts, axis=1).astype(bf16)
    packed = jnp.pad(packed, ((0, 0), (0, small_rows * features - packed.shape[1])))
    blocks = [packed.reshape(devices, small_rows, features)]
    for layer in range(LAYERS):
        for n in large_at:
            low, rows, wide = spans[n, layer]
            piece = owned[n][layer].reshape(wide, devices, rows, features)
            blocks.append(piece.transpose(1, 0, 2, 3).reshape(devices, rows * wide, features))
    if spare:
        blocks.append(jnp.zeros((devices, spare, features), bf16))
    reduced = scatter_all(jnp.concatenate(blocks, axis=1), devices)
    summed = reduced[:small_rows].reshape(-1)
    at = 0
    for n in small_at:
        size = flats[n].shape[0]
        owned[n] = summed[at : at + size].reshape(shards[n].shape)
        at += size
    for n in large_at:
        for layer in range(LAYERS):
            low, rows, wide = spans[n, layer]
            piece = reduced[low : low + rows * wide].reshape(wide, rows, features)
            owned[n][layer] = piece.transpose(1, 0, 2).reshape(rows, wide * features)
        owned[n] = jnp.stack(owned[n])
    return (outs, grad[None], *owned)


GATHERED = (
    (None, 0, 0, 0, 1, 'hlxy'),
    (0, 0, 0, 1, 3, 'xyhl'),
    (0, 0, 1, 2, 3, 'hlyx'),
    (0, 0, 2, 3, 3, 'hlyx'),
    (0, 1, 0, 1, 1, 'hxly'),
    (0, 2, 0, 1, 4, 'hlxy'),
    (0, 2, 1, 2, 4, 'hlyx'),
    (0, 2, 2, 3, 4, 'hlxy'),
    (0, 2, 3, 4, 4, 'hlxy'),
    (0, 3, 0, 1, 4, 'xhyl'),
    (0, 3, 1, 2, 4, 'hlxy'),
    (0, 3, 2, 4, 4, 'hlxy'),
    (1, 0, 0, 2, 3, 'hylx'),
    (1, 0, 2, 3, 3, 'yhlx'),
    (1, 1, 0, 1, 1, 'hlxy'),
    (1, 2, 0, 1, 4, 'hlyx'),
    (1, 2, 1, 2, 4, 'hlyx'),
    (1, 2, 2, 3, 4, 'yhlx'),
    (1, 2, 3, 4, 4, 'xyhl'),
    (1, 3, 0, 2, 4, 'xyhl'),
    (1, 3, 2, 4, 4, 'hxly'),
)
SCATTERED = (
    (1, 3, 0, 2, 4, 'ylxh'),
    (1, 3, 2, 4, 4, 'lxhy'),
    (1, 2, 0, 2, 4, 'xlhy'),
    (1, 2, 2, 4, 4, 'ylxh'),
    (1, 1, 0, 1, 1, 'lxyh'),
    (1, 0, 0, 1, 3, 'yxlh'),
    (0, 3, 0, 2, 4, 'xlyh'),
    (1, 0, 1, 3, 3, 'lhyx'),
    (0, 3, 2, 4, 4, 'ylxh'),
    (0, 0, 0, 2, 3, 'yxlh'),
    (0, 2, 0, 2, 4, 'yxlh'),
    (0, 2, 2, 4, 4, 'xylh'),
    (0, 1, 0, 1, 1, 'xylh'),
    (0, 0, 2, 3, 3, 'yxlh'),
    (None, 0, 0, 0, 1, 'ylxh'),
)
AGENDA = (
    (
        (0, 3, 0), (0, 5, 0), (0, 1, 0), (0, 18, 0), (0, 0, 0), (0, 19, 0),
        (0, 2, 0), (0, 13, 0), (0, 16, 0), (0, 20, 0), (0, 3, 1), (0, 4, 0),
        (0, 5, 1), (0, 1, 1), (0, 8, 0), (0, 17, 0), (0, 2, 1), (0, 19, 1),
        (0, 15, 0), (0, 0, 1), (0, 11, 0), (0, 16, 1), (0, 3, 2), (0, 9, 0),
        (0, 18, 1), (0, 12, 0), (0, 4, 1), (0, 5, 2), (0, 20, 1), (0, 2, 2),
        (0, 8, 1), (0, 6, 0), (0, 15, 1), (0, 13, 1), (0, 3, 3), (0, 16, 2),
        (0, 4, 2), (0, 0, 2), (0, 7, 0), (0, 5, 3), (0, 8, 2), (0, 6, 1),
        (0, 15, 2), (0, 10, 0), (0, 11, 1), (0, 1, 2), (0, 12, 1), (0, 2, 3),
        (0, 6, 2), (0, 4, 3), (0, 13, 2), (0, 14, 0), (0, 11, 2), (0, 7, 1),
        (0, 17, 1), (0, 10, 1), (0, 18, 2), (0, 8, 3), (0, 13, 3), (0, 7, 2),
        (0, 1, 3), (0, 9, 1), (0, 5, 4), (0, 12, 2), (0, 0, 3), (0, 3, 4),
        (0, 10, 2), (0, 14, 1),
    ),
    (
        (0, 6, 3), (0, 11, 3), (0, 8, 4), (0, 19, 2), (0, 0, 4), (0, 17, 2),
        (0, 20, 2), (0, 9, 2), (0, 16, 3), (0, 2, 4), (0, 14, 2), (0, 1, 4),
        (0, 12, 3), (0, 4, 4), (0, 7, 3),
    ),
    (
        (0, 10, 3), (0, 11, 4), (0, 13, 4),
    ),
    (
        (0, 9, 3), (0, 6, 4),
    ),
    (
        (0, 16, 4),
    ),
    (
        (0, 7, 4), (0, 18, 3), (0, 15, 3), (0, 17, 3), (0, 14, 3), (0, 20, 3),
        (0, 10, 4),
    ),
    (
        (0, 19, 3), (0, 9, 4), (0, 12, 4),
    ),
    (),
    (
        (0, 18, 4), (0, 14, 4), (0, 15, 4),
    ),
    (),
    (
        (0, 17, 4),
    ),
    (),
    (
        (0, 19, 4), (0, 20, 4),
    ),
    (),
    (
        (1, 0, 0), (1, 1, 0),
    ),
    (
        (1, 0, 1), (1, 1, 1), (1, 3, 0), (1, 2, 0),
    ),
    (
        (1, 4, 0),
    ),
    (
        (1, 3, 1), (1, 2, 1), (1, 4, 1),
    ),
    (),
    (
        (1, 7, 0), (1, 5, 0), (1, 1, 2), (1, 0, 2),
    ),
    (),
    (
        (1, 8, 0), (1, 7, 1), (1, 5, 1), (1, 4, 2),
    ),
    (
        (1, 11, 0), (1, 8, 1), (1, 2, 2), (1, 10, 0), (1, 0, 3),
    ),
    (
        (1, 11, 1), (1, 1, 3), (1, 6, 0), (1, 3, 2),
    ),
    (
        (1, 10, 1),
    ),
    (
        (1, 12, 0), (1, 4, 3), (1, 6, 1), (1, 7, 2),
    ),
    (
        (1, 9, 0), (1, 13, 0), (1, 8, 2), (1, 9, 1), (1, 2, 3), (1, 11, 2),
        (1, 5, 2),
    ),
    (
        (1, 10, 2), (1, 6, 2), (1, 14, 0), (1, 3, 3), (1, 14, 1), (1, 12, 1),
        (1, 0, 4), (1, 5, 3), (1, 3, 4), (1, 8, 3), (1, 10, 3), (1, 13, 1),
        (1, 9, 2), (1, 4, 4), (1, 1, 4), (1, 5, 4), (1, 11, 3), (1, 12, 2),
        (1, 6, 3), (1, 10, 4), (1, 14, 2), (1, 7, 3),
    ),
    (
        (1, 8, 4), (1, 13, 2), (1, 9, 3), (1, 5, 5), (1, 2, 4), (1, 11, 4),
        (1, 3, 5), (1, 12, 3), (1, 14, 3), (1, 6, 4), (1, 13, 3), (1, 9, 4),
        (1, 10, 5), (1, 7, 4), (1, 14, 4), (1, 0, 5), (1, 4, 5), (1, 1, 5),
        (1, 11, 5), (1, 12, 4), (1, 13, 4), (1, 6, 5),
    ),
    (
        (1, 9, 5), (1, 12, 5), (1, 8, 5), (1, 14, 5), (1, 2, 5), (1, 7, 5),
        (1, 13, 5),
    ),
)


def stack_rows(parts):
    return jnp.concatenate(parts, axis=0)


def permute_f32(matrix, rows):
    high = rows.astype(bf16)
    rest = rows - high.astype(f32)
    middle = rest.astype(bf16)
    low = (rest - middle.astype(f32)).astype(bf16)
    return dot_nn(matrix, high) + (dot_nn(matrix, middle) + dot_nn(matrix, low))


def slots_of(window):
    padded = -(-window // 8) * 8
    lanes_each = 64
    return padded, lanes_each


def places_in_windows(shift_by):
    token = np.arange(SIDE * SIDE)
    row = (token // SIDE - shift_by) % SIDE
    col = (token % SIDE - shift_by) % SIDE
    window = (row // WIN) * (SIDE // WIN) + col // WIN
    inside = (row % WIN) * WIN + col % WIN
    edges = SIDE - WIN, SIDE - shift_by
    a_row = (row >= edges[0]).astype(int) + (row >= edges[1]).astype(int)
    a_col = (col >= edges[0]).astype(int) + (col >= edges[1]).astype(int)
    return window, inside, 3 * a_row + a_col


def constants(heads, per_device_rows, devices):
    cells = WIN * WIN
    padded, wide = slots_of(cells)
    windows = (SIDE // WIN) ** 2
    tokens = SIDE * SIDE
    total = windows * padded
    perms = []
    for shift_by in (0, SHIFT):
        window, inside, label = places_in_windows(shift_by)
        perm = np.zeros((total, tokens), np.float32)
        perm[window * padded + inside, np.arange(tokens)] = 1.0
        perms.append(perm)
    mask = np.zeros((windows, padded, wide), np.float32)
    labels = np.zeros((windows, cells), int)
    labels[window, inside] = label
    mask[:, :cells, :cells] = np.where(labels[:, :, None] == labels[:, None, :], 0.0, mask_fill)
    group = 2 * lanes // wide
    mask = np.tile(mask, (1, 1, group))
    span = 2 * WIN - 1
    strips = -(-span * WIN // 16) * 16
    onehot = np.zeros((WIN, strips, devices * 8), np.float32)
    for c_q in range(WIN):
        for d_r in range(span):
            for c_k in range(WIN):
                t = d_r * span + c_q - c_k + WIN - 1
                spot = (t // per_device_rows) * 8 + t % per_device_rows
                onehot[c_q, (span - 1 - d_r) * WIN + c_k, spot] = 1.0
    onehot = onehot.reshape(WIN * strips, devices * 8)
    query = np.arange(heads * wide) % wide
    head = np.arange(heads * wide) // wide
    lane_row = np.where(query < cells, query // WIN, -1)
    lane_col = np.where(query < cells, query % WIN, -1)
    lane_of = np.zeros((8, heads * wide), np.int32)
    lane_of[0], lane_of[1] = lane_row, lane_col
    expand = np.zeros((lanes, heads * wide), np.float32)
    expand[head, np.arange(heads * wide)] = 1.0
    collect = np.zeros((heads * wide, lanes), np.float32)
    real = query < cells
    collect[np.arange(heads * wide)[real], (lane_col * heads + head)[real]] = 1.0
    fold = np.zeros((lanes, lanes), np.float32)
    for lane in range(WIN * heads):
        fold[lane, lane % heads] = 1.0
    plain, shifted = perms
    low = [plain, shifted, shifted @ plain.T, plain @ shifted.T, plain.T, shifted.T,
           onehot, onehot.T, expand, collect, fold]
    return [jnp.asarray(a, bf16) for a in low] + [jnp.asarray(lane_of), jnp.asarray(mask)]


AXES = "hlyxc"
FIXED = 13


class Links:
    def __init__(self, sems):
        me = lax.axis_index("fsdp")
        self.me = me
        self.own, self.peer = {}, {}
        for place, axis in enumerate(reversed(AXES)):
            bit = bit_of(me, place)
            self.own[axis] = bit
            self.peer[axis] = me + (1 - 2 * bit) * (1 << place)
        self.sems = sems
        self.copies = {}

    def greet(self):
        barrier = pltpu.get_barrier_semaphore()
        for axis in AXES:
            pl.semaphore_signal(
                barrier, inc=1, device_id=(self.peer[axis],), device_id_type=pl.DeviceIdType.MESH
            )

    def greeted(self):
        pl.semaphore_wait(pltpu.get_barrier_semaphore(), len(AXES))

    def send(self, key, way, source, target, axis):
        send_sem, recv_sem = self.sems[way]
        copy = pltpu.make_async_remote_copy(
            src_ref=source,
            dst_ref=target,
            send_sem=send_sem.at[key[1], key[0]],
            recv_sem=recv_sem.at[key[1], key[0]],
            device_id=(self.peer[axis],),
            device_id_type=pl.DeviceIdType.MESH,
        )
        copy.start()
        self.copies[(way,) + key] = copy

    def arrive(self, way, key):
        self.copies[(way,) + key].wait_recv()

    def finish(self):
        for copy in self.copies.values():
            copy.wait_send()


def all_kernel(
    gspans, rspans, agenda,
    count_ref, x_ref, cot_ref, again_ref, aoff_ref, wqkv_ref, bqv_ref, rel_ref, wproj_ref, bproj_ref,
    mgain_ref, moff_ref, w1_ref, b1_ref, w2_ref, b2_ref,
    *rest,
):
    far, rest = rest[:FIXED], rest[FIXED:]
    (
        out_ref, gin_ref, gagain_ref, gaoff_ref, gwqkv_ref, gbqv_ref, grel_ref, gwproj_ref, gbproj_ref,
        gmgain_ref, gmoff_ref, gw1_ref, gb1_ref, gw2_ref, gb2_ref,
        w, g, land_0, land_1, land_2, land_3, land_4, sm, sg, sland_0, sland_1, sland_2, sland_3, sland_4,
        xs, xn_s, qkv_s, probs_s, mixed_s, mid_s, yn_s, slope_s, act_s,
        bias_s, strip_s, kinds_s, b1_s, own_s, mixf_s, dmix_s, dqkv_s, dsum_s, kg_s, b1g_s, rg_s,
        gs_send, gs_recv, rs_send, rs_recv,
        *near,
    ) = rest
    (
        plain_ref, shifted_ref, forth_ref, back_ref, plain_t_ref, shifted_t_ref,
        onehot_ref, onehot_t_ref, expand_ref, collect_ref, fold_ref, lane_ref, mask_ref,
    ) = near[:FIXED]
    near_sem = near[FIXED]
    links = Links({"g": (gs_send, gs_recv), "r": (rs_send, rs_recv)})
    me = links.me
    every = slice(None)
    home = tuple(links.own[axis] for axis in AXES)
    devices = 1 << len(AXES)
    lands = ((land_0, sland_0), (land_1, sland_1), (land_2, sland_2), (land_3, sland_3), (land_4, sland_4))
    rows_each = wqkv_ref.shape[1]
    features = wproj_ref.shape[2]
    hidden = w1_ref.shape[2]
    parts = wqkv_ref.shape[2] // features
    wide_parts = hidden // features
    deep = w2_ref.shape[1]
    table_each = rel_ref.shape[0]
    heads = rel_ref.shape[2]
    size = features // heads
    scaling = size ** (-0.5)
    at_proj = parts * rows_each
    at_one = at_proj + rows_each
    at_two = at_one + wide_parts * rows_each
    cells = WIN * WIN
    padded, wide = slots_of(cells)
    windows = (SIDE // WIN) ** 2
    per = lanes // size
    group_lanes = per * wide
    share = features // devices
    pack = lanes // share
    share_one = hidden // devices
    pack_one = lanes // share_one
    span = 2 * WIN - 1
    strips = -(-span * WIN // 16) * 16

    links.greet()
    brought = [
        pltpu.make_async_copy(source, target, near_sem.at[n])
        for n, (source, target) in enumerate(zip(far, near[:FIXED]))
    ]
    for copy in brought:
        copy.start()
    own_s[...] = jnp.zeros_like(own_s)
    at = 0
    for ref in (again_ref, aoff_ref, bqv_ref, bproj_ref, mgain_ref, moff_ref, b2_ref):
        piece = ref[...].astype(f32)
        if ref.shape[0] == LAYERS and len(ref.shape) == 3:
            for layer in range(LAYERS):
                own_s[at : at + ref.shape[1], 0:share] = piece[layer]
                at += ref.shape[1]
        else:
            own_s[at : at + LAYERS, 0:share] = piece
            at += LAYERS
    row_at = lax.broadcasted_iota(jnp.int32, (lanes, lanes), 0)
    lane_at = lax.broadcasted_iota(jnp.int32, (lanes, lanes), 1)
    spot = share * lax.rem(me, pack)
    place = jnp.where((lane_at == row_at + spot) & (row_at < share), 1.0, 0.0).astype(bf16)
    kinds = dot_nn(own_s[...].astype(bf16), place)
    spot = share_one * lax.rem(me, pack_one)
    place = jnp.where((lane_at == row_at + spot) & (row_at < share_one), 1.0, 0.0).astype(bf16)
    own_s[...] = jnp.zeros_like(own_s)
    own_s[0:LAYERS, 0:share_one] = b1_ref[...].astype(f32)
    firsts = dot_nn(own_s[...].astype(bf16), place)
    own_s[...] = jnp.zeros_like(own_s)
    tables = rel_ref[...].astype(f32)
    for layer in range(LAYERS):
        own_s[layer * 8 : layer * 8 + table_each, 0:heads] = tables[:, layer, :]
        own_s[layer * 8 + table_each : layer * 8 + table_each + 1, :] = firsts[layer : layer + 1]
    sm[home + (every, slice(0, lanes))] = kinds.astype(bf16)
    sm[home + (every, slice(lanes, 2 * lanes))] = own_s[...].astype(bf16)
    for layer in range(LAYERS):
        for part in range(parts):
            w[(layer,) + home + (pl.ds(part * rows_each, rows_each), every)] = (
                wqkv_ref[layer, :, part * features : (part + 1) * features]
            )
        w[(layer,) + home + (pl.ds(at_proj, rows_each), every)] = wproj_ref[layer]
        for part in range(wide_parts):
            w[(layer,) + home + (pl.ds(at_one + part * rows_each, rows_each), every)] = (
                w1_ref[layer, :, part * features : (part + 1) * features]
            )
        w[(layer,) + home + (pl.ds(at_two, deep), every)] = w2_ref[layer]

    def view(where, span, picks):
        big, small = where
        layer, low, count, _ = span
        if layer is None:
            return small.at[picks]
        return big.at[(layer,) + picks + (pl.ds(low, count),)]

    def gather(n, stage):
        span = gspans[n]
        route = span[3] + AXES[-1]
        if stage:
            links.arrive("g", (stage - 1, n))
        got = route[:stage]
        ref = view((w, sm), span, tuple(every if a in got else links.own[a] for a in AXES))
        links.send((stage, n), "g", ref, ref, route[stage])

    def merge(n, stage):
        span = rspans[n]
        closed = (AXES[-1] + span[3])[: stage + 1]
        opened = [axis for axis in AXES if axis not in closed]

        fixed = min(2, len(opened))

        def one(at, carry):
            for inner in range(1 << fixed):
                bits = {
                    axis: (inner >> k) % 2 if k < fixed else bit_of(at, k - fixed)
                    for k, axis in enumerate(reversed(opened))
                }
                here = view((g, sg), span, tuple(bits.get(a, links.own[a]) for a in AXES))
                there = view(lands[stage], span, tuple(bits[a] for a in opened))
                here[...] = here[...] + there[...]
            return carry

        if len(opened) == fixed:
            one(0, 0)
        else:
            lax.fori_loop(0, 1 << (len(opened) - fixed), one, 0)

    def scatter(n, stage):
        span = rspans[n]
        layer, low, count, _ = span
        order = AXES[-1] + span[3]
        if stage:
            links.arrive("r", (stage - 1, n))
        if stage < len(AXES):
            if stage:
                merge(n, stage - 1)
            axis, closed = order[stage], order[:stage]
            where = {a: links.own[a] if a in closed else every for a in AXES}
            where[axis] = 1 - links.own[axis]
            source = view((g, sg), span, tuple(where[a] for a in AXES))
            target = view(lands[stage], span, (every,) * (len(AXES) - 1 - stage))
            links.send((stage, n), "r", source, target, axis)
            return
        if layer is None:
            small_out(sg[home].astype(f32) + sland_4[...].astype(f32))
            return
        for unit in range(low, low + count, rows_each):
            rows = pl.ds(unit, rows_each)
            total = g[(layer,) + home + (rows,)].astype(f32) + land_4[layer, rows, :].astype(f32)
            if unit < at_proj:
                part = unit // rows_each
                gwqkv_ref[layer, :, part * features : (part + 1) * features] = total
            elif unit < at_one:
                gwproj_ref[layer] = total
            elif unit < at_two:
                part = (unit - at_one) // rows_each
                gw1_ref[layer, :, part * features : (part + 1) * features] = total
            else:
                gw2_ref[layer, unit - at_two : unit - at_two + rows_each, :] = total

    def small_out(total):
        picked = jnp.where(lax.broadcasted_iota(jnp.int32, (16, lanes), 1) // share == lax.rem(me, pack),
                           total[:, 0:lanes], 0.0)
        folded = picked[:, 0:share]
        for n in range(1, pack):
            folded = folded + picked[:, n * share : (n + 1) * share]
        at = 0
        for ref in (gagain_ref, gaoff_ref, gbqv_ref, gbproj_ref, gmgain_ref, gmoff_ref, gb2_ref):
            if len(ref.shape) == 3:
                for layer in range(LAYERS):
                    ref[layer] = folded[at : at + ref.shape[1]]
                    at += ref.shape[1]
            else:
                ref[...] = folded[at : at + LAYERS]
                at += LAYERS
        tail = total[:, lanes : 2 * lanes]
        for layer in range(LAYERS):
            grel_ref[layer] = tail[layer * 8 : layer * 8 + table_each, 0:heads]
            row = tail[layer * 8 + table_each : layer * 8 + table_each + 1]
            keep = lax.broadcasted_iota(jnp.int32, (1, lanes), 1) // share_one
            row = jnp.where(keep == lax.rem(me, pack_one), row, 0.0)
            folded_row = row[:, 0:share_one]
            for n in range(1, pack_one):
                folded_row = folded_row + row[:, n * share_one : (n + 1) * share_one]
            gb1_ref[layer : layer + 1, :] = folded_row

    def qkv_part(layer, part):
        block = w[layer, :, :, :, :, :, part * rows_each : (part + 1) * rows_each, :]
        return block.reshape(features, features)

    def proj_of(layer):
        return w[layer, :, :, :, :, :, at_proj : at_proj + rows_each, :].reshape(features, features)

    def one_of(layer, part):
        low = at_one + part * rows_each
        return w[layer, :, :, :, :, :, low : low + rows_each, :].reshape(features, features)

    def two_of(layer, part):
        return w[layer, part // 2, part % 2, :, :, :, at_two : at_two + deep, :].reshape(features, features)

    def put(layer, low, value):
        g[layer, :, :, :, :, :, low : low + rows_each, :] = value.astype(bf16).reshape(
            2, 2, 2, 2, 2, rows_each, features
        )

    agenda = list(agenda)

    def go():
        for way, n, stage in agenda.pop(0):
            (gather if way == 0 else scatter)(n, stage)

    def have(layer, low, high):
        for n, span in enumerate(gspans):
            if span[0] == layer and (layer is None or low <= span[1] < high):
                links.arrive("g", (4, n))

    links.greeted()
    go()
    for copy in brought:
        copy.wait()

    stream = dot_nn(plain_ref[...], x_ref[0])
    xs[0] = stream
    qkv_s[:, :, 48:64, :] = jnp.zeros((LAYERS, windows, 16, parts * features), bf16)
    dmix_s[:, 48:64, :] = jnp.zeros((windows, 16, features), bf16)
    strip_s[...] = jnp.zeros_like(strip_s)

    go()
    have(None, 0, 0)
    small = sm[...].reshape(devices, 16, 2 * lanes).astype(f32)
    for tile in range(features // lanes):
        block = small[tile * pack : (tile + 1) * pack, :, 0:lanes]
        kinds_s[:, tile * lanes : (tile + 1) * lanes] = jnp.sum(block, axis=0)
    for tile in range(hidden // lanes):
        total = small[tile * pack_one, :, lanes : 2 * lanes]
        for n in range(1, pack_one):
            total = total + small[tile * pack_one + n, :, lanes : 2 * lanes]
        for layer in range(LAYERS):
            at = layer * 8 + table_each
            b1_s[layer : layer + 1, tile * lanes : (tile + 1) * lanes] = total[at : at + 1]

    def kind(n):
        return kinds_s[n : n + 1, :]

    lane_row = lane_ref[0:1, :]
    lane_col = lane_ref[1:2, :]
    for layer in range(LAYERS):
        table = small[:, layer * 8 : (layer + 1) * 8, lanes : 2 * lanes]
        table = table.reshape(devices * 8, lanes).astype(bf16)
        spread = dot_nn(table, expand_ref[...]).astype(bf16)
        strip = jnp.zeros((strips, heads * wide), f32)
        for col in range(WIN):
            found = dot_nn(onehot_ref[col * strips : (col + 1) * strips, :], spread)
            strip = jnp.where(lane_col == col, found, strip)
        strip_s[0:strips, :] = strip
        bias = jnp.zeros((padded, heads * wide), f32)
        for row in range(WIN):
            low = (WIN - 1 - row) * WIN
            bias = jnp.where(lane_row == row, strip_s[low : low + padded, :], bias)
        key_at = lax.broadcasted_iota(jnp.int32, (padded, heads * wide), 0)
        bias_s[layer] = jnp.where(key_at < cells, bias, outside_fill)

    keeps = [head_mask(one, size) for one in range(per)]

    def diagonal(block):
        return stack_rows([block * keep for keep in keeps])

    def undiagonal(block):
        total = block[0:padded] * keeps[0].astype(f32)
        for n in range(1, per):
            total = total + block[n * wide : n * wide + padded] * keeps[n].astype(f32)
        return total

    def both_halves(group):
        groups = heads // per
        go()
        lax.fori_loop(0, groups // 2, group, 0)
        go()
        lax.fori_loop(groups // 2, groups, group, 0)

    def attention_forward(layer):
        rows = xs[layer]
        go()
        have(layer, 0, at_proj)
        unit, _ = normalize(rows)
        xn = (unit * kind(layer) + kind(LAYERS + layer)).astype(bf16)
        xn_s[layer] = xn
        for part in range(parts):
            block = dot_nn(xn, qkv_part(layer, part))
            if part != 1:
                block = block + kind(2 * LAYERS + 2 * layer + part // 2)
            for window in range(windows):
                qkv_s[layer, window, 0:padded, part * features : (part + 1) * features] = (
                    block[window * padded : (window + 1) * padded].astype(bf16)
                )

        def group(n, carry):
            start = pl.multiple_of(n * lanes, lanes)
            bias = bias_s[layer, :, pl.ds(pl.multiple_of(n * group_lanes, lanes), group_lanes)]
            for window in range(windows):
                query = qkv_s[layer, window, :, pl.ds(start, lanes)]
                key = qkv_s[layer, window, 0:padded, pl.ds(pl.multiple_of(features + start, lanes), lanes)]
                value = qkv_s[layer, window, 0:padded, pl.ds(pl.multiple_of(2 * features + start, lanes), lanes)]
                scores = dot_nt(key, diagonal(query)) * scaling + bias
                if layer % 2:
                    scores = scores + mask_ref[window]
                raised = jnp.exp(scores - jnp.max(scores, axis=0, keepdims=True))
                probs = raised * (1.0 / jnp.sum(raised, axis=0, keepdims=True))
                probs_s[layer, n, window] = probs
                mixed = undiagonal(dot_tn(probs.astype(bf16), value))
                mixf_s[window * padded : (window + 1) * padded, pl.ds(start, lanes)] = mixed
            return carry

        both_halves(group)
        go()
        have(layer, at_proj, at_one)
        mixed = mixf_s[...].astype(bf16)
        mixed_s[layer] = mixed
        mid_s[layer] = rows + dot_nn(mixed, proj_of(layer)) + kind(4 * LAYERS + layer)

    def mlp_forward(layer):
        go()
        have(layer, at_one, at_two)
        middle = mid_s[layer]
        unit, _ = normalize(middle)
        yn = (unit * kind(5 * LAYERS + layer) + kind(6 * LAYERS + layer)).astype(bf16)
        yn_s[layer] = yn
        for part in range(wide_parts):
            cols = slice(part * features, (part + 1) * features)
            pre = dot_nn(yn, one_of(layer, part)) + b1_s[layer : layer + 1, cols]
            cumul = 0.5 * (1.0 + lax.erf(pre * half_root))
            slope_s[layer, :, cols] = cumul + pre * (jnp.exp(-0.5 * pre * pre) * inv_root_tau)
            act_s[layer, :, cols] = (pre * cumul).astype(bf16)

    def mlp_rest(layer):
        total = mid_s[layer] + kind(7 * LAYERS + layer)
        for part in range(wide_parts):
            cols = slice(part * features, (part + 1) * features)
            total = total + dot_nn(act_s[layer, :, cols], two_of(layer, part))
        return total

    attention_forward(0)
    mlp_forward(0)
    go()
    have(0, at_two, at_two + deep)
    xs[1] = permute_f32(forth_ref[...], mlp_rest(0))
    attention_forward(1)
    mlp_forward(1)
    active = count_ref[0] > 0

    def mlp_backward(layer, grad):
        low = grad.astype(bf16)
        kg_s[7 * LAYERS + layer : 7 * LAYERS + layer + 1, :] = jnp.sum(grad, axis=0, keepdims=True)
        go()
        for part in range(wide_parts):
            cols = slice(part * features, (part + 1) * features)
            g[layer, part // 2, part % 2, :, :, :, at_two : at_two + deep, :] = (
                dot_tn(act_s[layer, :, cols], low).astype(bf16).reshape(2, 2, 2, deep, features)
            )
        go()
        if layer == LAYERS - 1:
            have(layer, at_two, at_two + deep)
        yn = yn_s[layer]
        g_yn = jnp.zeros_like(grad)
        for part in range(wide_parts):
            cols = slice(part * features, (part + 1) * features)
            g_pre = dot_nt(low, two_of(layer, part)) * slope_s[layer, :, cols]
            b1g_s[layer : layer + 1, cols] = jnp.sum(g_pre, axis=0, keepdims=True)
            pre_low = g_pre.astype(bf16)
            put(layer, at_one + part * rows_each, dot_tn(yn, pre_low))
            g_yn = g_yn + dot_nt(pre_low, one_of(layer, part))
        back, g_gain, g_off = norm_pull(mid_s[layer], kind(5 * LAYERS + layer), g_yn)
        kg_s[5 * LAYERS + layer : 5 * LAYERS + layer + 1, :] = g_gain
        kg_s[6 * LAYERS + layer : 6 * LAYERS + layer + 1, :] = g_off
        g_mid = grad + back
        kg_s[4 * LAYERS + layer : 4 * LAYERS + layer + 1, :] = jnp.sum(g_mid, axis=0, keepdims=True)
        return g_mid

    def attention_backward(layer, g_mid):
        go()
        low = g_mid.astype(bf16)
        put(layer, at_proj, dot_tn(mixed_s[layer], low))
        d_mix = dot_nt(low, proj_of(layer))
        for window in range(windows):
            dmix_s[window, 0:padded, :] = d_mix[window * padded : (window + 1) * padded].astype(bf16)

        def group(n, carry):
            start = pl.multiple_of(n * lanes, lanes)
            k_at = pl.multiple_of(features + start, lanes)
            v_at = pl.multiple_of(2 * features + start, lanes)
            total = jnp.zeros((padded, group_lanes), f32)
            for window in range(windows):
                here = slice(window * padded, (window + 1) * padded)
                query = diagonal(qkv_s[layer, window, :, pl.ds(start, lanes)])
                key = qkv_s[layer, window, 0:padded, pl.ds(k_at, lanes)]
                value = qkv_s[layer, window, 0:padded, pl.ds(v_at, lanes)]
                d_out = diagonal(dmix_s[window, :, pl.ds(start, lanes)])
                probs = probs_s[layer, n, window]
                d_probs = dot_nt(value, d_out)
                dqkv_s[here, pl.ds(v_at, lanes)] = dot_nn(probs.astype(bf16), d_out)
                weighed = probs * d_probs
                d_scores = weighed - probs * jnp.sum(weighed, axis=0, keepdims=True)
                total = total + d_scores
                scores_low = d_scores.astype(bf16)
                dqkv_s[here, pl.ds(k_at, lanes)] = dot_nn(scores_low, query) * scaling
                dqkv_s[here, pl.ds(start, lanes)] = undiagonal(dot_tn(scores_low, key)) * scaling
            dsum_s[:, pl.ds(pl.multiple_of(n * group_lanes, lanes), group_lanes)] = total
            return carry

        both_halves(group)
        go()
        for n, part in ((0, 0), (1, 2)):
            column = jnp.sum(dqkv_s[:, part * features : (part + 1) * features], axis=0, keepdims=True)
            at = 2 * LAYERS + 2 * layer + n
            kg_s[at : at + 1, :] = column
        xn = xn_s[layer]
        g_xn = jnp.zeros_like(g_mid)
        for part in range(parts):
            block = dqkv_s[:, part * features : (part + 1) * features].astype(bf16)
            put(layer, part * rows_each, dot_tn(xn, block))
            g_xn = g_xn + dot_nt(block, qkv_part(layer, part))
        go()
        back, g_gain, g_off = norm_pull(xs[layer], kind(layer), g_xn)
        kg_s[layer : layer + 1, :] = g_gain
        kg_s[LAYERS + layer : LAYERS + layer + 1, :] = g_off
        strip_s[...] = jnp.zeros_like(strip_s)
        for row in range(WIN):
            at = (WIN - 1 - row) * WIN
            strip_s[at : at + padded, :] = strip_s[at : at + padded, :] + jnp.where(
                lane_row == row, dsum_s[...], 0.0
            )
        by_col = dot_nn(strip_s[0:strips, :].astype(bf16), collect_ref[...])
        col_at = lax.broadcasted_iota(jnp.int32, (1, lanes), 1) // heads
        stacked = stack_rows([jnp.where(col_at == col, by_col, 0.0).astype(bf16) for col in range(WIN)])
        table = dot_nn(onehot_t_ref[...], stacked)
        high = table.astype(bf16)
        rest = (table - high.astype(f32)).astype(bf16)
        table = dot_nn(high, fold_ref[...]) + dot_nn(rest, fold_ref[...])
        rg_s[:, layer * 8 : (layer + 1) * 8, :] = table.reshape(devices, 8, lanes)
        return g_mid + back

    grad = jnp.where(active, dot_nn(shifted_ref[...], cot_ref[0]), 0.0)
    g_x = attention_backward(1, mlp_backward(1, grad))
    grad = permute_f32(back_ref[...], g_x)
    g_x = attention_backward(0, mlp_backward(0, grad))
    for tile in range(hidden // lanes):
        for n in range(pack_one):
            for layer in range(LAYERS):
                at = layer * 8 + table_each
                rg_s[tile * pack_one + n, at : at + 1, :] = (
                    b1g_s[layer : layer + 1, tile * lanes : (tile + 1) * lanes]
                )
    for tile in range(features // lanes):
        block = kg_s[:, tile * lanes : (tile + 1) * lanes].astype(bf16)
        for n in range(pack):
            device = tile * pack + n
            sg[device // 16, (device // 8) % 2, (device // 4) % 2, (device // 2) % 2, device % 2, :, 0:lanes] = block
    sg[:, :, :, :, :, :, lanes : 2 * lanes] = rg_s[...].astype(bf16).reshape(2, 2, 2, 2, 2, 16, lanes)
    go()
    gin_ref[0] = permute_f32(plain_t_ref[...], g_x)
    go()
    out_ref[0] = jnp.where(active, permute_f32(shifted_t_ref[...], mlp_rest(1)), 0.0)
    go()
    links.finish()


def finish_kernel(*refs):
    count = len(refs) // 2
    for n, (source, target) in enumerate(zip(refs[:count], refs[count:])):
        if n < 2:
            target[...] = source[0][:, None, :]
        elif n == 6:
            for layer in range(LAYERS):
                target[:, layer, :] = source[layer]
        else:
            target[...] = source[...]


def whole(devices):
    def local(images, cotangent, counts, *shards):
        twos = (2,) * len(AXES)
        rows_each, features = shards[5].shape[1:]
        hidden = shards[9].shape[2]
        deep = shards[11].shape[1]
        parts, wide_parts = shards[2].shape[2] // features, hidden // features
        heads = shards[4].shape[2]
        cells = WIN * WIN
        padded, wide = slots_of(cells)
        windows = (SIDE // WIN) ** 2
        total = windows * padded
        tokens = images.shape[1]
        at_one = (parts + 1) * rows_each
        at_two = at_one + wide_parts * rows_each
        depth = at_two + deep
        edges = (0, parts * rows_each, at_one, at_two, depth)

        def spans_of(pieces):
            spans = []
            for layer, part, start, stop, of, route in pieces:
                if layer is None:
                    spans.append((None, 0, 0, route))
                    continue
                rows = edges[part + 1] - edges[part]
                low = edges[part] + rows * start // of
                spans.append((layer, low, edges[part] + rows * stop // of - low, route))
            return tuple(spans)

        gspans, rspans = spans_of(GATHERED), spans_of(SCATTERED)
        consts = constants(heads, shards[4].shape[1], devices)
        held = list(shards)
        held[4] = jnp.transpose(held[4], (1, 0, 2))
        args = [counts, images, cotangent, *held, *consts]
        outs = [shaped(images.shape, f32), shaped(images.shape, f32)]
        outs += [shaped(s.shape, f32) for s in shards]
        vmem = pltpu.VMEM
        strips = -(-(2 * WIN - 1) * WIN // 16) * 16
        tall = (WIN - 1) * WIN + padded
        tall = max(-(-tall // 8) * 8, strips)
        scratch = [
            *[vmem((LAYERS,) + twos + (depth, features), bf16)] * 2,
            *[vmem((LAYERS,) + twos[n:] + (depth, features), bf16) for n in range(1, len(AXES) + 1)],
            *[vmem(twos + (16, 2 * lanes), bf16)] * 2,
            *[vmem(twos[n:] + (16, 2 * lanes), bf16) for n in range(1, len(AXES) + 1)],
            vmem((LAYERS, total, features), f32),
            vmem((LAYERS, total, features), bf16),
            vmem((LAYERS, windows, wide, parts * features), bf16),
            vmem((LAYERS, heads * wide // (2 * lanes), windows, padded, 2 * lanes), f32),
            vmem((LAYERS, total, features), bf16),
            vmem((LAYERS, total, features), f32),
            vmem((LAYERS, total, features), bf16),
            vmem((LAYERS, total, hidden), f32),
            vmem((LAYERS, total, hidden), bf16),
            vmem((LAYERS, padded, heads * wide), f32),
            vmem((tall, heads * wide), f32),
            vmem((16, features), f32),
            vmem((8, hidden), f32),
            vmem((16, lanes), f32),
            vmem((total, features), f32),
            vmem((windows, wide, features), bf16),
            vmem((total, parts * features), f32),
            vmem((padded, heads * wide), f32),
            vmem((16, features), f32),
            vmem((8, hidden), f32),
            vmem((devices, 16, lanes), f32),
        ]
        scratch += [pltpu.SemaphoreType.DMA((len(gspans), len(AXES)))] * 2
        scratch += [pltpu.SemaphoreType.DMA((len(rspans), len(AXES)))] * 2
        scratch += [vmem(a.shape, a.dtype) for a in consts]
        scratch += [pltpu.SemaphoreType.DMA((FIXED,))]
        space = pl.BlockSpec(memory_space=pltpu.VMEM)
        results = pl.pallas_call(
            functools.partial(all_kernel, gspans, rspans, AGENDA),
            out_shape=tuple(outs),
            in_specs=[pl.BlockSpec(memory_space=pltpu.SMEM)]
            + [space] * (len(args) - 1 - FIXED)
            + [pl.BlockSpec(memory_space=pl.ANY)] * FIXED,
            out_specs=tuple([space] * len(outs)),
            scratch_shapes=scratch,
            compiler_params=pltpu.CompilerParams(
                collective_id=2, has_side_effects=True, vmem_limit_bytes=63 * 1024 * 1024
            ),
        )(*args)
        shapes = [r.shape for r in results]
        for n in (0, 1):
            shapes[n] = (tokens, 1, features)
        shapes[6] = (shapes[6][1], LAYERS, shapes[6][2])
        results = pl.pallas_call(
            finish_kernel,
            out_shape=tuple(shaped(s, f32) for s in shapes),
            in_specs=[space] * len(shapes),
            out_specs=tuple([space] * len(shapes)),
        )(*results)
        results = list(results)
        for n in (0, 1, 6):
            results[n] = jnp.transpose(results[n], (1, 0, 2))
        return tuple(results)

    return local


def fits_whole(devices, sizes):
    features, hidden, heads, table_rows, wide = sizes
    if devices != 1 << len(AXES) or features % devices or hidden % devices or table_rows % devices:
        return False
    rows_each, share_one, table_each = features // devices, hidden // devices, table_rows // devices
    return (
        rows_each % 16 == 0
        and lanes % rows_each == 0
        and lanes % share_one == 0
        and table_each <= 7
        and hidden * 8 == features * devices
        and lanes * heads == 4 * features
        and WIN * heads <= lanes
        and LAYERS == 2
        and share_one % (4 * 16) == 0
        and wide == 3 * features
    )


def solution(mesh):
    in_specs = (
        P("fsdp", None, None),
        P("fsdp", None, None),
        P("fsdp"),
        P(None, "fsdp"),
        P(None, "fsdp"),
        P(None, "fsdp", None),
        P(None, None, "fsdp"),
        P(None, "fsdp", None),
        P(None, "fsdp", None),
        P(None, "fsdp"),
        P(None, "fsdp"),
        P(None, "fsdp"),
        P(None, "fsdp", None),
        P(None, "fsdp"),
        P(None, "fsdp", None),
        P(None, "fsdp"),
    )
    out_specs = (
        P("fsdp", None, None),
        P("fsdp", None, None),
        P(None, "fsdp"),
        P(None, "fsdp"),
        P(None, "fsdp", None),
        P(None, None, "fsdp"),
        P(None, "fsdp", None),
        P(None, "fsdp", None),
        P(None, "fsdp"),
        P(None, "fsdp"),
        P(None, "fsdp"),
        P(None, "fsdp", None),
        P(None, "fsdp"),
        P(None, "fsdp", None),
        P(None, "fsdp"),
    )
    devices = mesh.shape["fsdp"]

    def step(images, cotangent, counts, *params):
        hidden, (_, table_rows, heads) = params[9].shape[2], params[4].shape
        sizes = (images.shape[2], hidden, heads, table_rows, params[2].shape[2])
        body = whole(devices) if fits_whole(devices, sizes) else local
        return jax.shard_map(
            body, mesh=mesh, in_specs=in_specs, out_specs=out_specs, check_vma=False
        )(images, cotangent, counts, *params)

    return step
```
